32 devices in a mesh: dp: 8 (over z, y), fsdp: 4 (over x, core).
Axes of the slice: x: 2, y: 2, z: 4, core: 2. Of those that a mesh axis runs over, the one named last changes fastest.
Arguments:
- tokens: bfloat16 [32768, 768], P(('dp', 'fsdp')), may hold values from -6 to 6
- cotangent: bfloat16 [32768, 768], P(('dp', 'fsdp')), may hold values from -6 to 6
- page_id: int32 [32768], P(('dp', 'fsdp')), may hold values from -1 to 4, as said below
- pos_row: int32 [32768], P(('dp', 'fsdp')), may hold values from 0 to 31, as said below
- pos_col: int32 [32768], P(('dp', 'fsdp')), may hold values from 0 to 31, as said below
- ln1_gain: bfloat16 [768], P('fsdp'), may hold values from 0.5 to 1.5
- ln1_shift: bfloat16 [768], P('fsdp'), may hold values from -3 to 3
- w_qkv: bfloat16 [768, 2304], P('fsdp'), may hold values from -0.21875 to 0.21875
- rel_table: bfloat16 [12, 2, 63], P('fsdp'), may hold values from -4 to 4
- w_out: bfloat16 [768, 768], P('fsdp'), may hold values from -0.625 to 0.625
- scale_attn: bfloat16 [768], P('fsdp'), may hold values from 0.5 to 2
- ln2_gain: bfloat16 [768], P('fsdp'), may hold values from 0.5 to 1.5
- ln2_shift: bfloat16 [768], P('fsdp'), may hold values from -3 to 3
- w_up: bfloat16 [768, 3072], P('fsdp'), may hold values from -0.21875 to 0.21875
- b_up: bfloat16 [3072], P('fsdp'), may hold values from -3 to 3
- w_down: bfloat16 [3072, 768], P('fsdp'), may hold values from -0.109375 to 0.109375
- b_down: bfloat16 [768], P('fsdp'), may hold values from -2 to 2
- scale_mlp: bfloat16 [768], P('fsdp'), may hold values from 0.5 to 2
Outputs:
- layer_out: bfloat16 [32768, 768], P(('dp', 'fsdp'))
- grad_tokens: bfloat16 [32768, 768], P(('dp', 'fsdp'))
- grad_ln1_gain: float32 [768], P('fsdp')
- grad_ln1_shift: float32 [768], P('fsdp')
- grad_w_qkv: float32 [768, 2304], P('fsdp')
- grad_rel_table: float32 [12, 2, 63], P('fsdp')
- grad_w_out: float32 [768, 768], P('fsdp')
- grad_scale_attn: float32 [768], P('fsdp')
- grad_ln2_gain: float32 [768], P('fsdp')
- grad_ln2_shift: float32 [768], P('fsdp')
- grad_w_up: float32 [768, 3072], P('fsdp')
- grad_b_up: float32 [3072], P('fsdp')
- grad_w_down: float32 [3072, 768], P('fsdp')
- grad_b_down: float32 [768], P('fsdp')
- grad_scale_mlp: float32 [768], P('fsdp')
The draws below stay inside these ranges and needn't reach their ends.
Inputs may be any that keep to these rules, and one draw needn't show every extreme that they name: `page_id`: each device's 1024 slots hold whole pages one after another, square grids of side 14, 24 or 32 in row-major order, numbered 0, 1, 2, ... in order within the device; empty slots follow them. Some device is full in every draw. `pos_row`: row of the patch in its page's grid; 0 on empty slots. `pos_col`: column of the patch in its page's grid; 0 on empty slots.
All inputs are finite; a program needn't handle non-finite values.
Results may differ from the reference program's by a relative error of at most 0.012.
Values may be sent and summed in bfloat16 or wider, within the bound.
A program may use at most 256 MiB of HBM per device.

```python
import math
import jax
import jax.numpy as jnp
from jax import lax

D = 768
HEADS = 12
HEAD = 64
FF = 3072
SIDE_S = 14
SIDE_M = 24
SIDE_L = 32
TOK_DEV = 1024
TOKENS = 32768


def page_layout(key):
    blocks = TOKENS // TOK_DEV
    cands = TOK_DEV // (SIDE_S * SIDE_S) + 4
    areas = jnp.array([SIDE_S * SIDE_S, SIDE_M * SIDE_M, SIDE_L * SIDE_L], jnp.int32)
    sides = jnp.array([SIDE_S, SIDE_M, SIDE_L], jnp.int32)
    kinds = jax.random.randint(jax.random.fold_in(key, 11), (blocks, cands), 0, 3)
    kinds = kinds.at[0].set(2)
    kinds = kinds.at[1].set(0)
    slot = jnp.arange(TOK_DEV, dtype=jnp.int32)

    def one_device(kind_row):

        def place(carry, kind):
            used, placed = carry
            area = areas[kind]
            fits = used + area <= TOK_DEV
            new_used = jnp.where(fits, used + area, used)
            new_placed = jnp.where(fits, placed + 1, placed)
            return ((new_used, new_placed), (fits, used, area, sides[kind], placed))
        _, (fits, start, area, side, label) = lax.scan(place, (jnp.int32(0), jnp.int32(0)), kind_row)
        inside = fits[None, :] & (slot[:, None] >= start[None, :]) & (slot[:, None] < (start + area)[None, :])
        has = jnp.any(inside, axis=1)
        which = jnp.sum(jnp.where(inside, label[None, :], 0), axis=1)
        first = jnp.sum(jnp.where(inside, start[None, :], 0), axis=1)
        width = jnp.maximum(jnp.sum(jnp.where(inside, side[None, :], 0), axis=1), 1)
        offset = slot - first
        page = jnp.where(has, which, -1)
        row = jnp.where(has, offset // width, 0)
        col = jnp.where(has, offset % width, 0)
        return (page, row, col)
    page, row, col = jax.vmap(one_device)(kinds)
    return (page.reshape(TOKENS).astype(jnp.int32), row.reshape(TOKENS).astype(jnp.int32), col.reshape(TOKENS).astype(jnp.int32))


def draw_page_id(key, part):
    return page_layout(jax.random.fold_in(key, 5))[0]


def draw_pos_row(key, part):
    return page_layout(jax.random.fold_in(key, 5))[1]


def draw_pos_col(key, part):
    return page_layout(jax.random.fold_in(key, 5))[2]


def block_levels(key, extent, cuts, low, high):
    level = 1.0
    for axis_at, parts in cuts:
        heights = jax.random.uniform(jax.random.fold_in(jax.random.fold_in(key, 6), axis_at), (parts,), jnp.float32, low / len(cuts), high / len(cuts))
        level = level * jnp.repeat(jnp.exp(heights), extent[axis_at] // parts).reshape((-1,) + (1,) * (len(extent) - 1 - axis_at))
    return level


def scatter_about(key, dims, scale, most, cuts=(), kind=jnp.bfloat16):
    entries = jax.random.normal(key, dims, jnp.float32) * scale
    if len(cuts) > 0:
        entries = block_levels(key, dims, cuts, -0.22, 0.18) * entries
    return jnp.clip(entries, min=-most, max=most).astype(kind)


def setup_inputs(seed: int = 0) -> dict:
    arg_keys = jax.random.split(jax.random.key(seed), 19)
    return {
        "tokens": scatter_about(arg_keys[0], (TOKENS, D), 1.0, 6.0, ((0, 32),)),
        "cotangent": scatter_about(arg_keys[1], (TOKENS, D), 1.0, 6.0, ((0, 32),)),
        "page_id": draw_page_id(jax.random.fold_in(arg_keys[18], 71), 0),
        "pos_row": draw_pos_row(jax.random.fold_in(arg_keys[18], 71), 0),
        "pos_col": draw_pos_col(jax.random.fold_in(arg_keys[18], 71), 0),
        "ln1_gain": jnp.clip(1.0 + 0.1 * jax.random.normal(arg_keys[5], (D,), jnp.float32), 0.5, 1.5).astype(jnp.bfloat16),
        "ln1_shift": scatter_about(arg_keys[6], (D,), 0.5, 3.0, ((0, 4),)),
        "w_qkv": scatter_about(arg_keys[7], (D, 3 * D), D ** -0.5, 0.21875, ((0, 4),)),
        "rel_table": scatter_about(arg_keys[8], (HEADS, 2, 2 * SIDE_L - 1), 1.0, 4.0, ((0, 4),)),
        "w_out": scatter_about(arg_keys[9], (D, D), (D // 8) ** -0.5, 0.625, ((0, 4),)),
        "scale_attn": jnp.clip(jnp.exp(math.log(2.0) - 1.3862944 * jax.random.uniform(arg_keys[10], (D,), jnp.float32) ** block_levels(arg_keys[10], (D,), ((0, 4),), -0.2, 0.2)), 0.5, 2.0).astype(jnp.bfloat16),
        "ln2_gain": jnp.clip(1.0 + 0.1 * jax.random.normal(arg_keys[11], (D,), jnp.float32), 0.5, 1.5).astype(jnp.bfloat16),
        "ln2_shift": scatter_about(arg_keys[12], (D,), 0.5, 3.0, ((0, 4),)),
        "w_up": scatter_about(arg_keys[13], (D, FF), D ** -0.5, 0.21875, ((0, 4),)),
        "b_up": scatter_about(arg_keys[14], (FF,), 0.5, 3.0, ((0, 4),)),
        "w_down": scatter_about(arg_keys[15], (FF, D), FF ** -0.5, 0.109375, ((0, 4),)),
        "b_down": scatter_about(arg_keys[16], (D,), 0.3, 2.0, ((0, 4),)),
        "scale_mlp": jnp.clip(jnp.exp(math.log(2.0) - 1.3862944 * jax.random.uniform(arg_keys[17], (D,), jnp.float32) ** block_levels(arg_keys[17], (D,), ((0, 4),), -0.2, 0.2)), 0.5, 2.0).astype(jnp.bfloat16),
    }


@jax.custom_vjp
def low(v):
    return lax.optimization_barrier(v.astype(jnp.bfloat16)).astype(jnp.float32)

@jax.custom_vjp
def low_back(v):
    return v

def low_keep(v):
    return (low(v), None)

def low_pass(kept, grad):
    return (grad,)

def back_keep(v):
    return (v, None)

def back_low(kept, grad):
    return (low(grad),)
low.defvjp(low_keep, low_pass)
low_back.defvjp(back_keep, back_low)
highest = lax.Precision.HIGHEST

def normalize(rows, gain, shift):
    center = rows - lax.optimization_barrier(jnp.mean(rows, axis=-1, keepdims=True))
    spread = lax.optimization_barrier(jnp.mean(center * center, axis=-1, keepdims=True))
    return center * lax.rsqrt(spread + 1e-06) * gain + shift

def forward_block(rows, pages, prow, pcol, params):
    g_one, s_one, wqkv, table, wout, scale_a, g_two, s_two, wup, bup, wdown, bdown, scale_m = params
    count = rows.shape[0]
    norm_one = low(normalize(rows, g_one, s_one))
    qkv = low(low_back(jnp.dot(norm_one, wqkv, precision=highest)))
    split = jnp.transpose(qkv.reshape(count, 3, HEADS, HEAD), (1, 2, 0, 3))
    queries, keys, values = (split[0], split[1], split[2])
    row_off = (prow[:, None] - prow[None, :] + SIDE_L - 1).astype(jnp.int32)
    col_off = (pcol[:, None] - pcol[None, :] + SIDE_L - 1).astype(jnp.int32)
    bias = table[:, 0, :][:, row_off] + table[:, 1, :][:, col_off]
    scores = jnp.einsum('hqe,hke->hqk', queries, keys, precision=highest) * 0.125 + bias
    same = pages[:, None] == pages[None, :]
    scores = low_back(jnp.where(same[None], scores, -1e+30))
    prob = low(jax.nn.softmax(scores, axis=-1))
    att = jnp.einsum('hqk,hke->hqe', prob, values, precision=highest)
    att = low(low_back(jnp.transpose(att, (1, 0, 2)).reshape(count, D)))
    proj = low_back(jnp.dot(att, wout, precision=highest))
    mid = rows + scale_a * proj
    norm_two = low(normalize(mid, g_two, s_two))
    upper = low_back(jnp.dot(norm_two, wup, precision=highest) + bup)
    act = low(jax.nn.gelu(upper, approximate=True))
    down = low_back(jnp.dot(act, wdown, precision=highest) + bdown)
    return mid + scale_m * down

def reference(tokens, cotangent, page_id, pos_row, pos_col, ln1_gain, ln1_shift, w_qkv, rel_table, w_out, scale_attn, ln2_gain, ln2_shift, w_up, b_up, w_down, b_down, scale_mlp):
    blocks = TOKENS // TOK_DEV
    params = tuple((p.astype(jnp.float32) for p in (ln1_gain, ln1_shift, w_qkv, rel_table, w_out, scale_attn, ln2_gain, ln2_shift, w_up, b_up, w_down, b_down, scale_mlp)))
    pages = page_id.reshape(blocks, TOK_DEV)
    prows = pos_row.reshape(blocks, TOK_DEV)
    pcols = pos_col.reshape(blocks, TOK_DEV)
    block_fn = jax.checkpoint(forward_block)

    def whole(rows_all, prm):

        def step(carry, item):
            rows, pg, pr, pc = item
            return (carry, block_fn(rows, pg, pr, pc, prm))
        _, outs = lax.scan(step, None, (rows_all.reshape(blocks, TOK_DEV, D), pages, prows, pcols))
        return outs.reshape(TOKENS, D)
    rows_in = tokens.astype(jnp.float32)
    result, pull = jax.vjp(whole, rows_in, params)
    grad = cotangent.astype(jnp.float32) * (page_id >= 0).astype(jnp.float32)[:, None]
    d_rows, grads = pull(grad)
    return (result.astype(jnp.bfloat16), d_rows.astype(jnp.bfloat16), grads[0], grads[1], grads[2], grads[3], grads[4], grads[5], grads[6], grads[7], grads[8], grads[9], grads[10], grads[11], grads[12])
```

```python
import jax
import jax.numpy as jnp
from jax import lax
from jax.experimental import pallas as pl
from jax.experimental.pallas import tpu as pltpu
from jax.sharding import PartitionSpec as P

F32 = jnp.float32
BF = jnp.bfloat16
NT = (((1,), (1,)), ((), ()))
NN = (((1,), (0,)), ((), ()))
VMEM = pl.BlockSpec(memory_space=pltpu.VMEM)
LIMIT = 60 << 20
MASKED = -1e30


def mm(a, b, dims=NN):
    return lax.dot_general(a, b, dims, preferred_element_type=F32)


def lanes(rows, width=128):
    return lax.broadcasted_iota(jnp.int32, (rows, width), 1)


def normalize(rows, gain, shift):
    center = rows - jnp.mean(rows, axis=-1, keepdims=True)
    spread = jnp.mean(center * center, axis=-1, keepdims=True)
    return center * lax.rsqrt(spread + 1e-06) * gain + shift


def pieces(x, lane):
    hi = x.astype(BF)
    rest = x - hi.astype(F32)
    mid = rest.astype(BF)
    low = (rest - mid.astype(F32)).astype(BF)
    third = lane % 3
    return jnp.where(third == 0, hi.astype(F32), jnp.where(third == 1, mid.astype(F32), low.astype(F32)))


def position_columns(pos, hot, page_q, page_k):
    for r in range(pos.shape[1]):
        code = (pos[0, r : r + 1, :] + 1) * 4096 + pos[1, r : r + 1, :] * 64 + pos[2, r : r + 1, :]
        code = jnp.broadcast_to(code.astype(F32), (128, 128)).T.astype(jnp.int32)
        lane = lanes(128)
        page, row, col = code >> 12, (code >> 6) & 63, code & 63
        near = lane & 63
        where = jnp.where(near < 32, row, col + 32)
        at = pl.ds(r * 128, 128)
        hot[at, :] = jnp.where(where == near, 1.0, 0.0).astype(BF)
        page_q[at, :] = jnp.where(page == lane, 1.0, 0.0)
        page_k[at, :] = jnp.where((lane < 6) & (page != lane), MASKED, 0.0).astype(BF)


def toeplitz(table, bias):
    lane = lanes(32)
    for p in range(bias.shape[0]):
        for axis in range(2):
            parts = []
            for head, at in ((2 * p + 1, 32 * axis), (2 * p, 64 + 32 * axis)):
                row = jnp.broadcast_to(table[2 * head + axis : 2 * head + axis + 1, :], (32, 128))
                rolled = pltpu.roll(row, (97 + at) % 128, axis=1, stride=1, stride_axis=0)
                parts.append(jnp.where((lane >= at) & (lane < at + 32), rolled, 0.0))
            bias[p, 32 * axis : 32 * axis + 32, :] = (parts[0] + parts[1]).astype(BF)


def forward_kernel(tok, pos, gain, shift, table, wqkv, norm, qkv, att, ext, hot, page_k, bias, lse, ka, va):
    count, width = tok.shape
    pairs = bias.shape[0]
    position_columns(pos, hot, lse, page_k)
    toeplitz(table, bias)

    @pl.loop(0, count // 256)
    def _(b):
        at = pl.ds(pl.multiple_of(b * 256, 256), 256)
        rows = normalize(tok[at, :].astype(F32), gain[...], shift[...]).astype(BF)
        norm[at, :] = rows
        for part in range(3):
            block = mm(rows, wqkv[:, part * width : (part + 1) * width]).astype(BF)
            if part == 0:
                block = block * jnp.asarray(0.125, BF)
            for p in range(pairs):
                qkv[part * pairs + p, at, :] = block[:, p * 128 : (p + 1) * 128]

    low_half = lanes(count) < 64

    @pl.loop(0, pairs)
    def _(p):
        keys, values = qkv[pairs + p], qkv[2 * pairs + p]
        side = mm(hot[:, :64], bias[p]).astype(BF)
        one = jnp.ones_like(values)
        ka[0, :, :128] = jnp.where(low_half, keys, side)
        ka[1, :, :128] = jnp.where(low_half, side, keys)
        va[0] = jnp.where(low_half, values, one)
        va[1] = jnp.where(low_half, one, values)
        for e in range(2):
            ka[e, :, 128:] = page_k[...]

        @pl.loop(0, count // 256)
        def _(b):
            at = pl.ds(pl.multiple_of(b * 256, 256), 256)
            queries, places = qkv[p, at, :], hot[at, :]
            kept = lse[at, :]
            lane = lanes(256)
            half = lane < 64
            page_hot = jnp.where(lane < 6, kept, 0.0).astype(BF)
            outs = []
            for e in range(2):
                first = jnp.where(half, queries, places) if e == 0 else jnp.where(half, places, queries)
                scores = mm(jnp.concatenate([first, page_hot], axis=1), ka[e], NT)
                top = jnp.max(scores, axis=1, keepdims=True)
                expo = jnp.exp(scores - top).astype(BF)
                out = mm(expo, va[e])
                turned = pltpu.roll(out, 64, axis=1)
                total = jnp.where(half, turned, out) if e == 0 else jnp.where(half, out, turned)
                outs.append(out / total)
                kept = jnp.where(lane // 3 == 2 + 2 * p + e, top + jnp.log(total), kept)
            lse[at, :] = kept
            att[at, pl.ds(pl.multiple_of(p * 128, 128), 128)] = jnp.where(half, outs[0], outs[1]).astype(BF)

    lane = lanes(count)
    ext[...] = jnp.where(lane < 6, lse[...], pieces(lse[...], lane)).astype(BF)


def forward_call(tok, pos, gain, shift, table, wqkv):
    count, width = tok.shape
    pairs = width // 128
    return pl.pallas_call(
        forward_kernel,
        out_shape=[
            jax.ShapeDtypeStruct((count, width), BF),
            jax.ShapeDtypeStruct((3 * pairs, count, 128), BF),
            jax.ShapeDtypeStruct((count, width), BF),
            jax.ShapeDtypeStruct((count, 128), BF),
            jax.ShapeDtypeStruct((count, 128), BF),
            jax.ShapeDtypeStruct((count, 128), BF),
            jax.ShapeDtypeStruct((pairs, 64, 128), BF),
        ],
        in_specs=[VMEM] * 6,
        out_specs=[VMEM] * 7,
        scratch_shapes=[
            pltpu.VMEM((count, 128), F32),
            pltpu.VMEM((2, count, 256), BF),
            pltpu.VMEM((2, count, 128), BF),
        ],
        compiler_params=pltpu.CompilerParams(vmem_limit_bytes=LIMIT),
        name="attention_forward",
    )(tok, pos, gain, shift, table, wqkv)


def backward_kernel(
    pos, qkv, ext, hot, page_k, bias, att, datt, dqkv, dtab, qa, ka, va, doa, kt, dqt, dext, hot_t, square
):
    count, width = att.shape
    pairs = bias.shape[0]
    col = lax.broadcasted_iota(jnp.int32, (width, 128), 0) // 64
    pick = jnp.where(lanes(width) // 3 == col, 1.0, 0.0).astype(BF)

    @pl.loop(0, count // 256)
    def _(b):
        at = pl.ds(pl.multiple_of(b * 256, 256), 256)
        prod = att[at, :].astype(F32) * datt[at, :].astype(F32)
        hi = prod.astype(BF)
        low = (prod - hi.astype(F32)).astype(BF)
        dext[at, :] = pieces(-(mm(hi, pick) + mm(low, pick)), lanes(256)).astype(BF)

    for r in range(pos.shape[1]):
        want = 31 - lax.broadcasted_iota(jnp.int32, (32, 128), 0)
        for axis in range(2):
            have = jnp.broadcast_to(pos[1 + axis, r : r + 1, :], (32, 128))
            hot_t[32 * axis : 32 * axis + 32, r * 128 : r * 128 + 128] = jnp.where(have == want, 1.0, 0.0).astype(BF)

    low_half = lanes(count) < 64
    third = lanes(count) // 3

    @pl.loop(0, pairs)
    def _(p):
        queries, keys, values = qkv[p], qkv[pairs + p], qkv[2 * pairs + p]
        side = mm(hot[:, :64], bias[p]).astype(BF)
        zero = jnp.zeros_like(values)
        places = hot[...]
        qa[0, :, :128] = jnp.where(low_half, queries, places)
        qa[1, :, :128] = jnp.where(low_half, places, queries)
        ka[0, :, :128] = jnp.where(low_half, keys, side)
        ka[1, :, :128] = jnp.where(low_half, side, keys)
        va[0, :, :128] = jnp.where(low_half, values, zero)
        va[1, :, :128] = jnp.where(low_half, zero, values)
        for e in range(2):
            head = 2 * p + e
            qa[e, :, 128:] = ext[...]
            ka[e, :, 128:] = jnp.where(third == 2 + head, -1.0, page_k[...].astype(F32)).astype(BF)
            va[e, :, 128:] = jnp.where(third == head, 1.0, 0.0).astype(BF)
        doa[:, :128] = datt[:, pl.ds(pl.multiple_of(p * 128, 128), 128)]
        doa[:, 128:] = dext[...]
        kt[...] = keys.T
        dqt[...] = jnp.zeros_like(dqt)
        square[...] = jnp.zeros_like(square)

        @pl.loop(0, count // 256)
        def _(b):
            at = pl.ds(pl.multiple_of(b * 256, 256), 256)
            dks, dvs = [], []
            for e in range(2):
                prob = jnp.exp(mm(ka[e, at, :], qa[e], NT))
                d_prob = mm(va[e, at, :], doa[...], NT)
                d_scores = (prob * d_prob).astype(BF)
                dvs.append(mm(prob.astype(BF), doa[:, :128]))
                dks.append(mm(d_scores, qa[e, :, :128]))
                dqt[64 * e : 64 * e + 64, :] += mm(kt[64 * e : 64 * e + 64, at], d_scores)
            half = lanes(256) < 64
            dqkv[at, pl.ds(pl.multiple_of(width + p * 128, 128), 128)] = jnp.where(half, dks[0], dks[1]).astype(BF)
            dqkv[at, pl.ds(pl.multiple_of(2 * width + p * 128, 128), 128)] = jnp.where(half, dvs[0], dvs[1]).astype(BF)
            part = jnp.where(half, dks[1], dks[0])
            hi = part.astype(BF)
            low = (part - hi.astype(F32)).astype(BF)
            both = mm(hot_t[:, at], jnp.concatenate([hi, low], axis=1))
            square[...] += both[:, :128] + both[:, 128:]

        dqkv[:, pl.ds(pl.multiple_of(p * 128, 128), 128)] = (dqt[...].T * 0.125).astype(BF)
        near = lanes(32) & 63
        for axis in range(2):
            part = square[32 * axis : 32 * axis + 32, :]
            part = jnp.where((near >= 32) if axis else (near < 32), part, 0.0)
            rolled = pltpu.roll(part, 96 * axis, axis=1, stride=1, stride_axis=0)
            dtab[p, axis : axis + 1, :] = jnp.sum(rolled, axis=0, keepdims=True)


def backward_call(pos, qkv, ext, hot, page_k, bias, att, datt):
    count, width = att.shape
    pairs = width // 128
    return pl.pallas_call(
        backward_kernel,
        out_shape=[
            jax.ShapeDtypeStruct((count, 3 * width), BF),
            jax.ShapeDtypeStruct((pairs, 2, 128), F32),
        ],
        in_specs=[VMEM] * 8,
        out_specs=[VMEM] * 2,
        scratch_shapes=[
            pltpu.VMEM((2, count, 256), BF),
            pltpu.VMEM((2, count, 256), BF),
            pltpu.VMEM((2, count, 256), BF),
            pltpu.VMEM((count, 256), BF),
            pltpu.VMEM((128, count), BF),
            pltpu.VMEM((128, count), F32),
            pltpu.VMEM((count, 128), BF),
            pltpu.VMEM((64, count), BF),
            pltpu.VMEM((64, 128), F32),
        ],
        compiler_params=pltpu.CompilerParams(vmem_limit_bytes=LIMIT),
        name="attention_backward",
    )(pos, qkv, ext, hot, page_k, bias, att, datt)


def gather(x):
    return lax.all_gather(x, "fsdp", axis=0, tiled=True)


def local(
    tokens,
    cotangent,
    page_id,
    pos_row,
    pos_col,
    ln1_gain,
    ln1_shift,
    w_qkv,
    rel_table,
    w_out,
    scale_attn,
    ln2_gain,
    ln2_shift,
    w_up,
    b_up,
    w_down,
    b_down,
    scale_mlp,
):
    f32 = F32
    bf16 = BF
    count, width = tokens.shape
    small = [ln1_gain, ln1_shift, scale_attn, ln2_gain, ln2_shift, b_down, scale_mlp]
    rows = jnp.stack(small)
    own = rows.shape[1]
    mine = jnp.concatenate([rows.reshape(-1), b_up, rel_table.reshape(-1)])
    pad = -mine.shape[0] % 1024
    every = lax.all_gather(jnp.pad(mine, (0, pad)), "fsdp", axis=0, tiled=False)
    shards = every.shape[0]
    n_small = len(small) * own
    vectors = jnp.transpose(every[:, :n_small].reshape(shards, len(small), own), (1, 0, 2)).reshape(len(small), -1)
    bup = every[:, n_small : n_small + b_up.shape[0]].reshape(-1)
    heads = rel_table.shape[0] * shards
    offsets = rel_table.shape[2]
    table = every[:, n_small + b_up.shape[0] : n_small + b_up.shape[0] + rel_table.size].reshape(heads * 2, offsets)
    table = jnp.pad(table.astype(f32), ((0, 0), (0, 128 - offsets)))
    vectors = vectors.astype(f32)
    g_one, s_one, scale_a, g_two, s_two, bdown, scale_m = [vectors[i] for i in range(len(small))]
    wqkv = gather(w_qkv)
    wout = gather(w_out)
    wup = gather(w_up)
    wdown = gather(w_down)
    pos = jnp.stack([page_id, pos_row, pos_col]).reshape(3, count // 128, 128)
    norm_one, qkv, att, ext, hot, page_k, bias = forward_call(tokens, pos, g_one[None], s_one[None], table, wqkv)
    tok = tokens.astype(f32)
    proj = jnp.dot(att, wout, preferred_element_type=f32)
    mid = tok + scale_a * proj
    norm_two = normalize(mid, g_two, s_two).astype(bf16)
    upper = jnp.dot(norm_two, wup, preferred_element_type=f32) + bup.astype(f32)
    act = jax.nn.gelu(upper, approximate=True).astype(bf16)
    down = jnp.dot(act, wdown, preferred_element_type=f32) + bdown
    layer_out = (mid + scale_m * down).astype(bf16)
    grad = cotangent.astype(f32) * (page_id >= 0).astype(f32)[:, None]
    d_scale_m = jnp.sum(grad * down, axis=0)
    d_down = (grad * scale_m).astype(bf16)
    d_bdown = jnp.sum(d_down.astype(f32), axis=0)
    d_wdown = jnp.einsum("nf,nd->fd", act, d_down, preferred_element_type=f32).astype(bf16)
    d_act = jnp.einsum("nd,fd->nf", d_down, wdown, preferred_element_type=f32)
    _, gelu_back = jax.vjp(lambda v: jax.nn.gelu(v, approximate=True), upper)
    d_upper = gelu_back(d_act)[0].astype(bf16)
    d_bup = jnp.sum(d_upper.astype(f32), axis=0)
    d_wup = jnp.einsum("nd,nf->df", norm_two, d_upper, preferred_element_type=f32).astype(bf16)
    d_norm_two = jnp.einsum("nf,df->nd", d_upper, wup, preferred_element_type=f32)
    _, norm_two_back = jax.vjp(normalize, mid, g_two, s_two)
    d_mid_norm, d_gain_two, d_shift_two = norm_two_back(d_norm_two)
    d_mid = grad + d_mid_norm
    d_scale_a = jnp.sum(d_mid * proj, axis=0)
    d_proj = (d_mid * scale_a).astype(bf16)
    d_wout = jnp.einsum("nd,ne->de", att, d_proj, preferred_element_type=f32).astype(bf16)
    d_att = jnp.einsum("ne,de->nd", d_proj, wout, preferred_element_type=f32).astype(bf16)
    d_qkv, d_tab = backward_call(pos, qkv, ext, hot, page_k, bias, att, d_att)
    d_wqkv = jnp.einsum("nd,nc->dc", norm_one, d_qkv, preferred_element_type=f32).astype(bf16)
    d_norm_one = jnp.einsum("nc,dc->nd", d_qkv, wqkv, preferred_element_type=f32)
    _, norm_one_back = jax.vjp(normalize, tok, g_one, s_one)
    d_rows_norm, d_gain_one, d_shift_one = norm_one_back(d_norm_one)
    grad_tokens = (d_mid + d_rows_norm).astype(bf16)
    d_table = jnp.transpose(d_tab.reshape(-1, 2, 2, 64)[:, :, ::-1, :offsets], (0, 2, 1, 3)).reshape(heads, 2, offsets)

    def scatter(g):
        return lax.psum(lax.psum_scatter(g, "fsdp", scatter_dimension=0, tiled=True), "dp").astype(f32)

    r_wdown = scatter(d_wdown)
    r_wup = scatter(d_wup)
    r_wout = scatter(d_wout)
    r_wqkv = scatter(d_wqkv)
    flat = jnp.concatenate(
        [
            jnp.stack([d_gain_one, d_shift_one, d_scale_a, d_gain_two, d_shift_two, d_bdown, d_scale_m]).reshape(-1),
            d_bup,
            d_table.reshape(-1),
        ]
    )
    total = lax.psum(flat, ("dp", "fsdp"))
    me = lax.axis_index("fsdp")
    vec = lax.dynamic_slice(total[: len(small) * width].reshape(len(small), width), (0, me * own), (len(small), own))
    r_bup = lax.dynamic_slice(total[len(small) * width :][: d_bup.shape[0]], (me * b_up.shape[0],), b_up.shape)
    r_table = lax.dynamic_slice(
        total[len(small) * width + d_bup.shape[0] :].reshape(heads, 2, offsets), (me * rel_table.shape[0], 0, 0), rel_table.shape
    )
    return (
        layer_out,
        grad_tokens,
        vec[0],
        vec[1],
        r_wqkv,
        r_table,
        r_wout,
        vec[2],
        vec[3],
        vec[4],
        r_wup,
        r_bup,
        r_wdown,
        vec[5],
        vec[6],
    )


def solution(mesh):
    rows = P(("dp", "fsdp"))
    slab = P(("dp", "fsdp"), None)
    vec = P("fsdp")
    mat = P("fsdp", None)
    cube = P("fsdp", None, None)
    in_specs = (slab, slab, rows, rows, rows, vec, vec, mat, cube, mat, vec, vec, vec, mat, vec, mat, vec, vec)
    out_specs = (slab, slab, vec, vec, mat, cube, mat, vec, vec, vec, mat, vec, mat, vec, vec)
    return jax.shard_map(local, mesh=mesh, in_specs=in_specs, out_specs=out_specs, check_vma=False)
```

```python
import functools

import jax
import jax.numpy as jnp
from jax import lax
from jax.experimental import pallas as pl
from jax.experimental.pallas import tpu as pltpu
from jax.sharding import PartitionSpec as P

F32 = jnp.float32
BF = jnp.bfloat16
NT = (((1,), (1,)), ((), ()))
NN = (((1,), (0,)), ((), ()))
VMEM = pl.BlockSpec(memory_space=pltpu.VMEM)
ANY = pl.BlockSpec(memory_space=pl.ANY)
MESH = pl.DeviceIdType.MESH
LIMIT = 63 << 20
MASKED = -1e30


def mm(a, b, dims=NN):
    return lax.dot_general(a, b, dims, preferred_element_type=F32)


def lanes(rows, width=128):
    return lax.broadcasted_iota(jnp.int32, (rows, width), 1)


def normalize(rows, gain, shift):
    center = rows - jnp.mean(rows, axis=-1, keepdims=True)
    spread = jnp.mean(center * center, axis=-1, keepdims=True)
    return center * lax.rsqrt(spread + 1e-06) * gain + shift


def pieces(x, lane):
    hi = x.astype(BF)
    rest = x - hi.astype(F32)
    mid = rest.astype(BF)
    low = (rest - mid.astype(F32)).astype(BF)
    third = lane % 3
    return jnp.where(third == 0, hi.astype(F32), jnp.where(third == 1, mid.astype(F32), low.astype(F32)))


def position_columns(pos, hot, page_q, page_k):
    for r in range(pos.shape[1]):
        code = (pos[0, r : r + 1, :] + 1) * 4096 + pos[1, r : r + 1, :] * 64 + pos[2, r : r + 1, :]
        code = jnp.broadcast_to(code.astype(F32), (128, 128)).T.astype(jnp.int32)
        lane = lanes(128)
        page, row, col = code >> 12, (code >> 6) & 63, code & 63
        near = lane & 63
        where = jnp.where(near < 32, row, col + 32)
        at = pl.ds(r * 128, 128)
        hot[at, :] = jnp.where(where == near, 1.0, 0.0).astype(BF)
        page_q[at, :] = jnp.where(page == lane, 1.0, 0.0)
        page_k[at, :] = jnp.where((lane < 6) & (page != lane), MASKED, 0.0).astype(BF)


def toeplitz(table, bias):
    lane = lanes(32)
    for p in range(bias.shape[0]):
        for axis in range(2):
            parts = []
            for head, at in ((2 * p + 1, 32 * axis), (2 * p, 64 + 32 * axis)):
                row = jnp.broadcast_to(table[2 * head + axis : 2 * head + axis + 1, :], (32, 128))
                rolled = pltpu.roll(row, (97 + at) % 128, axis=1, stride=1, stride_axis=0)
                parts.append(jnp.where((lane >= at) & (lane < at + 32), rolled, 0.0))
            bias[p, 32 * axis : 32 * axis + 32, :] = (parts[0] + parts[1]).astype(BF)


def forward_kernel(tok, pos, gain, shift, table, wqkv, norm, qkv, att, ext, hot, page_k, bias, lse, ka, va):
    count, width = tok.shape
    pairs = bias.shape[0]
    position_columns(pos, hot, lse, page_k)
    toeplitz(table, bias)

    @pl.loop(0, count // 256)
    def _(b):
        at = pl.ds(pl.multiple_of(b * 256, 256), 256)
        rows = normalize(tok[at, :].astype(F32), gain[...], shift[...]).astype(BF)
        norm[:, at] = rows.T
        for part in range(3):
            block = mm(rows, wqkv[:, part * width : (part + 1) * width]).astype(BF)
            if part == 0:
                block = block * jnp.asarray(0.125, BF)
            for p in range(pairs):
                qkv[part * pairs + p, at, :] = block[:, p * 128 : (p + 1) * 128]

    low_half = lanes(count) < 64

    @pl.loop(0, pairs)
    def _(p):
        keys, values = qkv[pairs + p], qkv[2 * pairs + p]
        side = mm(hot[:, :64], bias[p]).astype(BF)
        one = jnp.ones_like(values)
        ka[0, :, :128] = jnp.where(low_half, keys, side)
        ka[1, :, :128] = jnp.where(low_half, side, keys)
        va[0] = jnp.where(low_half, values, one)
        va[1] = jnp.where(low_half, one, values)
        for e in range(2):
            ka[e, :, 128:] = page_k[...]

        @pl.loop(0, count // 256)
        def _(b):
            at = pl.ds(pl.multiple_of(b * 256, 256), 256)
            queries, places = qkv[p, at, :], hot[at, :]
            kept = lse[at, :]
            lane = lanes(256)
            half = lane < 64
            page_hot = jnp.where(lane < 6, kept, 0.0).astype(BF)
            outs = []
            for e in range(2):
                first = jnp.where(half, queries, places) if e == 0 else jnp.where(half, places, queries)
                scores = mm(jnp.concatenate([first, page_hot], axis=1), ka[e], NT)
                top = jnp.max(scores, axis=1, keepdims=True)
                expo = jnp.exp(scores - top).astype(BF)
                out = mm(expo, va[e])
                turned = pltpu.roll(out, 64, axis=1)
                total = jnp.where(half, turned, out) if e == 0 else jnp.where(half, out, turned)
                outs.append(out / total)
                kept = jnp.where(lane // 3 == 2 + 2 * p + e, top + jnp.log(total), kept)
            lse[at, :] = kept
            att[at, pl.ds(pl.multiple_of(p * 128, 128), 128)] = jnp.where(half, outs[0], outs[1]).astype(BF)

    lane = lanes(count)
    ext[...] = jnp.where(lane < 6, lse[...], pieces(lse[...], lane)).astype(BF)


def forward_call(tok, pos, gain, shift, table, wqkv):
    count, width = tok.shape
    pairs = width // 128
    return pl.pallas_call(
        forward_kernel,
        out_shape=[
            jax.ShapeDtypeStruct((width, count), BF),
            jax.ShapeDtypeStruct((3 * pairs, count, 128), BF),
            jax.ShapeDtypeStruct((count, width), BF),
            jax.ShapeDtypeStruct((count, 128), BF),
            jax.ShapeDtypeStruct((count, 128), BF),
            jax.ShapeDtypeStruct((count, 128), BF),
            jax.ShapeDtypeStruct((pairs, 64, 128), BF),
        ],
        in_specs=[VMEM] * 6,
        out_specs=[VMEM] * 7,
        scratch_shapes=[
            pltpu.VMEM((count, 128), F32),
            pltpu.VMEM((2, count, 256), BF),
            pltpu.VMEM((2, count, 128), BF),
        ],
        compiler_params=pltpu.CompilerParams(vmem_limit_bytes=LIMIT),
        name="attention_forward",
    )(tok, pos, gain, shift, table, wqkv)


class Links:
    def __init__(self, ndp):
        self.dp, self.f = lax.axis_index("dp"), lax.axis_index("fsdp")
        self.core, self.x = self.f % 2, self.f // 2
        self.bits = ndp.bit_length() - 1
        self.bit = [(self.dp // 2**k) % 2 for k in range(self.bits)]

    def partner(self, kind, k=0):
        if kind == "core":
            return (self.dp, self.f + 1 - 2 * self.core)
        if kind == "x":
            return (self.dp, self.f + 2 - 4 * self.x)
        return (self.dp + (1 - 2 * self.bit[k]) * 2**k, self.f)

    def everyone(self):
        return [self.partner("core"), self.partner("x")] + [self.partner("dp", k) for k in range(self.bits)]

    def greet(self):
        barrier = pltpu.get_barrier_semaphore()
        for other in self.everyone():
            pl.semaphore_signal(barrier, inc=1, device_id=other, device_id_type=MESH)
        pl.semaphore_wait(barrier, self.bits + 2)


def remote(src, dst, send, recv, device):
    return pltpu.make_async_remote_copy(
        src_ref=src, dst_ref=dst, send_sem=send, recv_sem=recv, device_id=device, device_id_type=MESH
    )


def pick_index(n, table):
    out = 0
    for i, v in enumerate(table):
        if v:
            out = out + jnp.where(n == i, v, 0)
    return out


class Reduction:
    def __init__(self, links, order, parts, own, acc, bufs, total_h, load_sem, send_sem, recv_sem, out_sem):
        self.l, self.order, self.parts, self.own, self.acc, self.bufs = links, order, parts, own, acc, bufs
        self.total_h, self.load_sem, self.send_sem, self.recv_sem, self.out_sem = (
            total_h,
            load_sem,
            send_sem,
            recv_sem,
            out_sem,
        )
        self.halvings = min(3, links.bits)
        self.extra = links.bits - self.halvings
        self.stages = 2 + 2 * self.halvings + self.extra
        self.kept = (links.x,) + tuple(links.bit[: self.halvings])

    def source(self, n):
        mine = pick_index(n, [i for _, i in self.order])
        return mine, sum(jnp.where(n == i, 1, 0) for i, (kind, _) in enumerate(self.order) if kind == "q")

    def copy(self, k, n):
        l, h = self.l, self.halvings
        sems = (self.send_sem.at[k, n], self.recv_sem.at[k, n])
        if k == 1:
            return remote(self.acc.at[n, 1 - l.x], self.bufs[1].at[n], *sems, l.partner("x"))
        if k < 2 + h:
            j = k - 2
            at = (n,) + self.kept[: 1 + j] + (1 - l.bit[j],)
            return remote(self.acc.at[at], self.bufs[2 + j].at[n], *sems, l.partner("dp", j))
        if k < 2 + h + self.extra:
            j = k - 2
            src = self.bufs[2 + j - 1] if j > h else None
            at = (n,) + self.kept[1:]
            src = self.bufs[1].at[at] if j == h else self.bufs[1].at[at]
            return remote(src, self.bufs[2 + j].at[n], *sems, l.partner("dp", j))
        j = h - 1 - (k - 2 - h - self.extra)
        at = (n,) + self.kept[1 : 2 + j]
        return remote(self.bufs[1].at[at], self.bufs[1].at[at], *sems, l.partner("dp", j))

    def first(self, n, act):
        l = self.l
        mine, is_own = self.source(n)
        sems = (self.send_sem.at[0, n], self.recv_sem.at[0, n])

        def both(home):
            act(
                lambda: remote(home.at[mine, 1 - l.core], self.bufs[0].at[n], *sems, l.partner("core")),
                lambda: pltpu.make_async_copy(home.at[mine, l.core], self.acc.at[n], self.load_sem.at[n]),
            )

        @pl.when(is_own == 0)
        def _():
            both(self.parts)

        @pl.when(is_own == 1)
        def _():
            both(self.own)

    def out(self, n):
        return pltpu.make_async_copy(self.bufs[1].at[n], self.total_h.at[n], self.out_sem.at[n])

    def step(self, k, n):
        h = self.halvings
        if k == 0:

            def start(send, load):
                send().start()
                load().start()

            self.first(n, start)
            return
        if k == 1:

            def arrive(send, load):
                send().wait_recv()
                load().wait()

            self.first(n, arrive)
            self.acc[n] = self.acc[n] + self.bufs[0][n]
        elif k <= 1 + h:
            self.copy(k - 1, n).wait_recv()
            at = (n,) + self.kept[: k - 1]
            self.acc[at] = self.acc[at] + self.bufs[k - 1][n]
        elif k == 2 + h:
            self.copy(k - 1, n).wait_recv()
            self.bufs[1][(n,) + self.kept[1:]] = self.acc[(n,) + self.kept] + self.bufs[k - 1][n]
        elif k <= 2 + h + self.extra:
            self.copy(k - 1, n).wait()
            at = (n,) + self.kept[1:]
            self.bufs[1][at] = self.bufs[1][at] + self.bufs[k - 1][n]
        else:
            self.copy(k - 1, n).wait_recv()
        if k < self.stages:
            self.copy(k, n).start()
        else:
            self.out(n).start()

    def tick(self, t, period, lags):
        for k in reversed(range(self.stages + 1)):
            m = t - lags[k] + 64 * period
            n = m // period - 64

            @pl.when((m % period == 0) & (n >= 0) & (n < len(self.order)))
            def _(k=k, n=n):
                self.step(k, n)

    def finish(self):
        @pl.loop(0, len(self.order))
        def _(n):
            self.first(n, lambda send, load: send().wait_send())
            for k in range(1, self.stages):
                if not 2 + self.halvings <= k < 2 + self.halvings + self.extra:
                    self.copy(k, n).wait_send()
            self.out(n).wait()


ORDER = [("g", 0), ("g", 1), ("g", 2), ("q", 0), ("g", 3), ("g", 4), ("q", 1), ("g", 5), ("q", 2), ("g", 6), ("g", 7), ("g", 8)]
PERIOD = 3


def lag_list(stages, extra):
    lags = [0, 1, 5]
    while len(lags) < stages + 1:
        lags.append(lags[-1] + 2)
    return lags


def backward_kernel(
    ndp,
    pos,
    vec,
    small_in,
    qkv_h,
    ext_h,
    hot_h,
    page_k_h,
    bias,
    dext_h,
    datt_h,
    normt_h,
    wq_h,
    tok_h,
    dmid_h,
    parts_h,
    gtok_h,
    total_h,
    small_out,
    qkv,
    ext,
    hot,
    page_k,
    dext,
    datt,
    normt,
    wq,
    tok,
    dmid,
    gtok,
    dqkv,
    qa,
    ka,
    va,
    doa,
    kt,
    dqt,
    hot_t,
    square,
    dtab,
    own,
    acc,
    b0,
    b1,
    b2,
    b3,
    b4,
    more,
    small_acc,
    small_recv,
    in_sem,
    gt_sem,
    load_sem,
    send_sem,
    recv_sem,
    out_sem,
    small_send,
    small_got,
):
    count, width = tok.shape
    pairs = bias.shape[0]
    blocks = count // 256
    loads = []
    for i, (src, dst) in enumerate(
        [
            (qkv_h, qkv),
            (ext_h, ext),
            (hot_h, hot),
            (page_k_h, page_k),
            (dext_h, dext),
            (datt_h, datt),
            (normt_h, normt),
            (wq_h, wq),
            (tok_h, tok),
            (dmid_h, dmid),
        ]
    ):
        copy = pltpu.make_async_copy(src, dst, in_sem.at[i])
        copy.start()
        loads.append(copy)
    links = Links(ndp)
    links.greet()
    bufs = [b0, b1, b2, b3, b4] + [more.at[k] for k in range(max(0, links.bits - 3))]
    red = Reduction(links, ORDER, parts_h, own, acc, bufs, total_h, load_sem, send_sem, recv_sem, out_sem)
    lags = lag_list(red.stages, red.extra)

    for r in range(pos.shape[1]):
        want = 31 - lax.broadcasted_iota(jnp.int32, (32, 128), 0)
        for axis in range(2):
            have = jnp.broadcast_to(pos[1 + axis, r : r + 1, :], (32, 128))
            hot_t[32 * axis : 32 * axis + 32, r * 128 : r * 128 + 128] = jnp.where(have == want, 1.0, 0.0).astype(BF)
    small_acc[0] = small_in[...]
    low_half = lanes(count) < 64
    third = lanes(count) // 3
    for copy in loads[:6]:
        copy.wait()

    @pl.loop(0, pairs // 2)
    def _(g):
        @pl.loop(0, 2)
        def _(s):
            p = 2 * g + s
            queries, keys, values = qkv[p], qkv[pairs + p], qkv[2 * pairs + p]
            side = mm(hot[:, :64], bias[p]).astype(BF)
            zero = jnp.zeros_like(values)
            places = hot[...]
            qa[0, :, :128] = jnp.where(low_half, queries, places)
            qa[1, :, :128] = jnp.where(low_half, places, queries)
            ka[0, :, :128] = jnp.where(low_half, keys, side)
            ka[1, :, :128] = jnp.where(low_half, side, keys)
            va[0, :, :128] = jnp.where(low_half, values, zero)
            va[1, :, :128] = jnp.where(low_half, zero, values)
            for e in range(2):
                head = 2 * p + e
                qa[e, :, 128:] = ext[...]
                ka[e, :, 128:] = jnp.where(third == 2 + head, -1.0, page_k[...].astype(F32)).astype(BF)
                va[e, :, 128:] = jnp.where(third == head, 1.0, 0.0).astype(BF)
            doa[:, :128] = datt[:, pl.ds(pl.multiple_of(p * 128, 128), 128)]
            doa[:, 128:] = dext[...]
            kt[...] = keys.T
            dqt[...] = jnp.zeros_like(dqt)
            square[...] = jnp.zeros_like(square)

            @pl.loop(0, blocks)
            def _(b):
                red.tick(p * blocks + b, PERIOD, lags)
                at = pl.ds(pl.multiple_of(b * 256, 256), 256)
                dks, dvs = [], []
                for e in range(2):
                    prob = jnp.exp(mm(ka[e, at, :], qa[e], NT))
                    d_prob = mm(va[e, at, :], doa[...], NT)
                    d_scores = (prob * d_prob).astype(BF)
                    dvs.append(mm(prob.astype(BF), doa[:, :128]))
                    dks.append(mm(d_scores, qa[e, :, :128]))
                    dqt[64 * e : 64 * e + 64, :] += mm(kt[64 * e : 64 * e + 64, at], d_scores)
                half = lanes(256) < 64
                dqkv[g, at, pl.ds(pl.multiple_of(256 + s * 128, 128), 128)] = jnp.where(half, dks[0], dks[1]).astype(BF)
                dqkv[g, at, pl.ds(pl.multiple_of(512 + s * 128, 128), 128)] = jnp.where(half, dvs[0], dvs[1]).astype(BF)
                part = jnp.where(half, dks[1], dks[0])
                hi = part.astype(BF)
                low = (part - hi.astype(F32)).astype(BF)
                both = mm(hot_t[:, at], jnp.concatenate([hi, low], axis=1))
                square[...] += both[:, :128] + both[:, 128:]

            dqkv[g, :, pl.ds(pl.multiple_of(s * 128, 128), 128)] = (dqt[...].T * 0.125).astype(BF)
            near = lanes(32) & 63
            for axis in range(2):
                part = square[32 * axis : 32 * axis + 32, :]
                part = jnp.where((near >= 32) if axis else (near < 32), part, 0.0)
                rolled = pltpu.roll(part, 96 * axis, axis=1, stride=1, stride_axis=0)
                dtab[p, axis : axis + 1, :] = jnp.sum(rolled, axis=0, keepdims=True)

        @pl.when(g == 0)
        def _():
            for copy in loads[6:]:
                copy.wait()

        value = mm(normt[...], dqkv[g])
        for f in range(4):
            for r in range(4):
                for c in range(2):
                    rows = slice(192 * f + 48 * r, 192 * f + 48 * r + 48)
                    own[g, f % 2, f // 2, c, r // 2, r % 2] = value[rows, 384 * c : 384 * c + 384].astype(BF)

    for p in range(pairs):
        small_acc[0, 12 + 2 * p : 14 + 2 * p, 0:128] = dtab[p]

    def gtok_out(b):
        at = pl.ds(pl.multiple_of(b * 256, 256), 256)
        return pltpu.make_async_copy(gtok.at[at, :], gtok_h.at[at, :], gt_sem.at[b])

    first_tick = pairs * blocks

    @pl.loop(0, blocks)
    def _(b):
        red.tick(first_tick + b, PERIOD, lags)
        at = pl.ds(pl.multiple_of(b * 256, 256), 256)
        d_norm = mm(dqkv[0, at, :], wq[0], NT)
        for g in range(1, pairs // 2):
            d_norm += mm(dqkv[g, at, :], wq[g], NT)
        rows = tok[at, :].astype(F32)
        center = rows - jnp.mean(rows, axis=-1, keepdims=True)
        scale = lax.rsqrt(jnp.mean(center * center, axis=-1, keepdims=True) + 1e-06)
        unit = center * scale
        small_acc[0, 0:1, :] += jnp.sum(d_norm * unit, axis=0, keepdims=True)
        small_acc[0, 1:2, :] += jnp.sum(d_norm, axis=0, keepdims=True)
        d_unit = d_norm * vec[0:1, :]
        back = scale * (
            d_unit - jnp.mean(d_unit, axis=-1, keepdims=True) - unit * jnp.mean(d_unit * unit, axis=-1, keepdims=True)
        )
        gtok[at, :] = (dmid[at, :] + back).astype(BF)
        gtok_out(b).start()

    others = links.everyone()

    def small_copy(i):
        return remote(small_acc.at[i], small_recv.at[i], small_send.at[i], small_got.at[i], others[i])

    small_copy(0).start()
    at_tick = first_tick + blocks
    for i in range(len(others)):
        red.tick(at_tick + i, PERIOD, lags)
        small_copy(i).wait_recv()
        small_acc[i + 1] = small_acc[i] + small_recv[i]
        if i + 1 < len(others):
            small_copy(i + 1).start()
    small_out[...] = small_acc[len(others)]
    at_tick = at_tick + len(others)
    last = PERIOD * (len(ORDER) - 1) + lags[-1] + 1

    @pl.loop(at_tick, last)
    def _(t):
        red.tick(t, PERIOD, lags)

    red.finish()
    for i in range(len(others)):
        small_copy(i).wait_send()
    for b in range(blocks):
        gtok_out(b).wait()


def backward_call(ndp, pos, vec, small, qkv, ext, hot, page_k, bias, dext, datt, normt, wq, tok, dmid, parts):
    count, width = datt.shape
    bits = ndp.bit_length() - 1
    n = len(ORDER)
    stages = 2 + 2 * min(3, bits) + max(0, bits - 3)
    tall = pltpu.VMEM((count, width), BF)
    side = pltpu.VMEM((count, 128), BF)
    pair = pltpu.VMEM((2, count, 256), BF)
    return pl.pallas_call(
        functools.partial(backward_kernel, ndp),
        out_shape=[
            jax.ShapeDtypeStruct((count, width), BF),
            jax.ShapeDtypeStruct((n, 2, 2, 2, 48, 384), BF),
            jax.ShapeDtypeStruct(small.shape, F32),
        ],
        in_specs=[VMEM] * 3 + [ANY] * 4 + [VMEM] + [ANY] * 7,
        out_specs=[ANY] * 2 + [VMEM],
        scratch_shapes=[
            pltpu.VMEM(qkv.shape, BF),
            side,
            side,
            side,
            side,
            tall,
            pltpu.VMEM((width, count), BF),
            pltpu.VMEM(wq.shape, BF),
            tall,
            pltpu.VMEM((count, width), F32),
            tall,
            pltpu.VMEM((3, count, width), BF),
            pair,
            pair,
            pair,
            pltpu.VMEM((count, 256), BF),
            pltpu.VMEM((128, count), BF),
            pltpu.VMEM((128, count), F32),
            pltpu.VMEM((64, count), BF),
            pltpu.VMEM((64, 128), F32),
            pltpu.VMEM((width // 128, 2, 128), F32),
            pltpu.VMEM((3, 2, 2, 2, 2, 2, 48, 384), BF),
            pltpu.VMEM((n, 2, 2, 2, 2, 48, 384), BF),
            pltpu.VMEM((n, 2, 2, 2, 2, 48, 384), BF),
            pltpu.VMEM((n, 2, 2, 2, 48, 384), BF),
            pltpu.VMEM((n, 2, 2, 48, 384), BF),
            pltpu.VMEM((n, 2, 48, 384), BF),
            pltpu.VMEM((n, 48, 384), BF),
            pltpu.VMEM((max(1, bits - 3), n, 48, 384) if bits > 3 else (1, 1, 8, 128), BF),
            pltpu.VMEM((bits + 3,) + small.shape, F32),
            pltpu.VMEM((bits + 2,) + small.shape, F32),
            pltpu.SemaphoreType.DMA((10,)),
            pltpu.SemaphoreType.DMA((count // 256,)),
            pltpu.SemaphoreType.DMA((n,)),
            pltpu.SemaphoreType.DMA((stages, n)),
            pltpu.SemaphoreType.DMA((stages, n)),
            pltpu.SemaphoreType.DMA((n,)),
            pltpu.SemaphoreType.DMA((bits + 2,)),
            pltpu.SemaphoreType.DMA((bits + 2,)),
        ],
        compiler_params=pltpu.CompilerParams(vmem_limit_bytes=LIMIT, collective_id=1, has_side_effects=True),
        name="backward",
    )(pos, vec, small, qkv, ext, hot, page_k, bias, dext, datt, normt, wq, tok, dmid, parts)


def block_columns(ref, at, start, size=768):
    return ref[at, start : start + size]


def gelu_both(u):
    c = 0.7978845608028654
    square = u * u
    t = jnp.tanh(c * u * (1.0 + 0.044715 * square))
    half = 0.5 + 0.5 * t
    slope = half + (0.5 * c) * u * (1.0 - t * t) * (1.0 + 0.134145 * square)
    return u * half, slope


def middle_kernel(
    tok_h,
    cot_h,
    att_h,
    ext_h,
    vec,
    wout_h,
    wup_h,
    wdown_h,
    layer_h,
    dmid_h,
    datt_h,
    dext_h,
    part_h,
    small,
    tok,
    cot,
    att,
    ext,
    wout,
    wup,
    wdown,
    act,
    dup,
    n2t,
    ddt,
    att_t,
    dproj,
    slope,
    layer,
    dmid,
    datt,
    dext,
    stage,
    in_sem,
    out_sem,
    part_sem,
):
    count, width = tok.shape
    ff = wup.shape[1]
    cols = ff // width
    loads = []
    for i, (src, dst) in enumerate(
        [(att_h, att), (wout_h, wout), (tok_h, tok), (wup_h, wup), (wdown_h, wdown), (cot_h, cot), (ext_h, ext)]
    ):
        copy = pltpu.make_async_copy(src, dst, in_sem.at[i])
        copy.start()
        loads.append(copy)
    small[...] = jnp.zeros_like(small)
    head = lax.broadcasted_iota(jnp.int32, (width, 128), 0) // 64
    pick = jnp.where(lanes(width) // 3 == head, 1.0, 0.0).astype(BF)
    for copy in loads:
        copy.wait()

    def outs(b):
        at = pl.ds(pl.multiple_of(b * 256, 256), 256)
        return [
            pltpu.make_async_copy(src.at[at, :], dst.at[at, :], out_sem.at[i, b])
            for i, (src, dst) in enumerate([(layer, layer_h), (dmid, dmid_h), (datt, datt_h), (dext, dext_h)])
        ]

    @pl.loop(0, count // 256)
    def _(b):
        at = pl.ds(pl.multiple_of(b * 256, 256), 256)
        rows_att = att[at, :]
        proj = mm(rows_att, wout[...])
        mid = tok[at, :].astype(F32) + vec[2:3, :] * proj
        center = mid - jnp.mean(mid, axis=-1, keepdims=True)
        scale = lax.rsqrt(jnp.mean(center * center, axis=-1, keepdims=True) + 1e-06)
        unit = center * scale
        norm = (unit * vec[3:4, :] + vec[4:5, :]).astype(BF)
        down = jnp.zeros((256, width), F32)
        for j in range(cols):
            u = mm(norm, wup[:, j * width : (j + 1) * width]) + vec[8 + j : 9 + j, :]
            a, s = gelu_both(u)
            a = a.astype(BF)
            act[at, j * width : (j + 1) * width] = a
            slope[:, j * width : (j + 1) * width] = s
            down += mm(a, wdown[j * width : (j + 1) * width, :])
        down += vec[5:6, :]
        layer[at, :] = (mid + vec[6:7, :] * down).astype(BF)
        grad = cot[at, :].astype(F32) * (1.0 - ext[at, :].astype(F32)[:, 0:1])
        d_down = (grad * vec[6:7, :]).astype(BF)
        small[6:7, :] += jnp.sum(grad * down, axis=0, keepdims=True)
        small[5:6, :] += jnp.sum(d_down.astype(F32), axis=0, keepdims=True)
        d_norm = jnp.zeros((256, width), F32)
        for j in range(cols):
            d_act = mm(d_down, wdown[j * width : (j + 1) * width, :], NT)
            d_up = (d_act * slope[:, j * width : (j + 1) * width]).astype(BF)
            dup[at, j * width : (j + 1) * width] = d_up
            small[8 + j : 9 + j, :] += jnp.sum(d_up.astype(F32), axis=0, keepdims=True)
            d_norm += mm(d_up, wup[:, j * width : (j + 1) * width], NT)
        small[3:4, :] += jnp.sum(d_norm * unit, axis=0, keepdims=True)
        small[4:5, :] += jnp.sum(d_norm, axis=0, keepdims=True)
        d_unit = d_norm * vec[3:4, :]
        d_mid = grad + scale * (
            d_unit
            - jnp.mean(d_unit, axis=-1, keepdims=True)
            - unit * jnp.mean(d_unit * unit, axis=-1, keepdims=True)
        )
        dmid[at, :] = d_mid
        small[2:3, :] += jnp.sum(d_mid * proj, axis=0, keepdims=True)
        d_proj = (d_mid * vec[2:3, :]).astype(BF)
        dproj[at, :] = d_proj
        d_att = mm(d_proj, wout[...], NT).astype(BF)
        datt[at, :] = d_att
        prod = rows_att.astype(F32) * d_att.astype(F32)
        hi = prod.astype(BF)
        low = (prod - hi.astype(F32)).astype(BF)
        dext[at, :] = pieces(-(mm(hi, pick) + mm(low, pick)), lanes(256)).astype(BF)
        n2t[:, at] = norm.T
        ddt[:, at] = d_down.T
        att_t[:, at] = rows_att.T
        for copy in outs(b):
            copy.start()

    def put(slot, value):
        for i in range(4):
            for r in range(4):
                for c in range(2):
                    rows = slice(192 * i + 48 * r, 192 * i + 48 * r + 48)
                    stage[slot, i, c, r // 2, r % 2] = value[rows, 384 * c : 384 * c + 384].astype(BF)

    def sends(kind, j, slot):
        copies = []
        for i in range(4):
            if kind == 0:
                chunk, f = i, j
            elif kind == 1:
                chunk, f = 4 + j, i
            else:
                chunk, f = 8, i
            copies.append(pltpu.make_async_copy(stage.at[slot, i], part_h.at[chunk, f & 1, f >> 1], part_sem.at[slot, i]))
        return copies

    @pl.loop(0, cols)
    def _(j):
        col = pl.ds(pl.multiple_of(j * width, width), width)

        @pl.when(j > 0)
        def _():
            for copy in sends(0, j - 1, 0):
                copy.wait()

        put(0, mm(ddt[...], act[:, col]))
        for copy in sends(0, j, 0):
            copy.start()

        @pl.when(j > 0)
        def _():
            for copy in sends(1, j - 1, 1):
                copy.wait()

        put(1, mm(n2t[...], dup[:, col]))
        for copy in sends(1, j, 1):
            copy.start()

    for copy in sends(0, cols - 1, 0):
        copy.wait()
    put(0, mm(att_t[...], dproj[...]))
    for copy in sends(2, 0, 0):
        copy.start()
    for copy in sends(1, cols - 1, 1) + sends(2, 0, 0):
        copy.wait()
    for b in range(count // 256):
        for copy in outs(b):
            copy.wait()


def middle_call(tok, cot, att, ext, vec, wout, wup, wdown):
    count, width = tok.shape
    ff = wup.shape[1]
    tall = pltpu.VMEM((count, width), BF)
    wide = pltpu.VMEM((width, count), BF)
    return pl.pallas_call(
        middle_kernel,
        out_shape=[
            jax.ShapeDtypeStruct((count, width), BF),
            jax.ShapeDtypeStruct((count, width), F32),
            jax.ShapeDtypeStruct((count, width), BF),
            jax.ShapeDtypeStruct((count, 128), BF),
            jax.ShapeDtypeStruct((9, 2, 2, 2, 2, 2, 48, 384), BF),
            jax.ShapeDtypeStruct((24, width), F32),
        ],
        in_specs=[ANY] * 4 + [VMEM] + [ANY] * 3,
        out_specs=[ANY] * 5 + [VMEM],
        scratch_shapes=[
            tall,
            tall,
            tall,
            pltpu.VMEM((count, 128), BF),
            pltpu.VMEM(wout.shape, BF),
            pltpu.VMEM(wup.shape, BF),
            pltpu.VMEM(wdown.shape, BF),
            pltpu.VMEM((count, ff), BF),
            pltpu.VMEM((count, ff), BF),
            wide,
            wide,
            wide,
            tall,
            pltpu.VMEM((256, ff), F32),
            tall,
            pltpu.VMEM((count, width), F32),
            tall,
            pltpu.VMEM((count, 128), BF),
            pltpu.VMEM((2, 4, 2, 2, 2, 48, 384), BF),
            pltpu.SemaphoreType.DMA((7,)),
            pltpu.SemaphoreType.DMA((4, count // 256)),
            pltpu.SemaphoreType.DMA((2, 4)),
        ],
        compiler_params=pltpu.CompilerParams(vmem_limit_bytes=LIMIT),
        name="middle",
    )(tok, cot, att, ext, vec, wout, wup, wdown)


def gather(x):
    return lax.all_gather(x, "fsdp", axis=0, tiled=True)


def local(
    tokens,
    cotangent,
    page_id,
    pos_row,
    pos_col,
    ln1_gain,
    ln1_shift,
    w_qkv,
    rel_table,
    w_out,
    scale_attn,
    ln2_gain,
    ln2_shift,
    w_up,
    b_up,
    w_down,
    b_down,
    scale_mlp,
):
    f32 = F32
    bf16 = BF
    count, width = tokens.shape
    small = [ln1_gain, ln1_shift, scale_attn, ln2_gain, ln2_shift, b_down, scale_mlp]
    rows = jnp.stack(small)
    own = rows.shape[1]
    mine = jnp.concatenate([rows.reshape(-1), b_up, rel_table.reshape(-1)])
    pad = -mine.shape[0] % 1024
    every = lax.all_gather(jnp.pad(mine, (0, pad)), "fsdp", axis=0, tiled=False)
    shards = every.shape[0]
    n_small = len(small) * own
    vectors = jnp.transpose(every[:, :n_small].reshape(shards, len(small), own), (1, 0, 2)).reshape(len(small), -1)
    bup = every[:, n_small : n_small + b_up.shape[0]].reshape(-1)
    heads = rel_table.shape[0] * shards
    offsets = rel_table.shape[2]
    table = every[:, n_small + b_up.shape[0] : n_small + b_up.shape[0] + rel_table.size].reshape(heads * 2, offsets)
    table = jnp.pad(table.astype(f32), ((0, 0), (0, 128 - offsets)))
    vectors = vectors.astype(f32)
    g_one, s_one, scale_a, g_two, s_two, bdown, scale_m = [vectors[i] for i in range(len(small))]
    wqkv = gather(w_qkv)
    wout = gather(w_out)
    wup = gather(w_up)
    wdown = gather(w_down)
    pos = jnp.stack([page_id, pos_row, pos_col]).reshape(3, count // 128, 128)
    norm_one, qkv, att, ext, hot, page_k, bias = forward_call(tokens, pos, g_one[None], s_one[None], table, wqkv)
    tok = tokens.astype(f32)
    vec = jnp.pad(jnp.concatenate([vectors, jnp.zeros((1, width), f32), bup.astype(f32).reshape(-1, width)]), ((0, 12), (0, 0)))
    layer_out, d_mid, d_att, d_ext, parts, small_g = middle_call(tokens, cotangent, att, ext, vec, wout, wup, wdown)
    ndp = lax.axis_size("dp")
    wq = jnp.transpose(wqkv.reshape(width, 3, 3, 256), (2, 0, 1, 3)).reshape(3, width, width)
    grad_tokens, total, small_t = backward_call(
        ndp, pos, vec, small_g, qkv, ext, hot, page_k, bias, d_ext, d_att, norm_one, wq, tokens, d_mid, parts
    )
    total = jnp.transpose(total, (0, 2, 3, 4, 1, 5)).reshape(12, 192, 768).astype(f32)
    where = {kind: i for i, kind in enumerate(ORDER)}
    r_wdown = jnp.concatenate([total[where["g", i]] for i in range(4)], axis=0).T
    r_wup = jnp.concatenate([total[where["g", 4 + i]] for i in range(4)], axis=1)
    r_wout = total[where["g", 8]]
    r_wqkv = jnp.concatenate([total[where["q", g]][:, 256 * k : 256 * k + 256] for k in range(3) for g in range(3)], axis=1)
    me = lax.axis_index("fsdp")
    vec = lax.dynamic_slice(small_t, (0, me * own), (len(small), own))
    r_bup = lax.dynamic_slice(small_t, (8 + me, 0), (1, width)).reshape(-1)
    d_table = jnp.transpose(small_t[12:, :128].reshape(-1, 2, 2, 64)[:, :, ::-1, :offsets], (0, 2, 1, 3)).reshape(heads, 2, offsets)
    r_table = lax.dynamic_slice(d_table, (me * rel_table.shape[0], 0, 0), rel_table.shape)
    return (
        layer_out,
        grad_tokens,
        vec[0],
        vec[1],
        r_wqkv,
        r_table,
        r_wout,
        vec[2],
        vec[3],
        vec[4],
        r_wup,
        r_bup,
        r_wdown,
        vec[5],
        vec[6],
    )


def solution(mesh):
    rows = P(("dp", "fsdp"))
    slab = P(("dp", "fsdp"), None)
    vec = P("fsdp")
    mat = P("fsdp", None)
    cube = P("fsdp", None, None)
    in_specs = (slab, slab, rows, rows, rows, vec, vec, mat, cube, mat, vec, vec, vec, mat, vec, mat, vec, vec)
    out_specs = (slab, slab, vec, vec, mat, cube, mat, vec, vec, vec, mat, vec, mat, vec, vec)
    return jax.shard_map(local, mesh=mesh, in_specs=in_specs, out_specs=out_specs, check_vma=False)
```

```python
import functools

import jax
import jax.numpy as jnp
from jax import lax
from jax.experimental import pallas as pl
from jax.experimental.pallas import tpu as pltpu
from jax.sharding import PartitionSpec as P

F32 = jnp.float32
BF = jnp.bfloat16
NT = (((1,), (1,)), ((), ()))
NN = (((1,), (0,)), ((), ()))
VMEM = pl.BlockSpec(memory_space=pltpu.VMEM)
ANY = pl.BlockSpec(memory_space=pl.ANY)
MESH = pl.DeviceIdType.MESH
LIMIT = 63 << 20
MASKED = -1e30


def mm(a, b, dims=NN):
    return lax.dot_general(a, b, dims, preferred_element_type=F32)


def lanes(rows, width=128):
    return lax.broadcasted_iota(jnp.int32, (rows, width), 1)


def normalize(rows, gain, shift):
    center = rows - jnp.mean(rows, axis=-1, keepdims=True)
    spread = jnp.mean(center * center, axis=-1, keepdims=True)
    return center * lax.rsqrt(spread + 1e-06) * gain + shift


def pieces(x, lane):
    hi = x.astype(BF)
    rest = x - hi.astype(F32)
    mid = rest.astype(BF)
    low = (rest - mid.astype(F32)).astype(BF)
    third = lane % 3
    return jnp.where(third == 0, hi.astype(F32), jnp.where(third == 1, mid.astype(F32), low.astype(F32)))


def position_columns(pages, rows, cols, hot, page_q, page_k):
    for r in range(pages.shape[0]):
        code = (pages[r : r + 1, :] + 1) * 4096 + rows[r : r + 1, :] * 64 + cols[r : r + 1, :]
        code = jnp.broadcast_to(code.astype(F32), (128, 128)).T.astype(jnp.int32)
        lane = lanes(128)
        page, row, col = code >> 12, (code >> 6) & 63, code & 63
        near = lane & 63
        where = jnp.where(near < 32, row, col + 32)
        at = pl.ds(r * 128, 128)
        hot[at, :] = jnp.where(where == near, 1.0, 0.0).astype(BF)
        page_q[at, :] = jnp.where(page == lane, 1.0, 0.0)
        page_k[at, :] = jnp.where((lane < 6) & (page != lane), MASKED, 0.0).astype(BF)


def toeplitz(table, bias):
    lane = lanes(32)
    for p in range(bias.shape[0]):
        for axis in range(2):
            parts = []
            for head, at in ((2 * p + 1, 32 * axis), (2 * p, 64 + 32 * axis)):
                row = jnp.broadcast_to(table[2 * head + axis : 2 * head + axis + 1, :], (32, 128))
                rolled = pltpu.roll(row, (97 + at) % 128, axis=1, stride=1, stride_axis=0)
                parts.append(jnp.where((lane >= at) & (lane < at + 32), rolled, 0.0))
            bias[p, 32 * axis : 32 * axis + 32, :] = (parts[0] + parts[1]).astype(BF)


class Links:
    def __init__(self, ndp):
        self.dp, self.f = lax.axis_index("dp"), lax.axis_index("fsdp")
        self.core, self.x = self.f % 2, self.f // 2
        self.bits = ndp.bit_length() - 1
        self.bit = [(self.dp // 2**k) % 2 for k in range(self.bits)]

    def partner(self, kind, k=0):
        if kind == "core":
            return (self.dp, self.f + 1 - 2 * self.core)
        if kind == "x":
            return (self.dp, self.f + 2 - 4 * self.x)
        return (self.dp + (1 - 2 * self.bit[k]) * 2**k, self.f)

    def everyone(self):
        return [self.partner("core"), self.partner("x")] + [self.partner("dp", k) for k in range(self.bits)]

    def greet(self, others):
        barrier = pltpu.get_barrier_semaphore()
        for other in others:
            pl.semaphore_signal(barrier, inc=1, device_id=other, device_id_type=MESH)
        pl.semaphore_wait(barrier, len(others))


def remote(src, dst, send, recv, device):
    return pltpu.make_async_remote_copy(
        src_ref=src, dst_ref=dst, send_sem=send, recv_sem=recv, device_id=device, device_id_type=MESH
    )


def pick_index(n, table):
    out = 0
    for i, v in enumerate(table):
        if v:
            out = out + jnp.where(n == i, v, 0)
    return out


class Reduction:
    def __init__(self, links, halvings, order, homes, first, last, acc, recv, final, out_h, load_sem, send_sem, recv_sem, out_sem):
        self.l, self.order, self.homes, self.first = links, order, homes, first
        self.acc, self.recv, self.final, self.out_h = acc, recv, final, out_h
        self.load_sem, self.send_sem, self.recv_sem, self.out_sem = load_sem, send_sem, recv_sem, out_sem
        self.depth = max(0, first - 1)
        self.halvings = halvings
        self.halved = 1 + halvings
        self.extra = links.bits - halvings
        self.stages = 2 + 2 * halvings + self.extra
        self.last = self.stages if last is None else last
        self.kept = (links.x,) + tuple(links.bit[:halvings])

    def sems(self, k, n):
        return self.send_sem.at[k, n], self.recv_sem.at[k, n]

    def partner(self, k):
        l = self.l
        if k == 0:
            return l.partner("core")
        if k == 1:
            return l.partner("x")
        if k <= self.halved + self.extra:
            return l.partner("dp", k - 2)
        return l.partner("dp", self.halvings - 1 - (k - 1 - self.halved - self.extra))

    def copy(self, k, n):
        l = self.l
        if k <= self.halved:
            at = (n,) + self.kept[self.depth : k - 1] + (1 - self.kept[k - 1],)
            return remote(self.acc.at[at], self.recv[k].at[n], *self.sems(k, n), self.partner(k))
        if k <= self.halved + self.extra:
            return remote(self.final.at[(n,) + self.kept[1:]], self.recv[k].at[n], *self.sems(k, n), self.partner(k))
        j = self.halvings - 1 - (k - 1 - self.halved - self.extra)
        at = (n,) + self.kept[1 : 2 + j]
        return remote(self.final.at[at], self.final.at[at], *self.sems(k, n), self.partner(k))

    def opening(self, n, act):
        l = self.l
        for kind in sorted(self.homes):
            places = [i for i, (name, _) in enumerate(self.order) if name == kind]
            mine = pick_index(n, [i for _, i in self.order])
            home = self.homes[kind]

            @pl.when(sum(jnp.where(n == i, 1, 0) for i in places) > 0)
            def _(home=home):
                if self.first == 0:
                    act(
                        lambda: remote(
                            home.at[mine, 1 - l.core], self.recv[0].at[n], *self.sems(0, n), self.partner(0)
                        ),
                        lambda: pltpu.make_async_copy(home.at[mine, l.core], self.acc.at[n], self.load_sem.at[n]),
                    )
                else:
                    act(None, lambda: pltpu.make_async_copy(home.at[mine], self.acc.at[n], self.load_sem.at[n]))

    def out(self, n):
        if self.last == self.stages:
            return pltpu.make_async_copy(self.final.at[n], self.out_h.at[n], self.out_sem.at[n])
        src = self.acc.at[(n,) + self.kept[self.depth : self.last - 1]]
        return pltpu.make_async_copy(src, self.out_h.at[n], self.out_sem.at[n])

    def launch(self, n):
        def start(send, load):
            if send is not None:
                send().start()
            load().start()

        self.opening(n, start)

    def step(self, k, n):
        l = self.l

        def arrive(send, load):
            if send is not None:
                send().wait_recv()
            load().wait()

        if k == max(self.first, 1):
            self.opening(n, arrive)
            if self.first == 0:
                self.acc[n] = self.acc[n] + self.recv[0][n]
        elif k <= self.halved:
            self.copy(k - 1, n).wait_recv()
            at = (n,) + self.kept[self.depth : k - 1]
            self.acc[at] = self.acc[at] + self.recv[k - 1][n]
        elif k == self.halved + 1:
            self.copy(k - 1, n).wait_recv()
            at = (n,) + self.kept[self.depth :]
            self.final[(n,) + self.kept[1:]] = self.acc[at] + self.recv[k - 1][n]
        elif k <= self.halved + self.extra + 1:
            self.copy(k - 1, n).wait()
            at = (n,) + self.kept[1:]
            self.final[at] = self.final[at] + self.recv[k - 1][n]
        else:
            self.copy(k - 1, n).wait_recv()
        if k < self.last:
            self.copy(k, n).start()
        else:
            self.out(n).start()

    def tick(self, t, turns, lags):
        for k, lag in sorted(lags.items(), reverse=True):
            n = sum(jnp.where(t - lag >= turn, 1, 0) for turn in turns) - 1
            due = sum(jnp.where(t - lag == turn, 1, 0) for turn in turns)

            @pl.when(due > 0)
            def _(k=k, n=n):
                if k == -1:
                    self.launch(n)
                else:
                    self.step(k, n)

    def finish(self):
        l = self.l

        @pl.loop(0, len(self.order))
        def _(n):
            if self.first == 0:
                self.opening(n, lambda send, load: send().wait_send())
            for k in range(max(1, self.first), self.last):
                if not self.halved < k <= self.halved + self.extra:
                    self.copy(k, n).wait_send()
            self.out(n).wait()


def lag_table(first, last, start, step, special):
    table = {-1: start}
    at = start
    for k in range(max(1, first), last + 1):
        at += special.get(k, step)
        table[k] = at
    return table


def last_tick(lags, turns):
    return max(lags.values()) + max(turns) + 1


class Weights:
    def __init__(self, links, own, home, send_sem, recv_sem, keep_sem):
        self.l, self.own, self.home = links, own, home
        self.send_sem, self.recv_sem, self.keep_sem = send_sem, recv_sem, keep_sem
        l = links
        self.f = l.f
        self.y = l.bit[0]
        self.sibling = l.f + 1 - 2 * l.core
        self.across = l.f + 2 - 4 * l.x
        self.halves = (pl.ds(pl.multiple_of(self.y * 96, 32), 96), pl.ds(pl.multiple_of((1 - self.y) * 96, 32), 96))

    def branch(self, n, act):
        for (low, high), own, home in zip(((0, 3), (3, 4), (4, 8), (8, 12)), self.own, self.home):

            @pl.when((n >= low) & (n < high))
            def _(low=low, own=own, home=home):
                act(own(n - low), lambda f: home(n - low, f), low > 0)

    def copies(self, n, own, home):
        l, (this, other) = self.l, self.halves
        s = [(self.send_sem.at[k, n], self.recv_sem.at[k, n]) for k in range(5)]
        mine, across = home(self.f), home(self.across)
        sibling = l.partner("core")
        return [
            lambda: remote(own, mine, *s[0], sibling),
            lambda: remote(own.at[this, :], mine.at[this, :], *s[1], l.partner("x")),
            lambda: remote(across.at[this, :], across.at[this, :], *s[2], l.partner("dp", 0)),
            lambda: remote(across.at[this, :], across.at[this, :], *s[3], sibling),
            lambda: remote(across.at[other, :], across.at[other, :], *s[4], sibling),
        ]

    def step(self, k, n):
        def act(own, home, keep):
            copies = self.copies(n, own, home)
            if k == 0:
                copies[1]().start()
                copies[0]().start()
                if keep:
                    pltpu.make_async_copy(own, home(self.f), self.keep_sem.at[n]).start()
            elif k == 1:
                copies[1]().wait_recv()
                copies[2]().start()
                copies[3]().start()
            elif k == 2:
                copies[2]().wait_recv()
                copies[4]().start()
            elif k == 3:
                for i in (0, 3, 4):
                    copies[i]().wait_recv()
            else:
                for copy in copies:
                    copy().wait_send()
                if keep:
                    pltpu.make_async_copy(own, home(self.f), self.keep_sem.at[n]).wait()

        self.branch(n, act)

    def tick(self, t):
        for k, lag in ((3, 7), (2, 4), (1, 0)):
            m = t - lag + 128
            n = m // 2 - 63

            @pl.when((m % 2 == 0) & (n >= 1) & (n < 12))
            def _(k=k, n=n):
                self.step(k, n)
                if k == 1:

                    @pl.when(n + 3 < 12)
                    def _():
                        self.step(0, n + 3)


def pack_own(mine, vectors, bup, table):
    own = vectors[0].shape[0]
    mine[...] = jnp.zeros_like(mine)
    for i, ref in enumerate(vectors):
        mine[i : i + 1, 0:own] = ref[...].astype(F32).reshape(1, own)
    line = bup[...].astype(F32).reshape(1, bup.shape[0])
    for i in range(4):
        mine[7 + i : 8 + i, 0:own] = line[:, own * i : own * i + own]
    for h in range(table.shape[0]):
        for axis in range(2):
            at = 11 + 2 * h + axis
            mine[at : at + 1, 0 : table.shape[2]] = table[h, axis : axis + 1, :].astype(F32)


def unpack(shards, vec, table, own):
    for v in range(7):
        vec[v : v + 1, :] = jnp.concatenate([shards[f, v : v + 1, 0:own] for f in range(4)], axis=1)
    for f in range(4):
        vec[8 + f : 9 + f, :] = jnp.concatenate([shards[f, 7 + i : 8 + i, 0:own] for i in range(4)], axis=1)
        table[6 * f : 6 * f + 6, :] = shards[f, 11:17, 0:128]


def forward_kernel(
    ndp,
    page,
    row,
    col,
    v0,
    v1,
    v2,
    v3,
    v4,
    v5,
    v6,
    bup,
    rel,
    tok_h,
    wqkv_h,
    wout_s,
    wup_s,
    wdown_s,
    normt_h,
    qkv_h,
    att_h,
    ext_h,
    hot_h,
    page_k_h,
    bias,
    vec,
    wq_h,
    wout_h,
    wup_h,
    wdown_h,
    tok,
    norm,
    normt,
    qkv,
    att,
    ext,
    hot,
    page_k,
    lse,
    ka,
    va,
    wq,
    mine,
    shards,
    table,
    tok_sem,
    mine_sem,
    local_sem,
    pack_send,
    pack_got,
    send_sem,
    recv_sem,
    keep_sem,
    out_sem,
    group_sem,
):
    count, width = tok.shape
    pairs = bias.shape[0]
    blocks = count // 256
    links = Links(ndp)
    tok_copy = pltpu.make_async_copy(tok_h, tok, tok_sem)
    tok_copy.start()

    def own_group(g):
        return [
            pltpu.make_async_copy(
                wqkv_h.at[:, width * part + 256 * g + 128 * s : width * part + 256 * g + 128 * s + 128],
                wq.at[g, links.f, :, 384 * s + 128 * part : 384 * s + 128 * part + 128],
                local_sem.at[g, 3 * s + part],
            )
            for s in range(2)
            for part in range(3)
        ]

    for g in range(3):
        for copy in own_group(g):
            copy.start()
    own_loads = [pltpu.make_async_copy(wout_s, mine.at[0], mine_sem.at[0])]
    for j in range(4):
        part = pl.ds(j * width, width)
        own_loads.append(pltpu.make_async_copy(wup_s.at[:, part], mine.at[1 + j], mine_sem.at[1 + j]))
    for j in range(4):
        part = pl.ds(j * 192, 192)
        own_loads.append(pltpu.make_async_copy(wdown_s.at[part, :], mine.at[5 + j], mine_sem.at[5 + j]))
    for copy in own_loads:
        copy.start()
    pack_own(shards.at[links.f], [v0, v1, v2, v3, v4, v5, v6], bup, rel)
    diagonal = (links.dp, 3 - links.f)
    peers = [links.partner("core"), links.partner("x"), diagonal]
    barrier = pltpu.get_barrier_semaphore()
    for other in peers + [links.partner("dp", 0)]:
        pl.semaphore_signal(barrier, inc=1, device_id=other, device_id_type=MESH)
    pl.semaphore_wait(barrier, 4)

    gather = Weights(
        links,
        [
            lambda j: wq.at[j, links.f],
            lambda j: mine.at[j],
            lambda j: mine.at[1 + j],
            lambda j: mine.at[5 + j],
        ],
        [
            lambda j, f: wq.at[j, f],
            lambda j, f: wout_h.at[f],
            lambda j, f: wup_h.at[j, f],
            lambda j, f: wdown_h.at[f, j],
        ],
        send_sem,
        recv_sem,
        keep_sem,
    )

    def pack_copy(i):
        return remote(shards.at[links.f], shards.at[links.f], pack_send.at[i], pack_got.at[i], peers[i])

    for copy in own_group(0):
        copy.wait()
    gather.step(0, 0)
    for i in range(3):
        pack_copy(i).start()
    for g in (1, 2):
        for copy in own_group(g):
            copy.wait()
    for copy in own_loads:
        copy.wait()
    gather.step(0, 1)
    gather.step(0, 2)
    gather.step(0, 3)
    position_columns(page, row, col, hot, lse, page_k)
    for i in range(3):
        pack_copy(i).wait_recv()
    vec[...] = jnp.zeros_like(vec)
    unpack(shards, vec, table, v0.shape[0])
    toeplitz(table, bias)
    tok_copy.wait()

    @pl.loop(0, blocks)
    def _(b):
        at = pl.ds(pl.multiple_of(b * 256, 256), 256)
        rows = normalize(tok[at, :].astype(F32), vec[0:1, :], vec[1:2, :]).astype(BF)
        norm[at, :] = rows
        normt[:, at] = rows.T

    outs = [
        pltpu.make_async_copy(src, dst, out_sem.at[i])
        for i, (src, dst) in enumerate([(normt, normt_h), (hot, hot_h), (page_k, page_k_h), (att, att_h), (ext, ext_h)])
    ]
    for copy in outs[:3]:
        copy.start()
    for k in (1, 2, 3):
        gather.step(k, 0)
    low_half = lanes(count) < 64

    def group_out(g):
        copies = [pltpu.make_async_copy(wq.at[g], wq_h.at[g], group_sem.at[3, g])]
        for part in range(3):
            some = pl.ds(part * pairs + 2 * g, 2)
            copies.append(pltpu.make_async_copy(qkv.at[some], qkv_h.at[some], group_sem.at[part, g]))
        return copies

    @pl.loop(0, pairs // 2)
    def _(g):
        @pl.loop(0, blocks)
        def _(b):
            at = pl.ds(pl.multiple_of(b * 256, 256), 256)
            block = mm(norm[at, :], wq[g].reshape(width, width)).astype(BF)
            for s in range(2):
                for part in range(3):
                    value = block[:, 384 * s + 128 * part : 384 * s + 128 * part + 128]
                    qkv[part * pairs + 2 * g + s, at, :] = value if part else value * jnp.asarray(0.125, BF)

        for copy in group_out(g):
            copy.start()

        @pl.loop(0, 2)
        def _(s):
            p = 2 * g + s
            keys, values = qkv[pairs + p], qkv[2 * pairs + p]
            side = mm(hot[:, :64], bias[p]).astype(BF)
            one = jnp.ones_like(values)
            ka[0, :, :128] = jnp.where(low_half, keys, side)
            ka[1, :, :128] = jnp.where(low_half, side, keys)
            va[0] = jnp.where(low_half, values, one)
            va[1] = jnp.where(low_half, one, values)
            for e in range(2):
                ka[e, :, 128:] = page_k[...]

            @pl.loop(0, blocks)
            def _(b):
                gather.tick(p * blocks + b)
                at = pl.ds(pl.multiple_of(b * 256, 256), 256)
                queries, places = qkv[p, at, :], hot[at, :]
                kept = lse[at, :]
                lane = lanes(256)
                half = lane < 64
                page_hot = jnp.where(lane < 6, kept, 0.0).astype(BF)
                results = []
                for e in range(2):
                    first = jnp.where(half, queries, places) if e == 0 else jnp.where(half, places, queries)
                    scores = mm(jnp.concatenate([first, page_hot], axis=1), ka[e], NT)
                    top = jnp.max(scores, axis=1, keepdims=True)
                    expo = jnp.exp(scores - top).astype(BF)
                    out = mm(expo, va[e])
                    turned = pltpu.roll(out, 64, axis=1)
                    total = jnp.where(half, turned, out) if e == 0 else jnp.where(half, out, turned)
                    results.append(out / total)
                    kept = jnp.where(lane // 3 == 2 + 2 * p + e, top + jnp.log(total), kept)
                lse[at, :] = kept
                att[at, pl.ds(pl.multiple_of(p * 128, 128), 128)] = jnp.where(half, results[0], results[1]).astype(BF)

    lane = lanes(256)

    @pl.loop(0, blocks)
    def _(b):
        at = pl.ds(pl.multiple_of(b * 256, 256), 256)
        ext[at, :] = jnp.where(lane < 6, lse[at, :], pieces(lse[at, :], lane)).astype(BF)

    for copy in outs[3:]:
        copy.start()
    @pl.loop(pairs * blocks, 28)
    def _(t):
        gather.tick(t)


    @pl.loop(0, 12)
    def _(n):
        gather.step(4, n)

    for i in range(3):
        pack_copy(i).wait_send()

    @pl.loop(0, pairs // 2)
    def _(g):
        for copy in group_out(g):
            copy.wait()

    for copy in outs:
        copy.wait()


def forward_call(ndp, places, vectors, bup, rel, tok, wqkv, wout, wup, wdown):
    count, width = tok.shape
    pairs = width // 128
    tall = pltpu.VMEM((count, width), BF)
    side = pltpu.VMEM((count, 128), BF)
    return pl.pallas_call(
        functools.partial(forward_kernel, ndp),
        out_shape=[
            jax.ShapeDtypeStruct((width, count), BF),
            jax.ShapeDtypeStruct((3 * pairs, count, 128), BF),
            jax.ShapeDtypeStruct((count, width), BF),
            jax.ShapeDtypeStruct((count, 128), BF),
            jax.ShapeDtypeStruct((count, 128), BF),
            jax.ShapeDtypeStruct((count, 128), BF),
            jax.ShapeDtypeStruct((pairs, 64, 128), BF),
            jax.ShapeDtypeStruct((12, width), F32),
            jax.ShapeDtypeStruct((3, 4, 192, width), BF),
            jax.ShapeDtypeStruct((4, 192, width), BF),
            jax.ShapeDtypeStruct((4, 4, 192, width), BF),
            jax.ShapeDtypeStruct((4, 4, 192, width), BF),
        ],
        in_specs=[VMEM] * 12 + [ANY] * 5,
        out_specs=[ANY] * 6 + [VMEM] * 2 + [ANY] * 4,
        scratch_shapes=[
            tall,
            tall,
            pltpu.VMEM((width, count), BF),
            pltpu.VMEM((3 * pairs, count, 128), BF),
            tall,
            side,
            side,
            side,
            pltpu.VMEM((count, 128), F32),
            pltpu.VMEM((2, count, 256), BF),
            pltpu.VMEM((2, count, 128), BF),
            pltpu.VMEM((3, 4, 192, width), BF),
            pltpu.VMEM((9, 192, width), BF),
            pltpu.VMEM((4, 24, 256), F32),
            pltpu.VMEM((24, 128), F32),
            pltpu.SemaphoreType.DMA,
            pltpu.SemaphoreType.DMA((9,)),
            pltpu.SemaphoreType.DMA((3, 6)),
            pltpu.SemaphoreType.DMA((3,)),
            pltpu.SemaphoreType.DMA((3,)),
            pltpu.SemaphoreType.DMA((5, 12)),
            pltpu.SemaphoreType.DMA((5, 12)),
            pltpu.SemaphoreType.DMA((12,)),
            pltpu.SemaphoreType.DMA((5,)),
            pltpu.SemaphoreType.DMA((4, 3)),
        ],
        compiler_params=pltpu.CompilerParams(vmem_limit_bytes=LIMIT, collective_id=0, has_side_effects=True),
        name="forward",
    )(*places, *vectors, bup, rel, tok, wqkv, wout, wup, wdown)


def gelu_both(u):
    c = 0.7978845608028654
    square = u * u
    t = jnp.tanh(c * u * (1.0 + 0.044715 * square))
    half = 0.5 + 0.5 * t
    slope = half + (0.5 * c) * u * (1.0 - t * t) * (1.0 + 0.134145 * square)
    return u * half, slope


EARLY = [("d", 0), ("d", 1), ("d", 2), ("d", 3)]
EARLY_STOP = 3
EARLY_TURNS = [0, 5, 10, 15]
EARLY_LAGS = {1: 0, 2: 6, 3: 10}


def middle_kernel(
    ndp,
    tok_h,
    cot_h,
    att_h,
    ext_h,
    vec,
    wout_h,
    wup_h,
    wdown_h,
    layer_h,
    dmid_h,
    datt_h,
    dext_h,
    part_h,
    half_h,
    small,
    tok,
    cot,
    att,
    ext,
    wout,
    wup,
    wdown,
    act,
    dup,
    n2t,
    ddt,
    att_t,
    ddown,
    dproj,
    layer,
    dmid,
    datt,
    dext,
    stage,
    own,
    acc,
    r0,
    r1,
    r2,
    in_sem,
    out_sem,
    layer_sem,
    part_sem,
    load_sem,
    send_sem,
    recv_sem,
    half_sem,
):
    count, width = tok.shape
    cols = wup.shape[0]
    blocks = count // 256
    loads = []
    for i, (src, dst) in enumerate(
        [(att_h, att), (wout_h, wout), (tok_h, tok), (wup_h, wup), (wdown_h, wdown), (cot_h, cot), (ext_h, ext)]
    ):
        copy = pltpu.make_async_copy(src, dst, in_sem.at[i])
        copy.start()
        loads.append(copy)
    links = Links(ndp)
    links.greet(links.everyone()[:3])
    red = Reduction(
        links, 3, EARLY, {"d": own}, 0, EARLY_STOP, acc, [r0, r1, r2], None, half_h, load_sem, send_sem, recv_sem, half_sem
    )
    small[...] = jnp.zeros_like(small)
    head = lax.broadcasted_iota(jnp.int32, (width, 128), 0) // 64
    pick = jnp.where(lanes(width) // 3 == head, 1.0, 0.0).astype(BF)
    for copy in loads:
        copy.wait()

    def spot(b):
        return pl.ds(pl.multiple_of(b * 256, 256), 256)

    def layer_out(b):
        return pltpu.make_async_copy(layer.at[spot(b), :], layer_h.at[spot(b), :], layer_sem.at[b])

    def outs(b):
        at = spot(b)
        return [
            pltpu.make_async_copy(src.at[at, :], dst.at[at, :], out_sem.at[i, b])
            for i, (src, dst) in enumerate([(dmid, dmid_h), (datt, datt_h), (dext, dext_h)])
        ]

    def masked(at):
        return cot[at, :].astype(F32) * (1.0 - ext[at, :].astype(F32)[:, 0:1])

    def center_scale(mid):
        center = mid - jnp.mean(mid, axis=-1, keepdims=True)
        return center, lax.rsqrt(jnp.mean(center * center, axis=-1, keepdims=True) + 1e-06)

    @pl.loop(0, blocks)
    def _(b):
        at = spot(b)
        rows_att = att[at, :]
        proj = mm(rows_att, wout[...])
        mid = tok[at, :].astype(F32) + vec[2:3, :] * proj
        dmid[at, :] = mid
        datt[at, :] = proj.astype(BF)
        center, scale = center_scale(mid)
        norm = (center * scale * vec[3:4, :] + vec[4:5, :]).astype(BF)
        down = jnp.zeros((256, width), F32)
        for j in range(cols):
            u = mm(norm, wup[j]) + vec[8 + j : 9 + j, :]
            a, s = gelu_both(u)
            a = a.astype(BF)
            act[at, j * width : (j + 1) * width] = a
            dup[at, j * width : (j + 1) * width] = s.astype(BF)
            down += mm(a, wdown[j * width : (j + 1) * width, :])
        down += vec[5:6, :]
        layer[at, :] = (mid + vec[6:7, :] * down).astype(BF)
        layer_out(b).start()
        grad = masked(at)
        d_down = (grad * vec[6:7, :]).astype(BF)
        ddown[at, :] = d_down
        small[6:7, :] += jnp.sum(grad * down, axis=0, keepdims=True)
        small[5:6, :] += jnp.sum(d_down.astype(F32), axis=0, keepdims=True)
        n2t[:, at] = norm.T
        ddt[:, at] = d_down.T
        att_t[:, at] = rows_att.T

    @pl.loop(0, 2)
    def _(h):
        @pl.loop(0, cols)
        def _(j):
            col = pl.ds(pl.multiple_of(j * width, width), width)
            value = mm(ddt[pl.ds(pl.multiple_of(h * 384, 384), 384), :], act[:, col])
            for i in range(2):
                for r in range(4):
                    for c in range(2):
                        rows = slice(192 * i + 48 * r, 192 * i + 48 * r + 48)
                        own[2 * h + i, j % 2, j // 2, c, r // 2, r % 2] = value[rows, 384 * c : 384 * c + 384].astype(BF)

        red.launch(2 * h)
        red.launch(2 * h + 1)

    @pl.loop(0, blocks)
    def _(b):
        at = spot(b)
        d_down = ddown[at, :]
        d_norm = jnp.zeros((256, width), F32)
        for j in range(cols):
            red.tick(cols * b + j, EARLY_TURNS, EARLY_LAGS)
            d_act = mm(d_down, wdown[j * width : (j + 1) * width, :], NT)
            some = slice(j * width, (j + 1) * width)
            d_up = (d_act * dup[at, some].astype(F32)).astype(BF)
            dup[at, some] = d_up
            small[8 + j : 9 + j, :] += jnp.sum(d_up.astype(F32), axis=0, keepdims=True)
            d_norm += mm(d_up, wup[j], NT)
        center, scale = center_scale(dmid[at, :])
        unit = center * scale
        small[3:4, :] += jnp.sum(d_norm * unit, axis=0, keepdims=True)
        small[4:5, :] += jnp.sum(d_norm, axis=0, keepdims=True)
        d_unit = d_norm * vec[3:4, :]
        d_mid = masked(at) + scale * (
            d_unit - jnp.mean(d_unit, axis=-1, keepdims=True) - unit * jnp.mean(d_unit * unit, axis=-1, keepdims=True)
        )
        dmid[at, :] = d_mid
        small[2:3, :] += jnp.sum(d_mid * datt[at, :].astype(F32), axis=0, keepdims=True)
        d_proj = (d_mid * vec[2:3, :]).astype(BF)
        dproj[at, :] = d_proj
        d_att = mm(d_proj, wout[...], NT).astype(BF)
        datt[at, :] = d_att
        prod = att[at, :].astype(F32) * d_att.astype(F32)
        hi = prod.astype(BF)
        low = (prod - hi.astype(F32)).astype(BF)
        dext[at, :] = pieces(-(mm(hi, pick) + mm(low, pick)), lanes(256)).astype(BF)
        for copy in outs(b):
            copy.start()

    def put(slot, value):
        for i in range(4):
            for r in range(4):
                for c in range(2):
                    rows = slice(192 * i + 48 * r, 192 * i + 48 * r + 48)
                    stage[slot, i, c, r // 2, r % 2] = value[rows, 384 * c : 384 * c + 384].astype(BF)

    def sends(chunk, slot):
        return [
            pltpu.make_async_copy(stage.at[slot, i], part_h.at[chunk, i % 2, i // 2], part_sem.at[slot, i])
            for i in range(4)
        ]

    @pl.loop(0, cols)
    def _(j):
        red.tick(cols * blocks + j, EARLY_TURNS, EARLY_LAGS)
        col = pl.ds(pl.multiple_of(j * width, width), width)
        slot = j % 2

        @pl.when(j > 1)
        def _():
            for copy in sends(j - 2, slot):
                copy.wait()

        put(slot, mm(n2t[...], dup[:, col]))
        for copy in sends(j, slot):
            copy.start()

    for copy in sends(cols - 2, 0):
        copy.wait()
    put(0, mm(att_t[...], dproj[...]))
    for copy in sends(cols, 0):
        copy.start()

    @pl.loop(cols * blocks + cols, last_tick(EARLY_LAGS, EARLY_TURNS))
    def _(t):
        red.tick(t, EARLY_TURNS, EARLY_LAGS)

    for copy in sends(cols - 1, 1) + sends(cols, 0):
        copy.wait()

    @pl.loop(0, blocks)
    def _(b):
        layer_out(b).wait()
        for copy in outs(b):
            copy.wait()

    red.finish()


def middle_call(ndp, tok, cot, att, ext, vec, wout, wup, wdown):
    count, width = tok.shape
    ff = wdown.shape[0]
    n = len(EARLY)
    tall = pltpu.VMEM((count, width), BF)
    wide = pltpu.VMEM((width, count), BF)
    return pl.pallas_call(
        functools.partial(middle_kernel, ndp),
        out_shape=[
            jax.ShapeDtypeStruct((count, width), BF),
            jax.ShapeDtypeStruct((count, width), F32),
            jax.ShapeDtypeStruct((count, width), BF),
            jax.ShapeDtypeStruct((count, 128), BF),
            jax.ShapeDtypeStruct((5, 2, 2, 2, 2, 2, 48, 384), BF),
            jax.ShapeDtypeStruct((n, 2, 2, 48, 384), BF),
            jax.ShapeDtypeStruct((24, width), F32),
        ],
        in_specs=[ANY] * 4 + [VMEM] + [ANY] * 3,
        out_specs=[ANY] * 6 + [VMEM],
        scratch_shapes=[
            tall,
            tall,
            tall,
            pltpu.VMEM((count, 128), BF),
            pltpu.VMEM(wout.shape, BF),
            pltpu.VMEM(wup.shape, BF),
            pltpu.VMEM(wdown.shape, BF),
            pltpu.VMEM((count, ff), BF),
            pltpu.VMEM((count, ff), BF),
            wide,
            wide,
            wide,
            tall,
            tall,
            tall,
            pltpu.VMEM((count, width), F32),
            tall,
            pltpu.VMEM((count, 128), BF),
            pltpu.VMEM((2, 4, 2, 2, 2, 48, 384), BF),
            pltpu.VMEM((n, 2, 2, 2, 2, 2, 48, 384), BF),
            pltpu.VMEM((n, 2, 2, 2, 2, 48, 384), BF),
            pltpu.VMEM((n, 2, 2, 2, 2, 48, 384), BF),
            pltpu.VMEM((n, 2, 2, 2, 48, 384), BF),
            pltpu.VMEM((n, 2, 2, 48, 384), BF),
            pltpu.SemaphoreType.DMA((7,)),
            pltpu.SemaphoreType.DMA((3, count // 256)),
            pltpu.SemaphoreType.DMA((count // 256,)),
            pltpu.SemaphoreType.DMA((2, 4)),
            pltpu.SemaphoreType.DMA((n,)),
            pltpu.SemaphoreType.DMA((EARLY_STOP, n)),
            pltpu.SemaphoreType.DMA((EARLY_STOP, n)),
            pltpu.SemaphoreType.DMA((n,)),
        ],
        compiler_params=pltpu.CompilerParams(vmem_limit_bytes=LIMIT, collective_id=2, has_side_effects=True),
        name="middle",
    )(tok, cot, att, ext, vec, wout, wup, wdown)


ORDER = [("g", 0), ("g", 1), ("g", 2), ("q", 0), ("g", 3), ("g", 4), ("q", 1)]
TURNS = [0, 3, 6, 9, 12, 15, 18]
LAGS = {1: 1, 2: 5, 3: 4, 4: 3, 5: 3, 6: 3, 7: 3, 8: 4}
LATE_TURNS = [1, 4, 7, 10]
HALF = [("h", 0), ("h", 1)]
HALF_TURNS = [21, 24]


def backward_kernel(
    ndp,
    page,
    row,
    col,
    vec,
    small_in,
    qkv_h,
    ext_h,
    hot_h,
    page_k_h,
    bias,
    dext_h,
    datt_h,
    normt_h,
    wq_h,
    tok_h,
    dmid_h,
    parts_h,
    early_h,
    gtok_h,
    total_h,
    late_h,
    last_h,
    small_out,
    qkv,
    ext,
    hot,
    page_k,
    dext,
    datt,
    normt,
    wq,
    tok,
    dmid,
    gtok,
    dqkv,
    qa,
    ka,
    va,
    doa,
    kt,
    dqt,
    hot_t,
    square,
    dtab,
    own,
    own_half,
    acc,
    b0,
    b1,
    b2,
    b3,
    b4,
    late_acc,
    late_final,
    late_3,
    late_4,
    half_acc,
    half_final,
    half_0,
    half_1,
    half_2,
    half_3,
    more,
    late_more,
    half_more,
    small_acc,
    small_recv,
    in_sem,
    gt_sem,
    load_sem,
    send_sem,
    recv_sem,
    out_sem,
    late_load,
    late_send,
    late_recv,
    late_out,
    half_load,
    half_send,
    half_recv,
    half_out,
    small_send,
    small_got,
):
    count, width = tok.shape
    pairs = bias.shape[0]
    blocks = count // 256
    loads = []
    for i, (src, dst) in enumerate(
        [
            (qkv_h, qkv),
            (ext_h, ext),
            (hot_h, hot),
            (page_k_h, page_k),
            (dext_h, dext),
            (datt_h, datt),
            (normt_h, normt),
            (wq_h, wq),
            (tok_h, tok),
            (dmid_h, dmid),
        ]
    ):
        copy = pltpu.make_async_copy(src, dst, in_sem.at[i])
        copy.start()
        loads.append(copy)
    links = Links(ndp)
    links.greet(links.everyone())
    red = Reduction(
        links,
        3,
        ORDER,
        {"g": parts_h, "q": own},
        0,
        None,
        acc,
        [b0, b1, b2, b3, b4] + [more.at[k] for k in range(links.bits - 3)],
        b1,
        total_h,
        load_sem,
        send_sem,
        recv_sem,
        out_sem,
    )
    late = Reduction(
        links,
        3,
        EARLY,
        {"d": early_h},
        EARLY_STOP,
        None,
        late_acc,
        [None, None, None, late_3, late_4] + [late_more.at[k] for k in range(links.bits - 3)],
        late_final,
        late_h,
        late_load,
        late_send,
        late_recv,
        late_out,
    )
    half = Reduction(
        links,
        2,
        HALF,
        {"h": own_half},
        0,
        None,
        half_acc,
        [half_0, half_1, half_2, half_3] + [half_more.at[k] for k in range(links.bits - 2)],
        half_final,
        last_h,
        half_load,
        half_send,
        half_recv,
        half_out,
    )
    lags = lag_table(0, red.stages, 0, 3, LAGS)
    late_lags = lag_table(EARLY_STOP, late.stages, 0, 3, {EARLY_STOP: 1})
    half_lags = lag_table(0, half.stages, 0, 2, {1: 1})

    def tick(t):
        red.tick(t, TURNS, lags)
        late.tick(t, LATE_TURNS, late_lags)
        half.tick(t, HALF_TURNS, half_lags)

    for r in range(page.shape[0]):
        want = 31 - lax.broadcasted_iota(jnp.int32, (32, 128), 0)
        for axis in range(2):
            have = jnp.broadcast_to((col if axis else row)[r : r + 1, :], (32, 128))
            hot_t[32 * axis : 32 * axis + 32, r * 128 : r * 128 + 128] = jnp.where(have == want, 1.0, 0.0).astype(BF)
    small_acc[0] = small_in[...]
    low_half = lanes(count) < 64
    third = lanes(count) // 3
    for copy in loads[:6]:
        copy.wait()

    @pl.loop(0, pairs)
    def _(p):
        g, s = p // 2, p % 2
        queries, keys, values = qkv[p], qkv[pairs + p], qkv[2 * pairs + p]
        side = mm(hot[:, :64], bias[p]).astype(BF)
        zero = jnp.zeros_like(values)
        places = hot[...]
        qa[0, :, :128] = jnp.where(low_half, queries, places)
        qa[1, :, :128] = jnp.where(low_half, places, queries)
        ka[0, :, :128] = jnp.where(low_half, keys, side)
        ka[1, :, :128] = jnp.where(low_half, side, keys)
        va[0, :, :128] = jnp.where(low_half, values, zero)
        va[1, :, :128] = jnp.where(low_half, zero, values)
        for e in range(2):
            head = 2 * p + e
            qa[e, :, 128:] = ext[...]
            ka[e, :, 128:] = jnp.where(third == 2 + head, -1.0, page_k[...].astype(F32)).astype(BF)
            va[e, :, 128:] = jnp.where(third == head, 1.0, 0.0).astype(BF)
        doa[:, :128] = datt[:, pl.ds(pl.multiple_of(p * 128, 128), 128)]
        doa[:, 128:] = dext[...]
        kt[...] = keys.T
        dqt[...] = jnp.zeros_like(dqt)
        square[...] = jnp.zeros_like(square)

        @pl.loop(0, blocks)
        def _(b):
            tick(p * blocks + b)
            at = pl.ds(pl.multiple_of(b * 256, 256), 256)
            dks, dvs = [], []
            for e in range(2):
                prob = jnp.exp(mm(ka[e, at, :], qa[e], NT))
                d_prob = mm(va[e, at, :], doa[...], NT)
                d_scores = (prob * d_prob).astype(BF)
                dvs.append(mm(prob.astype(BF), doa[:, :128]))
                dks.append(mm(d_scores, qa[e, :, :128]))
                dqt[64 * e : 64 * e + 64, :] += mm(kt[64 * e : 64 * e + 64, at], d_scores)
            half = lanes(256) < 64
            dqkv[g, at, pl.ds(pl.multiple_of(s * 384 + 128, 128), 128)] = jnp.where(half, dks[0], dks[1]).astype(BF)
            dqkv[g, at, pl.ds(pl.multiple_of(s * 384 + 256, 128), 128)] = jnp.where(half, dvs[0], dvs[1]).astype(BF)
            part = jnp.where(half, dks[1], dks[0])
            hi = part.astype(BF)
            low = (part - hi.astype(F32)).astype(BF)
            both = mm(hot_t[:, at], jnp.concatenate([hi, low], axis=1))
            square[...] += both[:, :128] + both[:, 128:]

        dqkv[g, :, pl.ds(pl.multiple_of(s * 384, 128), 128)] = (dqt[...].T * 0.125).astype(BF)
        near = lanes(32) & 63
        for axis in range(2):
            part = square[32 * axis : 32 * axis + 32, :]
            part = jnp.where((near >= 32) if axis else (near < 32), part, 0.0)
            rolled = pltpu.roll(part, 96 * axis, axis=1, stride=1, stride_axis=0)
            dtab[p, axis : axis + 1, :] = jnp.sum(rolled, axis=0, keepdims=True)

        @pl.when(p == 0)
        def _():
            for copy in loads[6:]:
                copy.wait()

        value = mm(normt[...], dqkv[g, :, pl.ds(pl.multiple_of(s * 384, 128), 384)]).astype(BF)

        @pl.when(p < 2 * own.shape[0])
        def _():
            for f in range(4):
                for r in range(4):
                    own[g, f % 2, f // 2, s, r // 2, r % 2] = value[192 * f + 48 * r : 192 * f + 48 * r + 48, :]

        @pl.when(p >= 2 * own.shape[0])
        def _():
            for f in range(4):
                for r in range(4):
                    at = (p - 2 * own.shape[0], f % 2, f // 2, r // 2, r % 2)
                    own_half[at] = value[192 * f + 48 * r : 192 * f + 48 * r + 48, :]

    for p in range(pairs):
        small_acc[0, 12 + 2 * p : 14 + 2 * p, 0:128] = dtab[p]

    def gtok_out(b):
        at = pl.ds(pl.multiple_of(b * 256, 256), 256)
        return pltpu.make_async_copy(gtok.at[at, :], gtok_h.at[at, :], gt_sem.at[b])

    first_tick = pairs * blocks

    @pl.loop(0, blocks)
    def _(b):
        tick(first_tick + b)
        at = pl.ds(pl.multiple_of(b * 256, 256), 256)
        d_norm = mm(dqkv[0, at, :], wq[0], NT)
        for g in range(1, pairs // 2):
            d_norm += mm(dqkv[g, at, :], wq[g], NT)
        rows = tok[at, :].astype(F32)
        center = rows - jnp.mean(rows, axis=-1, keepdims=True)
        scale = lax.rsqrt(jnp.mean(center * center, axis=-1, keepdims=True) + 1e-06)
        unit = center * scale
        small_acc[0, 0:1, :] += jnp.sum(d_norm * unit, axis=0, keepdims=True)
        small_acc[0, 1:2, :] += jnp.sum(d_norm, axis=0, keepdims=True)
        d_unit = d_norm * vec[0:1, :]
        back = scale * (
            d_unit - jnp.mean(d_unit, axis=-1, keepdims=True) - unit * jnp.mean(d_unit * unit, axis=-1, keepdims=True)
        )
        gtok[at, :] = (dmid[at, :] + back).astype(BF)
        gtok_out(b).start()

    others = links.everyone()

    def small_copy(i):
        return remote(small_acc.at[i], small_recv.at[i], small_send.at[i], small_got.at[i], others[i])

    small_copy(0).start()
    at_tick = first_tick + blocks
    for i in range(len(others)):
        tick(at_tick + i)
        small_copy(i).wait_recv()
        small_acc[i + 1] = small_acc[i] + small_recv[i]
        if i + 1 < len(others):
            small_copy(i + 1).start()
    small_out[...] = small_acc[len(others)]
    at_tick = at_tick + len(others)
    last = max(last_tick(lags, TURNS), last_tick(late_lags, LATE_TURNS), last_tick(half_lags, HALF_TURNS))

    @pl.loop(at_tick, last)
    def _(t):
        tick(t)

    red.finish()
    late.finish()
    half.finish()
    for i in range(len(others)):
        small_copy(i).wait_send()
    for b in range(blocks):
        gtok_out(b).wait()


def backward_call(ndp, places, vec, small, qkv, ext, hot, page_k, bias, dext, datt, normt, wq, tok, dmid, parts, half):
    count, width = datt.shape
    bits = ndp.bit_length() - 1
    n, m, q = len(ORDER), len(EARLY), len(HALF)
    last_extra = max(0, bits - 2)
    extra = max(0, bits - 3)
    stages = 2 + 2 * min(3, bits) + extra
    tall = pltpu.VMEM((count, width), BF)
    side = pltpu.VMEM((count, 128), BF)
    pair = pltpu.VMEM((2, count, 256), BF)
    return pl.pallas_call(
        functools.partial(backward_kernel, ndp),
        out_shape=[
            jax.ShapeDtypeStruct((count, width), BF),
            jax.ShapeDtypeStruct((n, 2, 2, 2, 48, 384), BF),
            jax.ShapeDtypeStruct((m, 2, 2, 2, 48, 384), BF),
            jax.ShapeDtypeStruct((q, 2, 2, 48, 384), BF),
            jax.ShapeDtypeStruct(small.shape, F32),
        ],
        in_specs=[VMEM] * 5 + [ANY] * 4 + [VMEM] + [ANY] * 8,
        out_specs=[ANY] * 4 + [VMEM],
        scratch_shapes=[
            pltpu.VMEM(qkv.shape, BF),
            side,
            side,
            side,
            side,
            tall,
            pltpu.VMEM((width, count), BF),
            pltpu.VMEM(wq.shape, BF),
            tall,
            pltpu.VMEM((count, width), F32),
            tall,
            pltpu.VMEM((3, count, width), BF),
            pair,
            pair,
            pair,
            pltpu.VMEM((count, 256), BF),
            pltpu.VMEM((128, count), BF),
            pltpu.VMEM((128, count), F32),
            pltpu.VMEM((64, count), BF),
            pltpu.VMEM((64, 128), F32),
            pltpu.VMEM((width // 128, 2, 128), F32),
            pltpu.VMEM((2, 2, 2, 2, 2, 2, 48, 384), BF),
            pltpu.VMEM((q, 2, 2, 2, 2, 48, 384), BF),
            pltpu.VMEM((n, 2, 2, 2, 2, 48, 384), BF),
            pltpu.VMEM((n, 2, 2, 2, 2, 48, 384), BF),
            pltpu.VMEM((n, 2, 2, 2, 48, 384), BF),
            pltpu.VMEM((n, 2, 2, 48, 384), BF),
            pltpu.VMEM((n, 2, 48, 384), BF),
            pltpu.VMEM((n, 48, 384), BF),
            pltpu.VMEM((m, 2, 2, 48, 384), BF),
            pltpu.VMEM((m, 2, 2, 2, 48, 384), BF),
            pltpu.VMEM((m, 2, 48, 384), BF),
            pltpu.VMEM((m, 48, 384), BF),
            pltpu.VMEM((q, 2, 2, 2, 48, 384), BF),
            pltpu.VMEM((q, 2, 2, 48, 384), BF),
            pltpu.VMEM((q, 2, 2, 2, 48, 384), BF),
            pltpu.VMEM((q, 2, 2, 48, 384), BF),
            pltpu.VMEM((q, 2, 48, 384), BF),
            pltpu.VMEM((q, 48, 384), BF),
            pltpu.VMEM((extra, n, 48, 384) if extra else (1, 1, 16, 128), BF),
            pltpu.VMEM((extra, m, 48, 384) if extra else (1, 1, 16, 128), BF),
            pltpu.VMEM((last_extra, q, 48, 384) if last_extra else (1, 1, 16, 128), BF),
            pltpu.VMEM((bits + 3,) + small.shape, F32),
            pltpu.VMEM((bits + 2,) + small.shape, F32),
            pltpu.SemaphoreType.DMA((10,)),
            pltpu.SemaphoreType.DMA((count // 256,)),
            pltpu.SemaphoreType.DMA((n,)),
            pltpu.SemaphoreType.DMA((stages, n)),
            pltpu.SemaphoreType.DMA((stages, n)),
            pltpu.SemaphoreType.DMA((n,)),
            pltpu.SemaphoreType.DMA((m,)),
            pltpu.SemaphoreType.DMA((stages, m)),
            pltpu.SemaphoreType.DMA((stages, m)),
            pltpu.SemaphoreType.DMA((m,)),
            pltpu.SemaphoreType.DMA((q,)),
            pltpu.SemaphoreType.DMA((stages, q)),
            pltpu.SemaphoreType.DMA((stages, q)),
            pltpu.SemaphoreType.DMA((q,)),
            pltpu.SemaphoreType.DMA((bits + 2,)),
            pltpu.SemaphoreType.DMA((bits + 2,)),
        ],
        compiler_params=pltpu.CompilerParams(vmem_limit_bytes=LIMIT, collective_id=1, has_side_effects=True),
        name="backward",
    )(*places, vec, small, qkv, ext, hot, page_k, bias, dext, datt, normt, wq, tok, dmid, parts, half)


def finish_kernel(
    total_h,
    late_h,
    last_h,
    layer_i,
    gtok_i,
    small,
    layer_h,
    gtok_h,
    wqkv_h,
    rel,
    wout_h,
    wup_h,
    bup,
    wdown_h,
    v0,
    v1,
    v2,
    v3,
    v4,
    v5,
    v6,
    total,
    late,
    last,
    wqkv,
    wout,
    wup,
    wdown,
    layer,
    gtok,
    in_sem,
    out_sem,
):
    f = lax.axis_index("fsdp")
    own = v0.shape[0]
    n, m = total.shape[0], late.shape[0]
    loads = [pltpu.make_async_copy(late_h.at[i], late.at[i], in_sem.at[i]) for i in range(m)]
    loads += [pltpu.make_async_copy(total_h.at[i], total.at[i], in_sem.at[m + i]) for i in range(n)]
    loads.append(pltpu.make_async_copy(last_h, last, in_sem.at[m + n]))
    through = [(layer_i, layer, layer_h), (gtok_i, gtok, gtok_h)]
    loads += [pltpu.make_async_copy(src, mid, in_sem.at[m + n + 1 + i]) for i, (src, mid, _) in enumerate(through)]
    for copy in loads:
        copy.start()
    pending = []

    def leave(src, dst):
        copy = pltpu.make_async_copy(src, dst, out_sem.at[len(pending)])
        copy.start()
        pending.append(copy)

    for h in range(m // 2):
        for i in (2 * h, 2 * h + 1):
            loads[i].wait()
        sides = []
        for c in range(2):
            rows = [late[2 * h + i, c, r // 2, r % 2].astype(F32) for i in range(2) for r in range(4)]
            sides.append(jnp.concatenate(rows, axis=0).T)
        for c in range(2):
            wdown[384 * c : 384 * c + 384, 384 * h : 384 * h + 384] = sides[c]
    leave(wdown, wdown_h)
    for i, (_, mid, dst) in enumerate(through):
        loads[m + n + 1 + i].wait()
        leave(mid, dst)
    for i, (kind, j) in enumerate(ORDER):
        loads[m + i].wait()
        for c in range(2):
            for r in range(4):
                at = slice(48 * r, 48 * r + 48)
                value = total[i, c, r // 2, r % 2].astype(F32)
                if kind == "g" and j < 4:
                    wup[at, 768 * j + 384 * c : 768 * j + 384 * c + 384] = value
                elif kind == "g":
                    wout[at, 384 * c : 384 * c + 384] = value
                else:
                    for part in range(3):
                        start = 768 * part + 256 * j + 128 * c
                        wqkv[at, start : start + 128] = value[:, 128 * part : 128 * part + 128]
    leave(wup, wup_h)
    leave(wout, wout_h)
    loads[m + n].wait()
    for i in range(last.shape[0]):
        for r in range(4):
            value = last[i, r // 2, r % 2].astype(F32)
            for part in range(3):
                start = 768 * part + 128 * (4 + i)
                wqkv[48 * r : 48 * r + 48, start : start + 128] = value[:, 128 * part : 128 * part + 128]
    leave(wqkv, wqkv_h)

    def mine(rows, width, stride):
        out = jnp.zeros((rows.stop - rows.start, width), F32)
        for k in range(4):
            out = jnp.where(f == k, small[rows, stride * k : stride * k + width], out)
        return out

    vectors = mine(slice(0, 8), own, own)
    for i, ref in enumerate((v0, v1, v2, v3, v4, v5, v6)):
        ref[...] = vectors[i : i + 1, :].reshape(own)
    line = jnp.zeros((1, bup.shape[0]), F32)
    for k in range(4):
        line = jnp.where(f == k, small[8 + k : 9 + k, :], line)
    bup[...] = line.reshape(bup.shape[0])
    offsets = rel.shape[2]
    for i in range(rel.shape[0]):
        for axis in range(2):
            value = jnp.zeros((1, offsets), F32)
            for k in range(4):
                head = rel.shape[0] * k + i
                start = 64 * (1 - head % 2)
                at = 12 + 2 * (head // 2) + axis
                value = jnp.where(f == k, small[at : at + 1, start : start + offsets], value)
            rel[i, axis : axis + 1, :] = value
    for copy in pending:
        copy.wait()


def finish_call(total, late, last, layer, gtok, small, own, rel):
    width = small.shape[1]
    vec = jax.ShapeDtypeStruct((own,), F32)
    shapes = [(own, 3 * width), (own, width), (own, 4 * width), (4 * own, width)]
    wqkv, wout, wup, wdown = [jax.ShapeDtypeStruct(s, F32) for s in shapes]
    return pl.pallas_call(
        finish_kernel,
        out_shape=[jax.ShapeDtypeStruct(layer.shape, BF), jax.ShapeDtypeStruct(gtok.shape, BF)]
        + [wqkv, jax.ShapeDtypeStruct(rel.shape, F32), wout, wup, jax.ShapeDtypeStruct((4 * own,), F32), wdown]
        + [vec] * 7,
        in_specs=[ANY] * 5 + [VMEM],
        out_specs=[ANY, ANY, ANY, VMEM, ANY, ANY, VMEM, ANY] + [VMEM] * 7,
        scratch_shapes=[pltpu.VMEM(x.shape, BF) for x in (total, late, last)]
        + [pltpu.VMEM(s, F32) for s in shapes]
        + [pltpu.VMEM(layer.shape, BF), pltpu.VMEM(gtok.shape, BF)]
        + [pltpu.SemaphoreType.DMA((total.shape[0] + late.shape[0] + 3,)), pltpu.SemaphoreType.DMA((6,))],
        compiler_params=pltpu.CompilerParams(vmem_limit_bytes=LIMIT),
        name="finish",
    )(total, late, last, layer, gtok, small)


def local(
    tokens,
    cotangent,
    page_id,
    pos_row,
    pos_col,
    ln1_gain,
    ln1_shift,
    w_qkv,
    rel_table,
    w_out,
    scale_attn,
    ln2_gain,
    ln2_shift,
    w_up,
    b_up,
    w_down,
    b_down,
    scale_mlp,
):
    ndp = lax.axis_size("dp")
    count, width = tokens.shape
    places = [x.reshape(count // 128, 128) for x in (page_id, pos_row, pos_col)]
    vectors = [ln1_gain, ln1_shift, scale_attn, ln2_gain, ln2_shift, b_down, scale_mlp]
    normt, qkv, att, ext, hot, page_k, bias, vec, wq, wout, wup, wdown = forward_call(
        ndp, places, vectors, b_up, rel_table, tokens, w_qkv, w_out, w_up, w_down
    )
    wq = wq.reshape(-1, width, width)
    wout = wout.reshape(width, width)
    wup = wup.reshape(-1, width, width)
    wdown = wdown.reshape(-1, width)
    layer_out, d_mid, d_att, d_ext, parts, early, small = middle_call(ndp, tokens, cotangent, att, ext, vec, wout, wup, wdown)
    grad_tokens, total, late, last, small = backward_call(
        ndp, places, vec, small, qkv, ext, hot, page_k, bias, d_ext, d_att, normt, wq, tokens, d_mid, parts, early
    )
    layer_out, grad_tokens, g_wqkv, g_rel, g_wout, g_wup, g_bup, g_wdown, *g = finish_call(
        total, late, last, layer_out, grad_tokens, small, ln1_gain.shape[0], rel_table
    )
    return (
        layer_out,
        grad_tokens,
        g[0],
        g[1],
        g_wqkv,
        g_rel,
        g_wout,
        g[2],
        g[3],
        g[4],
        g_wup,
        g_bup,
        g_wdown,
        g[5],
        g[6],
    )


def solution(mesh):
    rows = P(("dp", "fsdp"))
    slab = P(("dp", "fsdp"), None)
    vec = P("fsdp")
    mat = P("fsdp", None)
    cube = P("fsdp", None, None)
    in_specs = (slab, slab, rows, rows, rows, vec, vec, mat, cube, mat, vec, vec, vec, mat, vec, mat, vec, vec)
    out_specs = (slab, slab, vec, vec, mat, cube, mat, vec, vec, vec, mat, vec, mat, vec, vec)
    return jax.shard_map(local, mesh=mesh, in_specs=in_specs, out_specs=out_specs, check_vma=False)
```

```python
import functools

import jax
import jax.numpy as jnp
from jax import lax
from jax.experimental import pallas as pl
from jax.experimental.pallas import tpu as pltpu
from jax.sharding import PartitionSpec as P

F32 = jnp.float32
BF = jnp.bfloat16
NT = (((1,), (1,)), ((), ()))
NN = (((1,), (0,)), ((), ()))
VMEM = pl.BlockSpec(memory_space=pltpu.VMEM)
ANY = pl.BlockSpec(memory_space=pl.ANY)
MESH = pl.DeviceIdType.MESH
LIMIT = 63 << 20
MASKED = -1e30


def mm(a, b, dims=NN):
    return lax.dot_general(a, b, dims, preferred_element_type=F32)


def lanes(rows, width=128):
    return lax.broadcasted_iota(jnp.int32, (rows, width), 1)


def normalize(rows, gain, shift):
    center = rows - jnp.mean(rows, axis=-1, keepdims=True)
    spread = jnp.mean(center * center, axis=-1, keepdims=True)
    return center * lax.rsqrt(spread + 1e-06) * gain + shift


def pieces(x, lane):
    hi = x.astype(BF)
    rest = x - hi.astype(F32)
    mid = rest.astype(BF)
    low = (rest - mid.astype(F32)).astype(BF)
    third = lane % 3
    return jnp.where(third == 0, hi.astype(F32), jnp.where(third == 1, mid.astype(F32), low.astype(F32)))


def position_columns(pages, rows, cols, hot, page_q, page_k):
    for r in range(pages.shape[0]):
        code = (pages[r : r + 1, :] + 1) * 4096 + rows[r : r + 1, :] * 64 + cols[r : r + 1, :]
        code = jnp.broadcast_to(code.astype(F32), (128, 128)).T.astype(jnp.int32)
        lane = lanes(128)
        page, row, col = code >> 12, (code >> 6) & 63, code & 63
        near = lane & 63
        where = jnp.where(near < 32, row, col + 32)
        at = pl.ds(r * 128, 128)
        hot[at, :] = jnp.where(where == near, 1.0, 0.0).astype(BF)
        page_q[at, :] = jnp.where(page == lane, 1.0, 0.0)
        page_k[at, :] = jnp.where((lane < 6) & (page != lane), MASKED, 0.0).astype(BF)


def toeplitz(table, bias):
    lane = lanes(32)
    for p in range(bias.shape[0]):
        for axis in range(2):
            parts = []
            for head, at in ((2 * p + 1, 32 * axis), (2 * p, 64 + 32 * axis)):
                row = jnp.broadcast_to(table[2 * head + axis : 2 * head + axis + 1, :], (32, 128))
                rolled = pltpu.roll(row, (97 + at) % 128, axis=1, stride=1, stride_axis=0)
                parts.append(jnp.where((lane >= at) & (lane < at + 32), rolled, 0.0))
            bias[p, 32 * axis : 32 * axis + 32, :] = (parts[0] + parts[1]).astype(BF)


class Links:
    def __init__(self, ndp):
        self.dp, self.f = lax.axis_index("dp"), lax.axis_index("fsdp")
        self.core, self.x = self.f % 2, self.f // 2
        self.bits = ndp.bit_length() - 1
        self.bit = [(self.dp // 2**k) % 2 for k in range(self.bits)]

    def partner(self, kind, k=0):
        if kind == "core":
            return (self.dp, self.f + 1 - 2 * self.core)
        if kind == "x":
            return (self.dp, self.f + 2 - 4 * self.x)
        return (self.dp + (1 - 2 * self.bit[k]) * 2**k, self.f)

    def everyone(self):
        return [self.partner("core"), self.partner("x")] + [self.partner("dp", k) for k in range(self.bits)]

    def greet(self, others):
        barrier = pltpu.get_barrier_semaphore()
        for other in others:
            pl.semaphore_signal(barrier, inc=1, device_id=other, device_id_type=MESH)
        pl.semaphore_wait(barrier, len(others))


def remote(src, dst, send, recv, device):
    return pltpu.make_async_remote_copy(
        src_ref=src, dst_ref=dst, send_sem=send, recv_sem=recv, device_id=device, device_id_type=MESH
    )


def pick_index(n, table):
    out = 0
    for i, v in enumerate(table):
        if v:
            out = out + jnp.where(n == i, v, 0)
    return out


class Reduction:
    def __init__(self, links, halvings, order, homes, first, last, acc, recv, final, out_h, load_sem, send_sem, recv_sem, out_sem):
        self.l, self.order, self.homes, self.first = links, order, homes, first
        self.acc, self.recv, self.final, self.out_h = acc, recv, final, out_h
        self.load_sem, self.send_sem, self.recv_sem, self.out_sem = load_sem, send_sem, recv_sem, out_sem
        self.depth = max(0, first - 1)
        self.halvings = halvings
        self.halved = 1 + halvings
        self.extra = links.bits - halvings
        self.stages = 2 + 2 * halvings + self.extra
        self.last = self.stages if last is None else last
        self.kept = (links.x,) + tuple(links.bit[:halvings])

    def sems(self, k, n):
        return self.send_sem.at[k, n], self.recv_sem.at[k, n]

    def partner(self, k):
        l = self.l
        if k == 0:
            return l.partner("core")
        if k == 1:
            return l.partner("x")
        j = k - 2 if k <= self.halved + self.extra else self.halvings - 1 - (k - 1 - self.halved - self.extra)
        return l.partner("dp", j)

    def copy(self, k, n):
        l = self.l
        if k <= self.halved:
            at = (n,) + self.kept[self.depth : k - 1] + (1 - self.kept[k - 1],)
            return remote(self.acc.at[at], self.recv[k].at[n], *self.sems(k, n), self.partner(k))
        if k <= self.halved + self.extra:
            return remote(self.final.at[(n,) + self.kept[1:]], self.recv[k].at[n], *self.sems(k, n), self.partner(k))
        j = self.halvings - 1 - (k - 1 - self.halved - self.extra)
        at = (n,) + self.kept[1 : 2 + j]
        return remote(self.final.at[at], self.final.at[at], *self.sems(k, n), self.partner(k))

    def opening(self, n, act):
        l = self.l
        for kind in sorted(self.homes):
            places = [i for i, (name, _) in enumerate(self.order) if name == kind]
            mine = pick_index(n, [i for _, i in self.order])
            home = self.homes[kind]

            @pl.when(sum(jnp.where(n == i, 1, 0) for i in places) > 0)
            def _(home=home):
                if self.first == 0:
                    act(
                        lambda: remote(
                            home.at[mine, 1 - l.core], self.recv[0].at[n], *self.sems(0, n), self.partner(0)
                        ),
                        lambda: pltpu.make_async_copy(home.at[mine, l.core], self.acc.at[n], self.load_sem.at[n]),
                    )
                else:
                    act(None, lambda: pltpu.make_async_copy(home.at[mine], self.acc.at[n], self.load_sem.at[n]))

    def out(self, n):
        if self.last == self.stages:
            return pltpu.make_async_copy(self.final.at[n], self.out_h.at[n], self.out_sem.at[n])
        src = self.acc.at[(n,) + self.kept[self.depth : self.last - 1]]
        return pltpu.make_async_copy(src, self.out_h.at[n], self.out_sem.at[n])

    def launch(self, n):
        def start(send, load):
            if send is not None:
                send().start()
            load().start()

        self.opening(n, start)

    def step(self, k, n):
        l = self.l

        def arrive(send, load):
            if send is not None:
                send().wait_recv()
            load().wait()

        if k == max(self.first, 1):
            self.opening(n, arrive)
            if self.first == 0:
                self.acc[n] = self.acc[n] + self.recv[0][n]
        elif k <= self.halved:
            self.copy(k - 1, n).wait_recv()
            at = (n,) + self.kept[self.depth : k - 1]
            self.acc[at] = self.acc[at] + self.recv[k - 1][n]
        elif k == self.halved + 1:
            self.copy(k - 1, n).wait_recv()
            at = (n,) + self.kept[self.depth :]
            self.final[(n,) + self.kept[1:]] = self.acc[at] + self.recv[k - 1][n]
        elif k <= self.halved + self.extra + 1:
            self.copy(k - 1, n).wait()
            at = (n,) + self.kept[1:]
            self.final[at] = self.final[at] + self.recv[k - 1][n]
        else:
            self.copy(k - 1, n).wait_recv()
        if k < self.last:
            self.copy(k, n).start()
        else:
            self.out(n).start()

    def tick(self, turn, r, start, period, lags):
        for k, lag in sorted(lags.items(), reverse=True):
            if (start + lag - r) % period:
                continue
            n = turn - (start + lag - r) // period
            if isinstance(n, int):
                if 0 <= n < len(self.order):
                    self.launch(n) if k == -1 else self.step(k, n)
                continue

            @pl.when((n >= 0) & (n < len(self.order)))
            def _(k=k, n=n):
                if k == -1:
                    self.launch(n)
                else:
                    self.step(k, n)

    def finish(self):
        l = self.l

        @pl.loop(0, len(self.order))
        def _(n):
            if self.first == 0:
                self.opening(n, lambda send, load: send().wait_send())
            for k in range(max(1, self.first), self.last):
                if not self.halved < k <= self.halved + self.extra:
                    self.copy(k, n).wait_send()
            self.out(n).wait()


def lag_table(first, last, start, step, special):
    table = {-1: start}
    at = start
    for k in range(max(1, first), last + 1):
        at += special.get(k, step)
        table[k] = at
    return table


def last_tick(start, period, count, lags):
    return start + period * (count - 1) + max(lags.values()) + 1


class Weights:
    def __init__(self, links, own, home, send_sem, recv_sem, keep_sem):
        self.l, self.own, self.home = links, own, home
        self.send_sem, self.recv_sem, self.keep_sem = send_sem, recv_sem, keep_sem
        l = links
        self.f = l.f
        self.y = l.bit[0]
        self.sibling = l.f + 1 - 2 * l.core
        self.across = l.f + 2 - 4 * l.x
        self.halves = (pl.ds(pl.multiple_of(self.y * 96, 32), 96), pl.ds(pl.multiple_of((1 - self.y) * 96, 32), 96))

    def branch(self, n, act):
        for (low, high), own, home in zip(((0, 3), (3, 4), (4, 8), (8, 12)), self.own, self.home):

            @pl.when((n >= low) & (n < high))
            def _(low=low, own=own, home=home):
                act(own(n - low), lambda f: home(n - low, f), low > 0)

    def copies(self, n, own, home):
        l, (this, other) = self.l, self.halves
        s = [(self.send_sem.at[k, n], self.recv_sem.at[k, n]) for k in range(5)]
        mine, across = home(self.f), home(self.across)
        sibling = l.partner("core")
        return [
            lambda: remote(own, mine, *s[0], sibling),
            lambda: remote(own.at[this, :], mine.at[this, :], *s[1], l.partner("x")),
            lambda: remote(across.at[this, :], across.at[this, :], *s[2], l.partner("dp", 0)),
            lambda: remote(across.at[this, :], across.at[this, :], *s[3], sibling),
            lambda: remote(across.at[other, :], across.at[other, :], *s[4], sibling),
        ]

    def step(self, k, n):
        def act(own, home, keep):
            copies = self.copies(n, own, home)
            if k == 0:
                copies[1]().start()
                copies[0]().start()
                if keep:
                    pltpu.make_async_copy(own, home(self.f), self.keep_sem.at[n]).start()
            elif k == 1:
                copies[1]().wait_recv()
                copies[2]().start()
                copies[3]().start()
            elif k == 2:
                copies[2]().wait_recv()
                copies[4]().start()
            elif k == 3:
                for i in (0, 3, 4):
                    copies[i]().wait_recv()
            else:
                for copy in copies:
                    copy().wait_send()
                if keep:
                    pltpu.make_async_copy(own, home(self.f), self.keep_sem.at[n]).wait()

        self.branch(n, act)

    def tick(self, t):
        for k, lag in ((3, 7), (2, 4), (1, 0)):
            m = t - lag + 128
            n = m // 2 - 63

            @pl.when((m % 2 == 0) & (n >= 1) & (n < 12))
            def _(k=k, n=n):
                self.step(k, n)
                if k == 1:

                    @pl.when(n + 3 < 12)
                    def _():
                        self.step(0, n + 3)


def pack_own(mine, vectors, bup, table):
    own = vectors[0].shape[0]
    mine[...] = jnp.zeros_like(mine)
    for i, ref in enumerate(vectors):
        mine[i : i + 1, 0:own] = ref[...].astype(F32).reshape(1, own)
    line = bup[...].astype(F32).reshape(1, bup.shape[0])
    for i in range(4):
        mine[7 + i : 8 + i, 0:own] = line[:, own * i : own * i + own]
    for h in range(table.shape[0]):
        for axis in range(2):
            at = 11 + 2 * h + axis
            mine[at : at + 1, 0 : table.shape[2]] = table[h, axis : axis + 1, :].astype(F32)


def unpack(shards, vec, table, own):
    for v in range(7):
        vec[v : v + 1, :] = jnp.concatenate([shards[f, v : v + 1, 0:own] for f in range(4)], axis=1)
    for f in range(4):
        vec[8 + f : 9 + f, :] = jnp.concatenate([shards[f, 7 + i : 8 + i, 0:own] for i in range(4)], axis=1)
        table[6 * f : 6 * f + 6, :] = shards[f, 11:17, 0:128]


def forward_kernel(
    ndp,
    page,
    row,
    col,
    v0,
    v1,
    v2,
    v3,
    v4,
    v5,
    v6,
    bup,
    rel,
    tok_h,
    wqkv_h,
    wout_s,
    wup_s,
    wdown_s,
    normt_h,
    qkv_h,
    att_h,
    ext_h,
    hot_h,
    page_k_h,
    bias,
    vec,
    wq_h,
    wout_h,
    wup_h,
    wdown_h,
    tok,
    norm,
    normt,
    qkv,
    att,
    ext,
    hot,
    page_k,
    lse,
    ka,
    va,
    wq,
    mine,
    shards,
    table,
    tok_sem,
    mine_sem,
    local_sem,
    pack_send,
    pack_got,
    send_sem,
    recv_sem,
    keep_sem,
    out_sem,
    group_sem,
):
    count, width = tok.shape
    pairs = bias.shape[0]
    blocks = count // 256
    links = Links(ndp)
    tok_copy = pltpu.make_async_copy(tok_h, tok, tok_sem)
    tok_copy.start()

    def own_group(g):
        return [
            pltpu.make_async_copy(
                wqkv_h.at[:, width * part + 256 * g + 128 * s : width * part + 256 * g + 128 * s + 128],
                wq.at[g, links.f, :, 384 * s + 128 * part : 384 * s + 128 * part + 128],
                local_sem.at[g, 3 * s + part],
            )
            for s in range(2)
            for part in range(3)
        ]

    for g in range(3):
        for copy in own_group(g):
            copy.start()
    own_loads = [pltpu.make_async_copy(wout_s, mine.at[0], mine_sem.at[0])]
    for j in range(4):
        part = pl.ds(j * width, width)
        own_loads.append(pltpu.make_async_copy(wup_s.at[:, part], mine.at[1 + j], mine_sem.at[1 + j]))
    for j in range(4):
        part = pl.ds(j * 192, 192)
        own_loads.append(pltpu.make_async_copy(wdown_s.at[part, :], mine.at[5 + j], mine_sem.at[5 + j]))
    for copy in own_loads:
        copy.start()
    pack_own(shards.at[links.f], [v0, v1, v2, v3, v4, v5, v6], bup, rel)
    diagonal = (links.dp, 3 - links.f)
    peers = [links.partner("core"), links.partner("x"), diagonal]
    barrier = pltpu.get_barrier_semaphore()
    for other in peers + [links.partner("dp", 0)]:
        pl.semaphore_signal(barrier, inc=1, device_id=other, device_id_type=MESH)
    pl.semaphore_wait(barrier, 4)

    gather = Weights(
        links,
        [
            lambda j: wq.at[j, links.f],
            lambda j: mine.at[j],
            lambda j: mine.at[1 + j],
            lambda j: mine.at[5 + j],
        ],
        [
            lambda j, f: wq.at[j, f],
            lambda j, f: wout_h.at[f],
            lambda j, f: wup_h.at[j, f],
            lambda j, f: wdown_h.at[f, j],
        ],
        send_sem,
        recv_sem,
        keep_sem,
    )

    def pack_copy(i):
        return remote(shards.at[links.f], shards.at[links.f], pack_send.at[i], pack_got.at[i], peers[i])

    for copy in own_group(0):
        copy.wait()
    gather.step(0, 0)
    for i in range(3):
        pack_copy(i).start()
    for g in (1, 2):
        for copy in own_group(g):
            copy.wait()
    for copy in own_loads:
        copy.wait()
    gather.step(0, 1)
    gather.step(0, 2)
    gather.step(0, 3)
    position_columns(page, row, col, hot, lse, page_k)
    for i in range(3):
        pack_copy(i).wait_recv()
    vec[...] = jnp.zeros_like(vec)
    unpack(shards, vec, table, v0.shape[0])
    toeplitz(table, bias)
    tok_copy.wait()

    @pl.loop(0, blocks)
    def _(b):
        at = pl.ds(pl.multiple_of(b * 256, 256), 256)
        rows = normalize(tok[at, :].astype(F32), vec[0:1, :], vec[1:2, :]).astype(BF)
        norm[at, :] = rows
        normt[:, at] = rows.T

    outs = [
        pltpu.make_async_copy(src, dst, out_sem.at[i])
        for i, (src, dst) in enumerate([(normt, normt_h), (hot, hot_h), (page_k, page_k_h), (att, att_h), (ext, ext_h)])
    ]
    for copy in outs[:3]:
        copy.start()
    for k in (1, 2, 3):
        gather.step(k, 0)
    low_half = lanes(count) < 64

    def group_out(g):
        copies = [pltpu.make_async_copy(wq.at[g], wq_h.at[g], group_sem.at[3, g])]
        for part in range(3):
            some = pl.ds(part * pairs + 2 * g, 2)
            copies.append(pltpu.make_async_copy(qkv.at[some], qkv_h.at[some], group_sem.at[part, g]))
        return copies

    @pl.loop(0, pairs // 2)
    def _(g):
        @pl.loop(0, blocks)
        def _(b):
            at = pl.ds(pl.multiple_of(b * 256, 256), 256)
            block = mm(norm[at, :], wq[g].reshape(width, width)).astype(BF)
            for s in range(2):
                for part in range(3):
                    value = block[:, 384 * s + 128 * part : 384 * s + 128 * part + 128]
                    qkv[part * pairs + 2 * g + s, at, :] = value if part else value * jnp.asarray(0.125, BF)

        for copy in group_out(g):
            copy.start()

        @pl.loop(0, 2)
        def _(s):
            p = 2 * g + s
            keys, values = qkv[pairs + p], qkv[2 * pairs + p]
            side = mm(hot[:, :64], bias[p]).astype(BF)
            one = jnp.ones_like(values)
            ka[0, :, :128] = jnp.where(low_half, keys, side)
            ka[1, :, :128] = jnp.where(low_half, side, keys)
            va[0] = jnp.where(low_half, values, one)
            va[1] = jnp.where(low_half, one, values)
            for e in range(2):
                ka[e, :, 128:] = page_k[...]

            @pl.loop(0, blocks)
            def _(b):
                gather.tick(p * blocks + b)
                at = pl.ds(pl.multiple_of(b * 256, 256), 256)
                queries, places = qkv[p, at, :], hot[at, :]
                kept = lse[at, :]
                lane = lanes(256)
                half = lane < 64
                page_hot = jnp.where(lane < 6, kept, 0.0).astype(BF)
                results = []
                for e in range(2):
                    first = jnp.where(half, queries, places) if e == 0 else jnp.where(half, places, queries)
                    scores = mm(jnp.concatenate([first, page_hot], axis=1), ka[e], NT)
                    top = jnp.max(scores, axis=1, keepdims=True)
                    expo = jnp.exp(scores - top).astype(BF)
                    out = mm(expo, va[e])
                    turned = pltpu.roll(out, 64, axis=1)
                    total = jnp.where(half, turned, out) if e == 0 else jnp.where(half, out, turned)
                    results.append(out / total)
                    kept = jnp.where(lane // 3 == 2 + 2 * p + e, top + jnp.log(total), kept)
                lse[at, :] = kept
                att[at, pl.ds(pl.multiple_of(p * 128, 128), 128)] = jnp.where(half, results[0], results[1]).astype(BF)

    lane = lanes(256)

    @pl.loop(0, blocks)
    def _(b):
        at = pl.ds(pl.multiple_of(b * 256, 256), 256)
        ext[at, :] = jnp.where(lane < 6, lse[at, :], pieces(lse[at, :], lane)).astype(BF)

    for copy in outs[3:]:
        copy.start()
    @pl.loop(pairs * blocks, 28)
    def _(t):
        gather.tick(t)


    @pl.loop(0, 12)
    def _(n):
        gather.step(4, n)

    for i in range(3):
        pack_copy(i).wait_send()

    @pl.loop(0, pairs // 2)
    def _(g):
        for copy in group_out(g):
            copy.wait()

    for copy in outs:
        copy.wait()


def forward_call(ndp, places, vectors, bup, rel, tok, wqkv, wout, wup, wdown):
    count, width = tok.shape
    pairs = width // 128
    tall = pltpu.VMEM((count, width), BF)
    side = pltpu.VMEM((count, 128), BF)
    return pl.pallas_call(
        functools.partial(forward_kernel, ndp),
        out_shape=[
            jax.ShapeDtypeStruct((width, count), BF),
            jax.ShapeDtypeStruct((3 * pairs, count, 128), BF),
            jax.ShapeDtypeStruct((count, width), BF),
            jax.ShapeDtypeStruct((count, 128), BF),
            jax.ShapeDtypeStruct((count, 128), BF),
            jax.ShapeDtypeStruct((count, 128), BF),
            jax.ShapeDtypeStruct((pairs, 64, 128), BF),
            jax.ShapeDtypeStruct((12, width), F32),
            jax.ShapeDtypeStruct((3, 4, 192, width), BF),
            jax.ShapeDtypeStruct((4, 192, width), BF),
            jax.ShapeDtypeStruct((4, 4, 192, width), BF),
            jax.ShapeDtypeStruct((4, 4, 192, width), BF),
        ],
        in_specs=[VMEM] * 12 + [ANY] * 5,
        out_specs=[ANY] * 6 + [VMEM] * 2 + [ANY] * 4,
        scratch_shapes=[
            tall,
            tall,
            pltpu.VMEM((width, count), BF),
            pltpu.VMEM((3 * pairs, count, 128), BF),
            tall,
            side,
            side,
            side,
            pltpu.VMEM((count, 128), F32),
            pltpu.VMEM((2, count, 256), BF),
            pltpu.VMEM((2, count, 128), BF),
            pltpu.VMEM((3, 4, 192, width), BF),
            pltpu.VMEM((9, 192, width), BF),
            pltpu.VMEM((4, 24, 256), F32),
            pltpu.VMEM((24, 128), F32),
            pltpu.SemaphoreType.DMA,
            pltpu.SemaphoreType.DMA((9,)),
            pltpu.SemaphoreType.DMA((3, 6)),
            pltpu.SemaphoreType.DMA((3,)),
            pltpu.SemaphoreType.DMA((3,)),
            pltpu.SemaphoreType.DMA((5, 12)),
            pltpu.SemaphoreType.DMA((5, 12)),
            pltpu.SemaphoreType.DMA((12,)),
            pltpu.SemaphoreType.DMA((5,)),
            pltpu.SemaphoreType.DMA((4, 3)),
        ],
        compiler_params=pltpu.CompilerParams(vmem_limit_bytes=LIMIT, collective_id=0, has_side_effects=True),
        name="forward",
    )(*places, *vectors, bup, rel, tok, wqkv, wout, wup, wdown)


def gelu_both(u):
    c = 0.7978845608028654
    square = u * u
    t = jnp.tanh(c * u * (1.0 + 0.044715 * square))
    half = 0.5 + 0.5 * t
    slope = half + (0.5 * c) * u * (1.0 - t * t) * (1.0 + 0.134145 * square)
    return u * half, slope


EARLY = [("d", 0), ("d", 1), ("d", 2)]
EARLY_STOP = 3
EARLY_PERIOD = 4
EARLY_LAGS = {1: 0, 2: 8, 3: 12}


def middle_kernel(
    ndp,
    tok_h,
    cot_h,
    att_h,
    ext_h,
    vec,
    wout_h,
    wup_h,
    wdown_h,
    layer_h,
    dmid_h,
    datt_h,
    dext_h,
    part_h,
    half_h,
    small,
    tok,
    cot,
    att,
    ext,
    wout,
    wup,
    wdown,
    act,
    dup,
    n2t,
    ddt,
    att_t,
    ddown,
    dproj,
    layer,
    dmid,
    datt,
    dext,
    stage,
    own,
    acc,
    r0,
    r1,
    r2,
    in_sem,
    out_sem,
    layer_sem,
    part_sem,
    spare_sem,
    load_sem,
    send_sem,
    recv_sem,
    half_sem,
):
    count, width = tok.shape
    cols = wup.shape[0]
    blocks = count // 256
    loads = []
    for i, (src, dst) in enumerate(
        [(att_h, att), (wout_h, wout), (tok_h, tok), (wup_h, wup), (wdown_h, wdown), (cot_h, cot), (ext_h, ext)]
    ):
        copy = pltpu.make_async_copy(src, dst, in_sem.at[i])
        copy.start()
        loads.append(copy)
    links = Links(ndp)
    links.greet(links.everyone()[:3])
    red = Reduction(
        links, 3, EARLY, {"d": own}, 0, EARLY_STOP, acc, [r0, r1, r2], None, half_h, load_sem, send_sem, recv_sem, half_sem
    )
    small[...] = jnp.zeros_like(small)
    head = lax.broadcasted_iota(jnp.int32, (width, 128), 0) // 64
    pick = jnp.where(lanes(width) // 3 == head, 1.0, 0.0).astype(BF)
    for copy in loads:
        copy.wait()

    def spot(b):
        return pl.ds(pl.multiple_of(b * 256, 256), 256)

    def layer_out(b):
        return pltpu.make_async_copy(layer.at[spot(b), :], layer_h.at[spot(b), :], layer_sem.at[b])

    def outs(b):
        at = spot(b)
        return [
            pltpu.make_async_copy(src.at[at, :], dst.at[at, :], out_sem.at[i, b])
            for i, (src, dst) in enumerate([(dmid, dmid_h), (datt, datt_h), (dext, dext_h)])
        ]

    def masked(at):
        return cot[at, :].astype(F32) * (1.0 - ext[at, :].astype(F32)[:, 0:1])

    def center_scale(mid):
        center = mid - jnp.mean(mid, axis=-1, keepdims=True)
        return center, lax.rsqrt(jnp.mean(center * center, axis=-1, keepdims=True) + 1e-06)

    @pl.loop(0, blocks)
    def _(b):
        at = spot(b)
        rows_att = att[at, :]
        proj = mm(rows_att, wout[...])
        mid = tok[at, :].astype(F32) + vec[2:3, :] * proj
        dmid[at, :] = mid
        datt[at, :] = proj.astype(BF)
        center, scale = center_scale(mid)
        norm = (center * scale * vec[3:4, :] + vec[4:5, :]).astype(BF)
        down = jnp.zeros((256, width), F32)
        for j in range(cols):
            u = mm(norm, wup[j]) + vec[8 + j : 9 + j, :]
            a, s = gelu_both(u)
            a = a.astype(BF)
            act[at, j * width : (j + 1) * width] = a
            dup[at, j * width : (j + 1) * width] = s.astype(BF)
            down += mm(a, wdown[j * width : (j + 1) * width, :])
        down += vec[5:6, :]
        layer[at, :] = (mid + vec[6:7, :] * down).astype(BF)
        layer_out(b).start()
        grad = masked(at)
        d_down = (grad * vec[6:7, :]).astype(BF)
        ddown[at, :] = d_down
        small[6:7, :] += jnp.sum(grad * down, axis=0, keepdims=True)
        small[5:6, :] += jnp.sum(d_down.astype(F32), axis=0, keepdims=True)
        n2t[:, at] = norm.T
        ddt[:, at] = d_down.T
        att_t[:, at] = rows_att.T

    @pl.loop(0, 2)
    def _(h):
        @pl.loop(0, cols)
        def _(j):
            col = pl.ds(pl.multiple_of(j * width, width), width)
            value = mm(ddt[pl.ds(pl.multiple_of(h * 384, 384), 384), :], act[:, col])
            for i in range(2):
                for r in range(4):
                    for c in range(2):
                        rows = slice(192 * i + 48 * r, 192 * i + 48 * r + 48)
                        own[2 * h + i, j % 2, j // 2, c, r // 2, r % 2] = value[rows, 384 * c : 384 * c + 384].astype(BF)

        red.launch(2 * h)

        @pl.when(h == 0)
        def _():
            red.launch(1)

    spare = pltpu.make_async_copy(own.at[3], part_h.at[5], spare_sem)
    spare.start()

    @pl.loop(0, blocks)
    def _(b):
        at = spot(b)
        d_down = ddown[at, :]
        d_norm = jnp.zeros((256, width), F32)
        for j in range(cols):
            red.tick(b, j, 0, EARLY_PERIOD, EARLY_LAGS)
            d_act = mm(d_down, wdown[j * width : (j + 1) * width, :], NT)
            some = slice(j * width, (j + 1) * width)
            d_up = (d_act * dup[at, some].astype(F32)).astype(BF)
            dup[at, some] = d_up
            small[8 + j : 9 + j, :] += jnp.sum(d_up.astype(F32), axis=0, keepdims=True)
            d_norm += mm(d_up, wup[j], NT)
        center, scale = center_scale(dmid[at, :])
        unit = center * scale
        small[3:4, :] += jnp.sum(d_norm * unit, axis=0, keepdims=True)
        small[4:5, :] += jnp.sum(d_norm, axis=0, keepdims=True)
        d_unit = d_norm * vec[3:4, :]
        d_mid = masked(at) + scale * (
            d_unit - jnp.mean(d_unit, axis=-1, keepdims=True) - unit * jnp.mean(d_unit * unit, axis=-1, keepdims=True)
        )
        dmid[at, :] = d_mid
        small[2:3, :] += jnp.sum(d_mid * datt[at, :].astype(F32), axis=0, keepdims=True)
        d_proj = (d_mid * vec[2:3, :]).astype(BF)
        dproj[at, :] = d_proj
        d_att = mm(d_proj, wout[...], NT).astype(BF)
        datt[at, :] = d_att
        prod = att[at, :].astype(F32) * d_att.astype(F32)
        hi = prod.astype(BF)
        low = (prod - hi.astype(F32)).astype(BF)
        dext[at, :] = pieces(-(mm(hi, pick) + mm(low, pick)), lanes(256)).astype(BF)
        for copy in outs(b):
            copy.start()

    def put(slot, value):
        for i in range(4):
            for r in range(4):
                for c in range(2):
                    rows = slice(192 * i + 48 * r, 192 * i + 48 * r + 48)
                    stage[slot, i, c, r // 2, r % 2] = value[rows, 384 * c : 384 * c + 384].astype(BF)

    def sends(chunk, slot):
        return [
            pltpu.make_async_copy(stage.at[slot, i], part_h.at[chunk, i % 2, i // 2], part_sem.at[slot, i])
            for i in range(4)
        ]

    @pl.loop(0, cols)
    def _(j):
        for r in range(cols):

            @pl.when(j == r)
            def _(r=r):
                red.tick(blocks, r, 0, EARLY_PERIOD, EARLY_LAGS)

        col = pl.ds(pl.multiple_of(j * width, width), width)
        slot = j % 2

        @pl.when(j > 1)
        def _():
            for copy in sends(j - 2, slot):
                copy.wait()

        put(slot, mm(n2t[...], dup[:, col]))
        for copy in sends(j, slot):
            copy.start()

    for copy in sends(cols - 2, 0):
        copy.wait()
    put(0, mm(att_t[...], dproj[...]))
    for copy in sends(cols, 0):
        copy.start()

    for t in range(EARLY_PERIOD * (blocks + 1), last_tick(0, EARLY_PERIOD, len(EARLY), EARLY_LAGS)):
        red.tick(t // EARLY_PERIOD, t % EARLY_PERIOD, 0, EARLY_PERIOD, EARLY_LAGS)

    for copy in sends(cols - 1, 1) + sends(cols, 0):
        copy.wait()

    @pl.loop(0, blocks)
    def _(b):
        layer_out(b).wait()
        for copy in outs(b):
            copy.wait()

    spare.wait()
    red.finish()


def middle_call(ndp, tok, cot, att, ext, vec, wout, wup, wdown):
    count, width = tok.shape
    ff = wdown.shape[0]
    n = len(EARLY)
    tall = pltpu.VMEM((count, width), BF)
    wide = pltpu.VMEM((width, count), BF)
    return pl.pallas_call(
        functools.partial(middle_kernel, ndp),
        out_shape=[
            jax.ShapeDtypeStruct((count, width), BF),
            jax.ShapeDtypeStruct((count, width), F32),
            jax.ShapeDtypeStruct((count, width), BF),
            jax.ShapeDtypeStruct((count, 128), BF),
            jax.ShapeDtypeStruct((6, 2, 2, 2, 2, 2, 48, 384), BF),
            jax.ShapeDtypeStruct((n, 2, 2, 48, 384), BF),
            jax.ShapeDtypeStruct((24, width), F32),
        ],
        in_specs=[ANY] * 4 + [VMEM] + [ANY] * 3,
        out_specs=[ANY] * 6 + [VMEM],
        scratch_shapes=[
            tall,
            tall,
            tall,
            pltpu.VMEM((count, 128), BF),
            pltpu.VMEM(wout.shape, BF),
            pltpu.VMEM(wup.shape, BF),
            pltpu.VMEM(wdown.shape, BF),
            pltpu.VMEM((count, ff), BF),
            pltpu.VMEM((count, ff), BF),
            wide,
            wide,
            wide,
            tall,
            tall,
            tall,
            pltpu.VMEM((count, width), F32),
            tall,
            pltpu.VMEM((count, 128), BF),
            pltpu.VMEM((2, 4, 2, 2, 2, 48, 384), BF),
            pltpu.VMEM((4, 2, 2, 2, 2, 2, 48, 384), BF),
            pltpu.VMEM((n, 2, 2, 2, 2, 48, 384), BF),
            pltpu.VMEM((n, 2, 2, 2, 2, 48, 384), BF),
            pltpu.VMEM((n, 2, 2, 2, 48, 384), BF),
            pltpu.VMEM((n, 2, 2, 48, 384), BF),
            pltpu.SemaphoreType.DMA((7,)),
            pltpu.SemaphoreType.DMA((3, count // 256)),
            pltpu.SemaphoreType.DMA((count // 256,)),
            pltpu.SemaphoreType.DMA((2, 4)),
            pltpu.SemaphoreType.DMA,
            pltpu.SemaphoreType.DMA((n,)),
            pltpu.SemaphoreType.DMA((EARLY_STOP, n)),
            pltpu.SemaphoreType.DMA((EARLY_STOP, n)),
            pltpu.SemaphoreType.DMA((n,)),
        ],
        compiler_params=pltpu.CompilerParams(vmem_limit_bytes=LIMIT, collective_id=2, has_side_effects=True),
        name="middle",
    )(tok, cot, att, ext, vec, wout, wup, wdown)


ORDER = [("g", 5), ("g", 0), ("g", 1), ("g", 2), ("q", 0), ("g", 3), ("g", 4)]
LAGS = {1: 1, 2: 5, 3: 4, 8: 4}
LATE_START = 1
HALF = [("h", 0), ("h", 1), ("h", 2), ("h", 3)]
HALF_START = 12


def backward_kernel(
    ndp,
    page,
    row,
    col,
    vec,
    small_in,
    qkv_h,
    ext_h,
    hot_h,
    page_k_h,
    bias,
    dext_h,
    datt_h,
    normt_h,
    wq_h,
    tok_h,
    dmid_h,
    parts_h,
    early_h,
    gtok_h,
    total_h,
    late_h,
    last_h,
    small_out,
    qkv,
    ext,
    hot,
    page_k,
    dext,
    datt,
    normt,
    wq,
    tok,
    dmid,
    gtok,
    dqkv,
    qa,
    ka,
    va,
    doa,
    kt,
    dqt,
    hot_t,
    square,
    dtab,
    own,
    own_half,
    acc,
    b0,
    b1,
    b2,
    b3,
    b4,
    late_acc,
    late_final,
    late_3,
    late_4,
    half_acc,
    half_final,
    half_0,
    half_1,
    half_2,
    half_3,
    more,
    late_more,
    half_more,
    small_acc,
    small_recv,
    in_sem,
    gt_sem,
    load_sem,
    send_sem,
    recv_sem,
    out_sem,
    late_load,
    late_send,
    late_recv,
    late_out,
    half_load,
    half_send,
    half_recv,
    half_out,
    small_send,
    small_got,
):
    count, width = tok.shape
    pairs = bias.shape[0]
    blocks = count // 256
    loads = []
    for i, (src, dst) in enumerate(
        [
            (qkv_h, qkv),
            (ext_h, ext),
            (hot_h, hot),
            (page_k_h, page_k),
            (dext_h, dext),
            (datt_h, datt),
            (normt_h, normt),
            (wq_h, wq),
            (tok_h, tok),
            (dmid_h, dmid),
        ]
    ):
        copy = pltpu.make_async_copy(src, dst, in_sem.at[i])
        copy.start()
        loads.append(copy)
    links = Links(ndp)
    links.greet(links.everyone())
    red = Reduction(
        links,
        3,
        ORDER,
        {"g": parts_h, "q": own},
        0,
        None,
        acc,
        [b0, b1, b2, b3, b4] + [more.at[k] for k in range(links.bits - 3)],
        b1,
        total_h,
        load_sem,
        send_sem,
        recv_sem,
        out_sem,
    )
    late = Reduction(
        links,
        3,
        EARLY,
        {"d": early_h},
        EARLY_STOP,
        None,
        late_acc,
        [None, None, None, late_3, late_4] + [late_more.at[k] for k in range(links.bits - 3)],
        late_final,
        late_h,
        late_load,
        late_send,
        late_recv,
        late_out,
    )
    half = Reduction(
        links,
        2,
        HALF,
        {"h": own_half},
        0,
        None,
        half_acc,
        [half_0, half_1, half_2, half_3] + [half_more.at[k] for k in range(links.bits - 2)],
        half_final,
        last_h,
        half_load,
        half_send,
        half_recv,
        half_out,
    )
    lags = lag_table(0, red.stages, 0, 3, LAGS)
    late_lags = lag_table(EARLY_STOP, late.stages, 0, 3, {EARLY_STOP: 1})
    half_lags = lag_table(0, half.stages, 0, 3, {1: 1, 2: 6})

    def tick(turn, r):
        red.tick(2 * turn + r // 2, r % 2, 0, 2, lags)
        late.tick(2 * turn + r // 2, r % 2, LATE_START, 2, late_lags)
        half.tick(turn, r, HALF_START, 4, half_lags)

    def tick_at(turn, place):
        for r in range(4):

            @pl.when(place == r)
            def _(r=r):
                tick(turn, r)

    for r in range(page.shape[0]):
        want = 31 - lax.broadcasted_iota(jnp.int32, (32, 128), 0)
        for axis in range(2):
            have = jnp.broadcast_to((col if axis else row)[r : r + 1, :], (32, 128))
            hot_t[32 * axis : 32 * axis + 32, r * 128 : r * 128 + 128] = jnp.where(have == want, 1.0, 0.0).astype(BF)
    small_acc[0] = small_in[...]
    low_half = lanes(count) < 64
    third = lanes(count) // 3
    for copy in loads[:6]:
        copy.wait()

    @pl.loop(0, pairs)
    def _(p):
        g, s = p // 2, p % 2
        queries, keys, values = qkv[p], qkv[pairs + p], qkv[2 * pairs + p]
        side = mm(hot[:, :64], bias[p]).astype(BF)
        zero = jnp.zeros_like(values)
        places = hot[...]
        qa[0, :, :128] = jnp.where(low_half, queries, places)
        qa[1, :, :128] = jnp.where(low_half, places, queries)
        ka[0, :, :128] = jnp.where(low_half, keys, side)
        ka[1, :, :128] = jnp.where(low_half, side, keys)
        va[0, :, :128] = jnp.where(low_half, values, zero)
        va[1, :, :128] = jnp.where(low_half, zero, values)
        for e in range(2):
            head = 2 * p + e
            qa[e, :, 128:] = ext[...]
            ka[e, :, 128:] = jnp.where(third == 2 + head, -1.0, page_k[...].astype(F32)).astype(BF)
            va[e, :, 128:] = jnp.where(third == head, 1.0, 0.0).astype(BF)
        doa[:, :128] = datt[:, pl.ds(pl.multiple_of(p * 128, 128), 128)]
        doa[:, 128:] = dext[...]
        kt[...] = keys.T
        dqt[...] = jnp.zeros_like(dqt)
        square[...] = jnp.zeros_like(square)

        @pl.loop(0, blocks)
        def _(b):
            tick_at(p, b)
            at = pl.ds(pl.multiple_of(b * 256, 256), 256)
            dks, dvs = [], []
            for e in range(2):
                prob = jnp.exp(mm(ka[e, at, :], qa[e], NT))
                d_prob = mm(va[e, at, :], doa[...], NT)
                d_scores = (prob * d_prob).astype(BF)
                dvs.append(mm(prob.astype(BF), doa[:, :128]))
                dks.append(mm(d_scores, qa[e, :, :128]))
                dqt[64 * e : 64 * e + 64, :] += mm(kt[64 * e : 64 * e + 64, at], d_scores)
            half = lanes(256) < 64
            dqkv[g, at, pl.ds(pl.multiple_of(s * 384 + 128, 128), 128)] = jnp.where(half, dks[0], dks[1]).astype(BF)
            dqkv[g, at, pl.ds(pl.multiple_of(s * 384 + 256, 128), 128)] = jnp.where(half, dvs[0], dvs[1]).astype(BF)
            part = jnp.where(half, dks[1], dks[0])
            hi = part.astype(BF)
            low = (part - hi.astype(F32)).astype(BF)
            both = mm(hot_t[:, at], jnp.concatenate([hi, low], axis=1))
            square[...] += both[:, :128] + both[:, 128:]

        dqkv[g, :, pl.ds(pl.multiple_of(s * 384, 128), 128)] = (dqt[...].T * 0.125).astype(BF)
        near = lanes(32) & 63
        for axis in range(2):
            part = square[32 * axis : 32 * axis + 32, :]
            part = jnp.where((near >= 32) if axis else (near < 32), part, 0.0)
            rolled = pltpu.roll(part, 96 * axis, axis=1, stride=1, stride_axis=0)
            dtab[p, axis : axis + 1, :] = jnp.sum(rolled, axis=0, keepdims=True)

        @pl.when(p == 0)
        def _():
            for copy in loads[6:]:
                copy.wait()

        value = mm(normt[...], dqkv[g, :, pl.ds(pl.multiple_of(s * 384, 128), 384)]).astype(BF)

        @pl.when(p < 2 * own.shape[0])
        def _():
            for f in range(4):
                for r in range(4):
                    own[g, f % 2, f // 2, s, r // 2, r % 2] = value[192 * f + 48 * r : 192 * f + 48 * r + 48, :]

        @pl.when(p >= 2 * own.shape[0])
        def _():
            for f in range(4):
                for r in range(4):
                    at = (p - 2 * own.shape[0], f % 2, f // 2, r // 2, r % 2)
                    own_half[at] = value[192 * f + 48 * r : 192 * f + 48 * r + 48, :]

    for p in range(pairs):
        small_acc[0, 12 + 2 * p : 14 + 2 * p, 0:128] = dtab[p]

    def gtok_out(b):
        at = pl.ds(pl.multiple_of(b * 256, 256), 256)
        return pltpu.make_async_copy(gtok.at[at, :], gtok_h.at[at, :], gt_sem.at[b])

    first_tick = pairs * blocks

    @pl.loop(0, blocks)
    def _(b):
        tick_at(pairs, b)
        at = pl.ds(pl.multiple_of(b * 256, 256), 256)
        d_norm = mm(dqkv[0, at, :], wq[0], NT)
        for g in range(1, pairs // 2):
            d_norm += mm(dqkv[g, at, :], wq[g], NT)
        rows = tok[at, :].astype(F32)
        center = rows - jnp.mean(rows, axis=-1, keepdims=True)
        scale = lax.rsqrt(jnp.mean(center * center, axis=-1, keepdims=True) + 1e-06)
        unit = center * scale
        small_acc[0, 0:1, :] += jnp.sum(d_norm * unit, axis=0, keepdims=True)
        small_acc[0, 1:2, :] += jnp.sum(d_norm, axis=0, keepdims=True)
        d_unit = d_norm * vec[0:1, :]
        back = scale * (
            d_unit - jnp.mean(d_unit, axis=-1, keepdims=True) - unit * jnp.mean(d_unit * unit, axis=-1, keepdims=True)
        )
        gtok[at, :] = (dmid[at, :] + back).astype(BF)
        gtok_out(b).start()

    others = links.everyone()

    def small_copy(i):
        return remote(small_acc.at[i], small_recv.at[i], small_send.at[i], small_got.at[i], others[i])

    small_copy(0).start()
    at_tick = first_tick + blocks
    for i in range(len(others)):
        tick((at_tick + i) // 4, (at_tick + i) % 4)
        small_copy(i).wait_recv()
        small_acc[i + 1] = small_acc[i] + small_recv[i]
        if i + 1 < len(others):
            small_copy(i + 1).start()
    small_out[...] = small_acc[len(others)]
    at_tick = at_tick + len(others)
    while at_tick % 4:
        tick(at_tick // 4, at_tick % 4)
        at_tick += 1
    last = max(
        last_tick(0, 2, len(ORDER), lags),
        last_tick(LATE_START, 2, len(EARLY), late_lags),
        last_tick(HALF_START, 4, len(HALF), half_lags),
    )

    @pl.loop(at_tick // 4, -(-last // 4))
    def _(turn):
        for r in range(4):
            tick(turn, r)

    red.finish()
    late.finish()
    half.finish()
    for i in range(len(others)):
        small_copy(i).wait_send()
    for b in range(blocks):
        gtok_out(b).wait()


def backward_call(ndp, places, vec, small, qkv, ext, hot, page_k, bias, dext, datt, normt, wq, tok, dmid, parts, half):
    count, width = datt.shape
    bits = ndp.bit_length() - 1
    n, m, q = len(ORDER), len(EARLY), len(HALF)
    last_extra = max(0, bits - 2)
    extra = max(0, bits - 3)
    stages = 2 + 2 * min(3, bits) + extra
    tall = pltpu.VMEM((count, width), BF)
    side = pltpu.VMEM((count, 128), BF)
    pair = pltpu.VMEM((2, count, 256), BF)
    return pl.pallas_call(
        functools.partial(backward_kernel, ndp),
        out_shape=[
            jax.ShapeDtypeStruct((count, width), BF),
            jax.ShapeDtypeStruct((n, 2, 2, 2, 48, 384), BF),
            jax.ShapeDtypeStruct((m, 2, 2, 2, 48, 384), BF),
            jax.ShapeDtypeStruct((q, 2, 2, 48, 384), BF),
            jax.ShapeDtypeStruct(small.shape, F32),
        ],
        in_specs=[VMEM] * 5 + [ANY] * 4 + [VMEM] + [ANY] * 8,
        out_specs=[ANY] * 4 + [VMEM],
        scratch_shapes=[
            pltpu.VMEM(qkv.shape, BF),
            side,
            side,
            side,
            side,
            tall,
            pltpu.VMEM((width, count), BF),
            pltpu.VMEM(wq.shape, BF),
            tall,
            pltpu.VMEM((count, width), F32),
            tall,
            pltpu.VMEM((3, count, width), BF),
            pair,
            pair,
            pair,
            pltpu.VMEM((count, 256), BF),
            pltpu.VMEM((128, count), BF),
            pltpu.VMEM((128, count), F32),
            pltpu.VMEM((64, count), BF),
            pltpu.VMEM((64, 128), F32),
            pltpu.VMEM((width // 128, 2, 128), F32),
            pltpu.VMEM((1, 2, 2, 2, 2, 2, 48, 384), BF),
            pltpu.VMEM((q, 2, 2, 2, 2, 48, 384), BF),
            pltpu.VMEM((n, 2, 2, 2, 2, 48, 384), BF),
            pltpu.VMEM((n, 2, 2, 2, 2, 48, 384), BF),
            pltpu.VMEM((n, 2, 2, 2, 48, 384), BF),
            pltpu.VMEM((n, 2, 2, 48, 384), BF),
            pltpu.VMEM((n, 2, 48, 384), BF),
            pltpu.VMEM((n, 48, 384), BF),
            pltpu.VMEM((m, 2, 2, 48, 384), BF),
            pltpu.VMEM((m, 2, 2, 2, 48, 384), BF),
            pltpu.VMEM((m, 2, 48, 384), BF),
            pltpu.VMEM((m, 48, 384), BF),
            pltpu.VMEM((q, 2, 2, 2, 48, 384), BF),
            pltpu.VMEM((q, 2, 2, 48, 384), BF),
            pltpu.VMEM((q, 2, 2, 2, 48, 384), BF),
            pltpu.VMEM((q, 2, 2, 48, 384), BF),
            pltpu.VMEM((q, 2, 48, 384), BF),
            pltpu.VMEM((q, 48, 384), BF),
            pltpu.VMEM((extra, n, 48, 384) if extra else (1, 1, 16, 128), BF),
            pltpu.VMEM((extra, m, 48, 384) if extra else (1, 1, 16, 128), BF),
            pltpu.VMEM((last_extra, q, 48, 384) if last_extra else (1, 1, 16, 128), BF),
            pltpu.VMEM((bits + 3,) + small.shape, F32),
            pltpu.VMEM((bits + 2,) + small.shape, F32),
            pltpu.SemaphoreType.DMA((10,)),
            pltpu.SemaphoreType.DMA((count // 256,)),
            pltpu.SemaphoreType.DMA((n,)),
            pltpu.SemaphoreType.DMA((stages, n)),
            pltpu.SemaphoreType.DMA((stages, n)),
            pltpu.SemaphoreType.DMA((n,)),
            pltpu.SemaphoreType.DMA((m,)),
            pltpu.SemaphoreType.DMA((stages, m)),
            pltpu.SemaphoreType.DMA((stages, m)),
            pltpu.SemaphoreType.DMA((m,)),
            pltpu.SemaphoreType.DMA((q,)),
            pltpu.SemaphoreType.DMA((stages, q)),
            pltpu.SemaphoreType.DMA((stages, q)),
            pltpu.SemaphoreType.DMA((q,)),
            pltpu.SemaphoreType.DMA((bits + 2,)),
            pltpu.SemaphoreType.DMA((bits + 2,)),
        ],
        compiler_params=pltpu.CompilerParams(vmem_limit_bytes=LIMIT, collective_id=1, has_side_effects=True),
        name="backward",
    )(*places, vec, small, qkv, ext, hot, page_k, bias, dext, datt, normt, wq, tok, dmid, parts, half)


def finish_kernel(
    total_h,
    late_h,
    last_h,
    layer_i,
    gtok_i,
    small,
    layer_h,
    gtok_h,
    wqkv_h,
    rel,
    wout_h,
    wup_h,
    bup,
    wdown_h,
    v0,
    v1,
    v2,
    v3,
    v4,
    v5,
    v6,
    total,
    late,
    last,
    wqkv,
    wout,
    wup,
    wdown,
    layer,
    gtok,
    in_sem,
    out_sem,
):
    f = lax.axis_index("fsdp")
    own = v0.shape[0]
    n, m = total.shape[0], late.shape[0]
    loads = [pltpu.make_async_copy(late_h.at[i], late.at[i], in_sem.at[i]) for i in range(m)]
    loads += [pltpu.make_async_copy(total_h.at[i], total.at[i], in_sem.at[m + i]) for i in range(n)]
    loads.append(pltpu.make_async_copy(last_h, last, in_sem.at[m + n]))
    through = [(layer_i, layer, layer_h), (gtok_i, gtok, gtok_h)]
    loads += [pltpu.make_async_copy(src, mid, in_sem.at[m + n + 1 + i]) for i, (src, mid, _) in enumerate(through)]
    for copy in loads:
        copy.start()
    pending = []

    def leave(src, dst):
        copy = pltpu.make_async_copy(src, dst, out_sem.at[len(pending)])
        copy.start()
        pending.append(copy)

    spare = [kind for kind, _ in ORDER].index("g")
    for h in range(2):
        loads[2 * h].wait()
        loads[2 * h + 1 if h == 0 else m + spare].wait()
        sides = []
        for c in range(2):
            both = [late.at[2 * h], late.at[2 * h + 1] if h == 0 else total.at[spare]]
            rows = [one[c, r // 2, r % 2].astype(F32) for one in both for r in range(4)]
            sides.append(jnp.concatenate(rows, axis=0).T)
        for c in range(2):
            wdown[384 * c : 384 * c + 384, 384 * h : 384 * h + 384] = sides[c]
    leave(wdown, wdown_h)
    for i, (_, mid, dst) in enumerate(through):
        loads[m + n + 1 + i].wait()
        leave(mid, dst)
    for i, (kind, j) in enumerate(ORDER):
        if i == spare:
            continue
        loads[m + i].wait()
        for c in range(2):
            for r in range(4):
                at = slice(48 * r, 48 * r + 48)
                value = total[i, c, r // 2, r % 2].astype(F32)
                if kind == "g" and j < 4:
                    wup[at, 768 * j + 384 * c : 768 * j + 384 * c + 384] = value
                elif kind == "g":
                    wout[at, 384 * c : 384 * c + 384] = value
                else:
                    for part in range(3):
                        start = 768 * part + 256 * j + 128 * c
                        wqkv[at, start : start + 128] = value[:, 128 * part : 128 * part + 128]
    leave(wup, wup_h)
    leave(wout, wout_h)
    loads[m + n].wait()
    for i in range(last.shape[0]):
        for r in range(4):
            value = last[i, r // 2, r % 2].astype(F32)
            for part in range(3):
                start = 768 * part + 128 * (2 + i)
                wqkv[48 * r : 48 * r + 48, start : start + 128] = value[:, 128 * part : 128 * part + 128]
    leave(wqkv, wqkv_h)

    def mine(rows, width, stride):
        out = jnp.zeros((rows.stop - rows.start, width), F32)
        for k in range(4):
            out = jnp.where(f == k, small[rows, stride * k : stride * k + width], out)
        return out

    vectors = mine(slice(0, 8), own, own)
    for i, ref in enumerate((v0, v1, v2, v3, v4, v5, v6)):
        ref[...] = vectors[i : i + 1, :].reshape(own)
    line = jnp.zeros((1, bup.shape[0]), F32)
    for k in range(4):
        line = jnp.where(f == k, small[8 + k : 9 + k, :], line)
    bup[...] = line.reshape(bup.shape[0])
    offsets = rel.shape[2]
    for i in range(rel.shape[0]):
        for axis in range(2):
            value = jnp.zeros((1, offsets), F32)
            for k in range(4):
                head = rel.shape[0] * k + i
                start = 64 * (1 - head % 2)
                at = 12 + 2 * (head // 2) + axis
                value = jnp.where(f == k, small[at : at + 1, start : start + offsets], value)
            rel[i, axis : axis + 1, :] = value
    for copy in pending:
        copy.wait()


def finish_call(total, late, last, layer, gtok, small, own, rel):
    width = small.shape[1]
    vec = jax.ShapeDtypeStruct((own,), F32)
    shapes = [(own, 3 * width), (own, width), (own, 4 * width), (4 * own, width)]
    wqkv, wout, wup, wdown = [jax.ShapeDtypeStruct(s, F32) for s in shapes]
    return pl.pallas_call(
        finish_kernel,
        out_shape=[jax.ShapeDtypeStruct(layer.shape, BF), jax.ShapeDtypeStruct(gtok.shape, BF)]
        + [wqkv, jax.ShapeDtypeStruct(rel.shape, F32), wout, wup, jax.ShapeDtypeStruct((4 * own,), F32), wdown]
        + [vec] * 7,
        in_specs=[ANY] * 5 + [VMEM],
        out_specs=[ANY, ANY, ANY, VMEM, ANY, ANY, VMEM, ANY] + [VMEM] * 7,
        scratch_shapes=[pltpu.VMEM(x.shape, BF) for x in (total, late, last)]
        + [pltpu.VMEM(s, F32) for s in shapes]
        + [pltpu.VMEM(layer.shape, BF), pltpu.VMEM(gtok.shape, BF)]
        + [pltpu.SemaphoreType.DMA((total.shape[0] + late.shape[0] + 3,)), pltpu.SemaphoreType.DMA((6,))],
        compiler_params=pltpu.CompilerParams(vmem_limit_bytes=LIMIT),
        name="finish",
    )(total, late, last, layer, gtok, small)


def local(
    tokens,
    cotangent,
    page_id,
    pos_row,
    pos_col,
    ln1_gain,
    ln1_shift,
    w_qkv,
    rel_table,
    w_out,
    scale_attn,
    ln2_gain,
    ln2_shift,
    w_up,
    b_up,
    w_down,
    b_down,
    scale_mlp,
):
    ndp = lax.axis_size("dp")
    count, width = tokens.shape
    places = [x.reshape(count // 128, 128) for x in (page_id, pos_row, pos_col)]
    vectors = [ln1_gain, ln1_shift, scale_attn, ln2_gain, ln2_shift, b_down, scale_mlp]
    normt, qkv, att, ext, hot, page_k, bias, vec, wq, wout, wup, wdown = forward_call(
        ndp, places, vectors, b_up, rel_table, tokens, w_qkv, w_out, w_up, w_down
    )
    wq = wq.reshape(-1, width, width)
    wout = wout.reshape(width, width)
    wup = wup.reshape(-1, width, width)
    wdown = wdown.reshape(-1, width)
    layer_out, d_mid, d_att, d_ext, parts, early, small = middle_call(ndp, tokens, cotangent, att, ext, vec, wout, wup, wdown)
    grad_tokens, total, late, last, small = backward_call(
        ndp, places, vec, small, qkv, ext, hot, page_k, bias, d_ext, d_att, normt, wq, tokens, d_mid, parts, early
    )
    layer_out, grad_tokens, g_wqkv, g_rel, g_wout, g_wup, g_bup, g_wdown, *g = finish_call(
        total, late, last, layer_out, grad_tokens, small, ln1_gain.shape[0], rel_table
    )
    return (
        layer_out,
        grad_tokens,
        g[0],
        g[1],
        g_wqkv,
        g_rel,
        g_wout,
        g[2],
        g[3],
        g[4],
        g_wup,
        g_bup,
        g_wdown,
        g[5],
        g[6],
    )


def solution(mesh):
    rows = P(("dp", "fsdp"))
    slab = P(("dp", "fsdp"), None)
    vec = P("fsdp")
    mat = P("fsdp", None)
    cube = P("fsdp", None, None)
    in_specs = (slab, slab, rows, rows, rows, vec, vec, mat, cube, mat, vec, vec, vec, mat, vec, mat, vec, vec)
    out_specs = (slab, slab, vec, vec, mat, cube, mat, vec, vec, vec, mat, vec, mat, vec, vec)
    return jax.shard_map(local, mesh=mesh, in_specs=in_specs, out_specs=out_specs, check_vma=False)
```

```python
import functools

import jax
import jax.numpy as jnp
from jax import lax
from jax.experimental import pallas as pl
from jax.experimental.pallas import tpu as pltpu
from jax.sharding import PartitionSpec as P

F32 = jnp.float32
BF = jnp.bfloat16
NT = (((1,), (1,)), ((), ()))
NN = (((1,), (0,)), ((), ()))
VMEM = pl.BlockSpec(memory_space=pltpu.VMEM)
ANY = pl.BlockSpec(memory_space=pl.ANY)
MESH = pl.DeviceIdType.MESH
LIMIT = 63 << 20
MASKED = -1e30


def mm(a, b, dims=NN):
    return lax.dot_general(a, b, dims, preferred_element_type=F32)


def lanes(rows, width=128):
    return lax.broadcasted_iota(jnp.int32, (rows, width), 1)


def normalize(rows, gain, shift):
    center = rows - jnp.mean(rows, axis=-1, keepdims=True)
    spread = jnp.mean(center * center, axis=-1, keepdims=True)
    return center * lax.rsqrt(spread + 1e-06) * gain + shift


def pieces(x, lane):
    hi = x.astype(BF)
    rest = x - hi.astype(F32)
    mid = rest.astype(BF)
    low = (rest - mid.astype(F32)).astype(BF)
    third = lane % 3
    return jnp.where(third == 0, hi.astype(F32), jnp.where(third == 1, mid.astype(F32), low.astype(F32)))


def position_columns(pages, rows, cols, hot, page_q, page_k):
    for r in range(pages.shape[0]):
        code = (pages[r : r + 1, :] + 1) * 4096 + rows[r : r + 1, :] * 64 + cols[r : r + 1, :]
        code = jnp.broadcast_to(code.astype(F32), (128, 128)).T.astype(jnp.int32)
        lane = lanes(128)
        page, row, col = code >> 12, (code >> 6) & 63, code & 63
        near = lane & 63
        where = jnp.where(near < 32, row, col + 32)
        at = pl.ds(r * 128, 128)
        hot[at, :] = jnp.where(where == near, 1.0, 0.0).astype(BF)
        page_q[at, :] = jnp.where(page == lane, 1.0, 0.0)
        page_k[at, :] = jnp.where((lane < 6) & (page != lane), MASKED, 0.0).astype(BF)


def toeplitz(table, bias):
    lane = lanes(32)
    for p in range(bias.shape[0]):
        for axis in range(2):
            parts = []
            for head, at in ((2 * p + 1, 32 * axis), (2 * p, 64 + 32 * axis)):
                row = jnp.broadcast_to(table[2 * head + axis : 2 * head + axis + 1, :], (32, 128))
                rolled = pltpu.roll(row, (97 + at) % 128, axis=1, stride=1, stride_axis=0)
                parts.append(jnp.where((lane >= at) & (lane < at + 32), rolled, 0.0))
            bias[p, 32 * axis : 32 * axis + 32, :] = (parts[0] + parts[1]).astype(BF)


class Links:
    def __init__(self, ndp):
        self.dp, self.f = lax.axis_index("dp"), lax.axis_index("fsdp")
        self.core, self.x = self.f % 2, self.f // 2
        self.bits = ndp.bit_length() - 1
        self.bit = [(self.dp // 2**k) % 2 for k in range(self.bits)]

    def partner(self, kind, k=0):
        if kind == "core":
            return (self.dp, self.f + 1 - 2 * self.core)
        if kind == "x":
            return (self.dp, self.f + 2 - 4 * self.x)
        return (self.dp + (1 - 2 * self.bit[k]) * 2**k, self.f)

    def everyone(self):
        return [self.partner("core"), self.partner("x")] + [self.partner("dp", k) for k in range(self.bits)]

    def greet(self, others):
        barrier = pltpu.get_barrier_semaphore()
        for other in others:
            pl.semaphore_signal(barrier, inc=1, device_id=other, device_id_type=MESH)
        pl.semaphore_wait(barrier, len(others))


def remote(src, dst, send, recv, device):
    return pltpu.make_async_remote_copy(
        src_ref=src, dst_ref=dst, send_sem=send, recv_sem=recv, device_id=device, device_id_type=MESH
    )


def pick_index(n, table):
    out = 0
    for i, v in enumerate(table):
        if v:
            out = out + jnp.where(n == i, v, 0)
    return out


class Reduction:
    def __init__(self, links, halvings, order, homes, first, last, acc, recv, final, out_h, load_sem, send_sem, recv_sem, out_sem):
        self.l, self.order, self.homes, self.first = links, order, homes, first
        self.acc, self.recv, self.final, self.out_h = acc, recv, final, out_h
        self.load_sem, self.send_sem, self.recv_sem, self.out_sem = load_sem, send_sem, recv_sem, out_sem
        self.depth = max(0, first - 1)
        self.halvings = halvings
        self.halved = 1 + halvings
        self.extra = links.bits - halvings
        self.stages = 2 + 2 * halvings + self.extra
        self.last = self.stages if last is None else last
        self.kept = (links.x,) + tuple(links.bit[:halvings])

    def sems(self, k, n):
        return self.send_sem.at[k, n], self.recv_sem.at[k, n]

    def partner(self, k):
        l = self.l
        if k == 0:
            return l.partner("core")
        if k == 1:
            return l.partner("x")
        j = k - 2 if k <= self.halved + self.extra else self.halvings - 1 - (k - 1 - self.halved - self.extra)
        return l.partner("dp", j)

    def copy(self, k, n):
        l = self.l
        if k <= self.halved:
            at = (n,) + self.kept[self.depth : k - 1] + (1 - self.kept[k - 1],)
            return remote(self.acc.at[at], self.recv[k].at[n], *self.sems(k, n), self.partner(k))
        if k <= self.halved + self.extra:
            return remote(self.final.at[(n,) + self.kept[1:]], self.recv[k].at[n], *self.sems(k, n), self.partner(k))
        j = self.halvings - 1 - (k - 1 - self.halved - self.extra)
        at = (n,) + self.kept[1 : 2 + j]
        return remote(self.final.at[at], self.final.at[at], *self.sems(k, n), self.partner(k))

    def opening(self, n, act):
        l = self.l
        for kind in sorted(self.homes):
            places = [i for i, (name, _) in enumerate(self.order) if name == kind]
            mine = pick_index(n, [i for _, i in self.order])
            home = self.homes[kind]

            @pl.when(sum(jnp.where(n == i, 1, 0) for i in places) > 0)
            def _(home=home):
                if self.first == 0:
                    act(
                        lambda: remote(
                            home.at[mine, 1 - l.core], self.recv[0].at[n], *self.sems(0, n), self.partner(0)
                        ),
                        lambda: pltpu.make_async_copy(home.at[mine, l.core], self.acc.at[n], self.load_sem.at[n]),
                    )
                else:
                    act(None, lambda: pltpu.make_async_copy(home.at[mine], self.acc.at[n], self.load_sem.at[n]))

    def out(self, n):
        if self.last == self.stages:
            return pltpu.make_async_copy(self.final.at[n], self.out_h.at[n], self.out_sem.at[n])
        src = self.acc.at[(n,) + self.kept[self.depth : self.last - 1]]
        return pltpu.make_async_copy(src, self.out_h.at[n], self.out_sem.at[n])

    def launch(self, n):
        def start(send, load):
            if send is not None:
                send().start()
            load().start()

        self.opening(n, start)

    def step(self, k, n):
        l = self.l

        def arrive(send, load):
            if send is not None:
                send().wait_recv()
            load().wait()

        if k == max(self.first, 1):
            self.opening(n, arrive)
            if self.first == 0:
                self.acc[n] = self.acc[n] + self.recv[0][n]
        elif k <= self.halved:
            self.copy(k - 1, n).wait_recv()
            at = (n,) + self.kept[self.depth : k - 1]
            self.acc[at] = self.acc[at] + self.recv[k - 1][n]
        elif k == self.halved + 1:
            self.copy(k - 1, n).wait_recv()
            at = (n,) + self.kept[self.depth :]
            self.final[(n,) + self.kept[1:]] = self.acc[at] + self.recv[k - 1][n]
        elif k <= self.halved + self.extra + 1:
            self.copy(k - 1, n).wait()
            at = (n,) + self.kept[1:]
            self.final[at] = self.final[at] + self.recv[k - 1][n]
        else:
            self.copy(k - 1, n).wait_recv()
        if k < self.last:
            self.copy(k, n).start()
        else:
            self.out(n).start()

    def tick(self, turn, r, start, period, lags):
        for k, lag in sorted(lags.items(), reverse=True):
            if (start + lag - r) % period:
                continue
            n = turn - (start + lag - r) // period
            if isinstance(n, int):
                if 0 <= n < len(self.order):
                    self.launch(n) if k == -1 else self.step(k, n)
                continue

            @pl.when((n >= 0) & (n < len(self.order)))
            def _(k=k, n=n):
                if k == -1:
                    self.launch(n)
                else:
                    self.step(k, n)

    def finish(self):
        l = self.l

        @pl.loop(0, len(self.order))
        def _(n):
            if self.first == 0:
                self.opening(n, lambda send, load: send().wait_send())
            for k in range(max(1, self.first), self.last):
                if not self.halved < k <= self.halved + self.extra:
                    self.copy(k, n).wait_send()
            self.out(n).wait()


def lag_table(first, last, start, step, special):
    table = {-1: start}
    at = start
    for k in range(max(1, first), last + 1):
        at += special.get(k, step)
        table[k] = at
    return table


def last_tick(start, period, count, lags):
    return start + period * (count - 1) + max(lags.values()) + 1


class Weights:
    def __init__(self, links, own, home, send_sem, recv_sem, keep_sem):
        self.l, self.own, self.home = links, own, home
        self.send_sem, self.recv_sem, self.keep_sem = send_sem, recv_sem, keep_sem
        l = links
        self.f = l.f
        self.y = l.bit[0]
        self.sibling = l.f + 1 - 2 * l.core
        self.across = l.f + 2 - 4 * l.x
        self.halves = (pl.ds(pl.multiple_of(self.y * 96, 32), 96), pl.ds(pl.multiple_of((1 - self.y) * 96, 32), 96))

    def branch(self, n, act):
        for (low, high), own, home in zip(((0, 3), (3, 4), (4, 8), (8, 12)), self.own, self.home):

            @pl.when((n >= low) & (n < high))
            def _(low=low, own=own, home=home):
                act(own(n - low), lambda f: home(n - low, f), low > 0)

    def copies(self, n, own, home):
        l, (this, other) = self.l, self.halves
        s = [(self.send_sem.at[k, n], self.recv_sem.at[k, n]) for k in range(5)]
        mine, across = home(self.f), home(self.across)
        sibling = l.partner("core")
        return [
            lambda: remote(own, mine, *s[0], sibling),
            lambda: remote(own.at[this, :], mine.at[this, :], *s[1], l.partner("x")),
            lambda: remote(across.at[this, :], across.at[this, :], *s[2], l.partner("dp", 0)),
            lambda: remote(across.at[this, :], across.at[this, :], *s[3], sibling),
            lambda: remote(across.at[other, :], across.at[other, :], *s[4], sibling),
        ]

    def step(self, k, n):
        def act(own, home, keep):
            copies = self.copies(n, own, home)
            if k == 0:
                copies[1]().start()
                copies[0]().start()
                if keep:
                    pltpu.make_async_copy(own, home(self.f), self.keep_sem.at[n]).start()
            elif k == 1:
                copies[1]().wait_recv()
                copies[2]().start()
                copies[3]().start()
            elif k == 2:
                copies[2]().wait_recv()
                copies[4]().start()
            elif k == 3:
                for i in (0, 3, 4):
                    copies[i]().wait_recv()
            else:
                for copy in copies:
                    copy().wait_send()
                if keep:
                    pltpu.make_async_copy(own, home(self.f), self.keep_sem.at[n]).wait()

        self.branch(n, act)

    def tick(self, t):
        for k, lag in ((3, 7), (2, 4), (1, 0)):
            m = t - lag + 128
            n = m // 2 - 63

            @pl.when((m % 2 == 0) & (n >= 1) & (n < 12))
            def _(k=k, n=n):
                self.step(k, n)
                if k == 1:

                    @pl.when(n + 3 < 12)
                    def _():
                        self.step(0, n + 3)


def pack_own(mine, vectors, bup, table):
    own = vectors[0].shape[0]
    mine[...] = jnp.zeros_like(mine)
    for i, ref in enumerate(vectors):
        mine[i : i + 1, 0:own] = ref[...].astype(F32).reshape(1, own)
    line = bup[...].astype(F32).reshape(1, bup.shape[0])
    for i in range(4):
        mine[7 + i : 8 + i, 0:own] = line[:, own * i : own * i + own]
    for h in range(table.shape[0]):
        for axis in range(2):
            at = 11 + 2 * h + axis
            mine[at : at + 1, 0 : table.shape[2]] = table[h, axis : axis + 1, :].astype(F32)


def unpack(shards, vec, table, own):
    for v in range(7):
        vec[v : v + 1, :] = jnp.concatenate([shards[f, v : v + 1, 0:own] for f in range(4)], axis=1)
    for f in range(4):
        vec[8 + f : 9 + f, :] = jnp.concatenate([shards[f, 7 + i : 8 + i, 0:own] for i in range(4)], axis=1)
        table[6 * f : 6 * f + 6, :] = shards[f, 11:17, 0:128]


def forward_kernel(
    ndp,
    page,
    row,
    col,
    v0,
    v1,
    v2,
    v3,
    v4,
    v5,
    v6,
    bup,
    rel,
    tok_h,
    wqkv_h,
    wout_s,
    wup_s,
    wdown_s,
    normt_h,
    qkv_h,
    att_h,
    ext_h,
    hot_h,
    page_k_h,
    bias,
    vec,
    wq_h,
    wout_h,
    wup_h,
    wdown_h,
    tok,
    norm,
    normt,
    qkv,
    att,
    ext,
    hot,
    page_k,
    lse,
    ka,
    va,
    wq,
    mine,
    shards,
    table,
    tok_sem,
    mine_sem,
    local_sem,
    pack_send,
    pack_got,
    send_sem,
    recv_sem,
    keep_sem,
    out_sem,
    group_sem,
):
    count, width = tok.shape
    pairs = bias.shape[0]
    blocks = count // 256
    links = Links(ndp)
    tok_copy = pltpu.make_async_copy(tok_h, tok, tok_sem)
    tok_copy.start()

    def own_group(g):
        return [
            pltpu.make_async_copy(
                wqkv_h.at[:, width * part + 256 * g + 128 * s : width * part + 256 * g + 128 * s + 128],
                wq.at[g, links.f, :, 384 * s + 128 * part : 384 * s + 128 * part + 128],
                local_sem.at[g, 3 * s + part],
            )
            for s in range(2)
            for part in range(3)
        ]

    for g in range(3):
        for copy in own_group(g):
            copy.start()
    own_loads = [pltpu.make_async_copy(wout_s, mine.at[0], mine_sem.at[0])]
    for j in range(4):
        part = pl.ds(j * width, width)
        own_loads.append(pltpu.make_async_copy(wup_s.at[:, part], mine.at[1 + j], mine_sem.at[1 + j]))
    for j in range(4):
        part = pl.ds(j * 192, 192)
        own_loads.append(pltpu.make_async_copy(wdown_s.at[part, :], mine.at[5 + j], mine_sem.at[5 + j]))
    for copy in own_loads:
        copy.start()
    pack_own(shards.at[links.f], [v0, v1, v2, v3, v4, v5, v6], bup, rel)
    diagonal = (links.dp, 3 - links.f)
    peers = [links.partner("core"), links.partner("x"), diagonal]
    barrier = pltpu.get_barrier_semaphore()
    for other in peers + [links.partner("dp", 0)]:
        pl.semaphore_signal(barrier, inc=1, device_id=other, device_id_type=MESH)
    pl.semaphore_wait(barrier, 4)

    gather = Weights(
        links,
        [
            lambda j: wq.at[j, links.f],
            lambda j: mine.at[j],
            lambda j: mine.at[1 + j],
            lambda j: mine.at[5 + j],
        ],
        [
            lambda j, f: wq.at[j, f],
            lambda j, f: wout_h.at[f],
            lambda j, f: wup_h.at[j, f],
            lambda j, f: wdown_h.at[f, j],
        ],
        send_sem,
        recv_sem,
        keep_sem,
    )

    def pack_copy(i):
        return remote(shards.at[links.f], shards.at[links.f], pack_send.at[i], pack_got.at[i], peers[i])

    for copy in own_group(0):
        copy.wait()
    gather.step(0, 0)
    for i in range(3):
        pack_copy(i).start()
    for g in (1, 2):
        for copy in own_group(g):
            copy.wait()
    for copy in own_loads:
        copy.wait()
    gather.step(0, 1)
    gather.step(0, 2)
    gather.step(0, 3)
    position_columns(page, row, col, hot, lse, page_k)
    for i in range(3):
        pack_copy(i).wait_recv()
    vec[...] = jnp.zeros_like(vec)
    unpack(shards, vec, table, v0.shape[0])
    toeplitz(table, bias)
    tok_copy.wait()

    @pl.loop(0, blocks)
    def _(b):
        at = pl.ds(pl.multiple_of(b * 256, 256), 256)
        rows = normalize(tok[at, :].astype(F32), vec[0:1, :], vec[1:2, :]).astype(BF)
        norm[at, :] = rows
        normt[:, at] = rows.T

    outs = [
        pltpu.make_async_copy(src, dst, out_sem.at[i])
        for i, (src, dst) in enumerate([(normt, normt_h), (hot, hot_h), (page_k, page_k_h), (att, att_h), (ext, ext_h)])
    ]
    for copy in outs[:3]:
        copy.start()
    for k in (1, 2, 3):
        gather.step(k, 0)
    low_half = lanes(count) < 64

    def group_out(g):
        copies = [pltpu.make_async_copy(wq.at[g], wq_h.at[g], group_sem.at[3, g])]
        for part in range(3):
            some = pl.ds(part * pairs + 2 * g, 2)
            copies.append(pltpu.make_async_copy(qkv.at[some], qkv_h.at[some], group_sem.at[part, g]))
        return copies

    @pl.loop(0, pairs // 2)
    def _(g):
        @pl.loop(0, blocks)
        def _(b):
            at = pl.ds(pl.multiple_of(b * 256, 256), 256)
            block = mm(norm[at, :], wq[g].reshape(width, width)).astype(BF)
            for s in range(2):
                for part in range(3):
                    value = block[:, 384 * s + 128 * part : 384 * s + 128 * part + 128]
                    qkv[part * pairs + 2 * g + s, at, :] = value if part else value * jnp.asarray(0.125, BF)

        for copy in group_out(g):
            copy.start()

        @pl.loop(0, 2)
        def _(s):
            p = 2 * g + s
            keys, values = qkv[pairs + p], qkv[2 * pairs + p]
            side = mm(hot[:, :64], bias[p]).astype(BF)
            one = jnp.ones_like(values)
            ka[0, :, :128] = jnp.where(low_half, keys, side)
            ka[1, :, :128] = jnp.where(low_half, side, keys)
            va[0] = jnp.where(low_half, values, one)
            va[1] = jnp.where(low_half, one, values)
            for e in range(2):
                ka[e, :, 128:] = page_k[...]

            @pl.loop(0, blocks)
            def _(b):
                gather.tick(p * blocks + b)
                at = pl.ds(pl.multiple_of(b * 256, 256), 256)
                queries, places = qkv[p, at, :], hot[at, :]
                kept = lse[at, :]
                lane = lanes(256)
                half = lane < 64
                page_hot = jnp.where(lane < 6, kept, 0.0).astype(BF)
                results = []
                for e in range(2):
                    first = jnp.where(half, queries, places) if e == 0 else jnp.where(half, places, queries)
                    scores = mm(jnp.concatenate([first, page_hot], axis=1), ka[e], NT)
                    top = jnp.max(scores, axis=1, keepdims=True)
                    expo = jnp.exp(scores - top).astype(BF)
                    out = mm(expo, va[e])
                    turned = pltpu.roll(out, 64, axis=1)
                    total = jnp.where(half, turned, out) if e == 0 else jnp.where(half, out, turned)
                    results.append(out / total)
                    kept = jnp.where(lane // 3 == 2 + 2 * p + e, top + jnp.log(total), kept)
                lse[at, :] = kept
                att[at, pl.ds(pl.multiple_of(p * 128, 128), 128)] = jnp.where(half, results[0], results[1]).astype(BF)

    lane = lanes(256)

    @pl.loop(0, blocks)
    def _(b):
        at = pl.ds(pl.multiple_of(b * 256, 256), 256)
        ext[at, :] = jnp.where(lane < 6, lse[at, :], pieces(lse[at, :], lane)).astype(BF)

    for copy in outs[3:]:
        copy.start()
    @pl.loop(pairs * blocks, 28)
    def _(t):
        gather.tick(t)


    @pl.loop(0, 12)
    def _(n):
        gather.step(4, n)

    for i in range(3):
        pack_copy(i).wait_send()

    @pl.loop(0, pairs // 2)
    def _(g):
        for copy in group_out(g):
            copy.wait()

    for copy in outs:
        copy.wait()


def forward_call(ndp, places, vectors, bup, rel, tok, wqkv, wout, wup, wdown):
    count, width = tok.shape
    pairs = width // 128
    tall = pltpu.VMEM((count, width), BF)
    side = pltpu.VMEM((count, 128), BF)
    return pl.pallas_call(
        functools.partial(forward_kernel, ndp),
        out_shape=[
            jax.ShapeDtypeStruct((width, count), BF),
            jax.ShapeDtypeStruct((3 * pairs, count, 128), BF),
            jax.ShapeDtypeStruct((count, width), BF),
            jax.ShapeDtypeStruct((count, 128), BF),
            jax.ShapeDtypeStruct((count, 128), BF),
            jax.ShapeDtypeStruct((count, 128), BF),
            jax.ShapeDtypeStruct((pairs, 64, 128), BF),
            jax.ShapeDtypeStruct((12, width), F32),
            jax.ShapeDtypeStruct((3, 4, 192, width), BF),
            jax.ShapeDtypeStruct((4, 192, width), BF),
            jax.ShapeDtypeStruct((4, 4, 192, width), BF),
            jax.ShapeDtypeStruct((4, 4, 192, width), BF),
        ],
        in_specs=[VMEM] * 12 + [ANY] * 5,
        out_specs=[ANY] * 6 + [VMEM] * 2 + [ANY] * 4,
        scratch_shapes=[
            tall,
            tall,
            pltpu.VMEM((width, count), BF),
            pltpu.VMEM((3 * pairs, count, 128), BF),
            tall,
            side,
            side,
            side,
            pltpu.VMEM((count, 128), F32),
            pltpu.VMEM((2, count, 256), BF),
            pltpu.VMEM((2, count, 128), BF),
            pltpu.VMEM((3, 4, 192, width), BF),
            pltpu.VMEM((9, 192, width), BF),
            pltpu.VMEM((4, 24, 256), F32),
            pltpu.VMEM((24, 128), F32),
            pltpu.SemaphoreType.DMA,
            pltpu.SemaphoreType.DMA((9,)),
            pltpu.SemaphoreType.DMA((3, 6)),
            pltpu.SemaphoreType.DMA((3,)),
            pltpu.SemaphoreType.DMA((3,)),
            pltpu.SemaphoreType.DMA((5, 12)),
            pltpu.SemaphoreType.DMA((5, 12)),
            pltpu.SemaphoreType.DMA((12,)),
            pltpu.SemaphoreType.DMA((5,)),
            pltpu.SemaphoreType.DMA((4, 3)),
        ],
        compiler_params=pltpu.CompilerParams(vmem_limit_bytes=LIMIT, collective_id=0, has_side_effects=True),
        name="forward",
    )(*places, *vectors, bup, rel, tok, wqkv, wout, wup, wdown)


def gelu_both(u):
    c = 0.7978845608028654
    square = u * u
    t = jnp.tanh(c * u * (1.0 + 0.044715 * square))
    half = 0.5 + 0.5 * t
    slope = half + (0.5 * c) * u * (1.0 - t * t) * (1.0 + 0.134145 * square)
    return u * half, slope


EARLY = [("d", 0), ("d", 1), ("d", 2)]
EARLY_STOP = 3
EARLY_PERIOD = 4
EARLY_LAGS = {1: 0, 2: 8, 3: 12}


def middle_kernel(
    ndp,
    tok_h,
    cot_h,
    att_h,
    ext_h,
    vec,
    wout_h,
    wup_h,
    wdown_h,
    layer_h,
    dmid_h,
    datt_h,
    dext_h,
    part_h,
    half_h,
    small,
    tok,
    cot,
    att,
    ext,
    wout,
    wup,
    wdown,
    act,
    dup,
    n2t,
    ddt,
    att_t,
    ddown,
    dproj,
    layer,
    dmid,
    datt,
    dext,
    stage,
    own,
    acc,
    r0,
    r1,
    r2,
    in_sem,
    out_sem,
    layer_sem,
    part_sem,
    spare_sem,
    load_sem,
    send_sem,
    recv_sem,
    half_sem,
):
    count, width = tok.shape
    cols = wup.shape[0]
    blocks = count // 256
    loads = []
    for i, (src, dst) in enumerate(
        [(att_h, att), (wout_h, wout), (tok_h, tok), (wup_h, wup), (wdown_h, wdown), (cot_h, cot), (ext_h, ext)]
    ):
        copy = pltpu.make_async_copy(src, dst, in_sem.at[i])
        copy.start()
        loads.append(copy)
    links = Links(ndp)
    links.greet(links.everyone()[:3])
    red = Reduction(
        links, 3, EARLY, {"d": own}, 0, EARLY_STOP, acc, [r0, r1, r2], None, half_h, load_sem, send_sem, recv_sem, half_sem
    )
    small[...] = jnp.zeros_like(small)
    head = lax.broadcasted_iota(jnp.int32, (width, 128), 0) // 64
    pick = jnp.where(lanes(width) // 3 == head, 1.0, 0.0).astype(BF)
    for copy in loads:
        copy.wait()

    def spot(b):
        return pl.ds(pl.multiple_of(b * 256, 256), 256)

    def layer_out(b):
        return pltpu.make_async_copy(layer.at[spot(b), :], layer_h.at[spot(b), :], layer_sem.at[b])

    def outs(b):
        at = spot(b)
        return [
            pltpu.make_async_copy(src.at[at, :], dst.at[at, :], out_sem.at[i, b])
            for i, (src, dst) in enumerate([(dmid, dmid_h), (datt, datt_h), (dext, dext_h)])
        ]

    def masked(at):
        return cot[at, :].astype(F32) * (1.0 - ext[at, :].astype(F32)[:, 0:1])

    def center_scale(mid):
        center = mid - jnp.mean(mid, axis=-1, keepdims=True)
        return center, lax.rsqrt(jnp.mean(center * center, axis=-1, keepdims=True) + 1e-06)

    @pl.loop(0, blocks)
    def _(b):
        at = spot(b)
        rows_att = att[at, :]
        proj = mm(rows_att, wout[...])
        mid = tok[at, :].astype(F32) + vec[2:3, :] * proj
        dmid[at, :] = mid
        datt[at, :] = proj.astype(BF)
        center, scale = center_scale(mid)
        norm = (center * scale * vec[3:4, :] + vec[4:5, :]).astype(BF)
        down = jnp.zeros((256, width), F32)
        for j in range(cols):
            u = mm(norm, wup[j]) + vec[8 + j : 9 + j, :]
            a, s = gelu_both(u)
            a = a.astype(BF)
            act[at, j * width : (j + 1) * width] = a
            dup[at, j * width : (j + 1) * width] = s.astype(BF)
            down += mm(a, wdown[j * width : (j + 1) * width, :])
        down += vec[5:6, :]
        layer[at, :] = (mid + vec[6:7, :] * down).astype(BF)
        layer_out(b).start()
        grad = masked(at)
        d_down = (grad * vec[6:7, :]).astype(BF)
        ddown[at, :] = d_down
        small[6:7, :] += jnp.sum(grad * down, axis=0, keepdims=True)
        small[5:6, :] += jnp.sum(d_down.astype(F32), axis=0, keepdims=True)
        n2t[:, at] = norm.T
        ddt[:, at] = d_down.T
        att_t[:, at] = rows_att.T

    @pl.loop(0, 2)
    def _(h):
        @pl.loop(0, cols)
        def _(j):
            col = pl.ds(pl.multiple_of(j * width, width), width)
            value = mm(ddt[pl.ds(pl.multiple_of(h * 384, 384), 384), :], act[:, col])
            for i in range(2):
                for r in range(4):
                    for c in range(2):
                        rows = slice(192 * i + 48 * r, 192 * i + 48 * r + 48)
                        own[2 * h + i, j % 2, j // 2, c, r // 2, r % 2] = value[rows, 384 * c : 384 * c + 384].astype(BF)

        red.launch(2 * h)

        @pl.when(h == 0)
        def _():
            red.launch(1)

    spare = pltpu.make_async_copy(own.at[3], part_h.at[5], spare_sem)
    spare.start()

    @pl.loop(0, blocks)
    def _(b):
        at = spot(b)
        d_down = ddown[at, :]
        d_norm = jnp.zeros((256, width), F32)
        for j in range(cols):
            red.tick(b, j, 0, EARLY_PERIOD, EARLY_LAGS)
            d_act = mm(d_down, wdown[j * width : (j + 1) * width, :], NT)
            some = slice(j * width, (j + 1) * width)
            d_up = (d_act * dup[at, some].astype(F32)).astype(BF)
            dup[at, some] = d_up
            small[8 + j : 9 + j, :] += jnp.sum(d_up.astype(F32), axis=0, keepdims=True)
            d_norm += mm(d_up, wup[j], NT)
        center, scale = center_scale(dmid[at, :])
        unit = center * scale
        small[3:4, :] += jnp.sum(d_norm * unit, axis=0, keepdims=True)
        small[4:5, :] += jnp.sum(d_norm, axis=0, keepdims=True)
        d_unit = d_norm * vec[3:4, :]
        d_mid = masked(at) + scale * (
            d_unit - jnp.mean(d_unit, axis=-1, keepdims=True) - unit * jnp.mean(d_unit * unit, axis=-1, keepdims=True)
        )
        dmid[at, :] = d_mid
        small[2:3, :] += jnp.sum(d_mid * datt[at, :].astype(F32), axis=0, keepdims=True)
        d_proj = (d_mid * vec[2:3, :]).astype(BF)
        dproj[at, :] = d_proj
        d_att = mm(d_proj, wout[...], NT).astype(BF)
        datt[at, :] = d_att
        prod = att[at, :].astype(F32) * d_att.astype(F32)
        hi = prod.astype(BF)
        low = (prod - hi.astype(F32)).astype(BF)
        dext[at, :] = pieces(-(mm(hi, pick) + mm(low, pick)), lanes(256)).astype(BF)
        for copy in outs(b):
            copy.start()

    def put(slot, value):
        for i in range(4):
            for r in range(4):
                for c in range(2):
                    rows = slice(192 * i + 48 * r, 192 * i + 48 * r + 48)
                    stage[slot, i, c, r // 2, r % 2] = value[rows, 384 * c : 384 * c + 384].astype(BF)

    def sends(chunk, slot):
        return [
            pltpu.make_async_copy(stage.at[slot, i], part_h.at[chunk, i % 2, i // 2], part_sem.at[slot, i])
            for i in range(4)
        ]

    @pl.loop(0, cols)
    def _(j):
        for r in range(cols):

            @pl.when(j == r)
            def _(r=r):
                red.tick(blocks, r, 0, EARLY_PERIOD, EARLY_LAGS)

        col = pl.ds(pl.multiple_of(j * width, width), width)
        slot = j % 2

        @pl.when(j > 1)
        def _():
            for copy in sends(j - 2, slot):
                copy.wait()

        put(slot, mm(n2t[...], dup[:, col]))
        for copy in sends(j, slot):
            copy.start()

    for copy in sends(cols - 2, 0):
        copy.wait()
    put(0, mm(att_t[...], dproj[...]))
    for copy in sends(cols, 0):
        copy.start()

    for t in range(EARLY_PERIOD * (blocks + 1), last_tick(0, EARLY_PERIOD, len(EARLY), EARLY_LAGS)):
        red.tick(t // EARLY_PERIOD, t % EARLY_PERIOD, 0, EARLY_PERIOD, EARLY_LAGS)

    for copy in sends(cols - 1, 1) + sends(cols, 0):
        copy.wait()

    @pl.loop(0, blocks)
    def _(b):
        layer_out(b).wait()
        for copy in outs(b):
            copy.wait()

    spare.wait()
    red.finish()


def middle_call(ndp, tok, cot, att, ext, vec, wout, wup, wdown):
    count, width = tok.shape
    ff = wdown.shape[0]
    n = len(EARLY)
    tall = pltpu.VMEM((count, width), BF)
    wide = pltpu.VMEM((width, count), BF)
    return pl.pallas_call(
        functools.partial(middle_kernel, ndp),
        out_shape=[
            jax.ShapeDtypeStruct((count, width), BF),
            jax.ShapeDtypeStruct((count, width), F32),
            jax.ShapeDtypeStruct((count, width), BF),
            jax.ShapeDtypeStruct((count, 128), BF),
            jax.ShapeDtypeStruct((6, 2, 2, 2, 2, 2, 48, 384), BF),
            jax.ShapeDtypeStruct((n, 2, 2, 48, 384), BF),
            jax.ShapeDtypeStruct((16, width), F32),
        ],
        in_specs=[ANY] * 4 + [VMEM] + [ANY] * 3,
        out_specs=[ANY] * 6 + [VMEM],
        scratch_shapes=[
            tall,
            tall,
            tall,
            pltpu.VMEM((count, 128), BF),
            pltpu.VMEM(wout.shape, BF),
            pltpu.VMEM(wup.shape, BF),
            pltpu.VMEM(wdown.shape, BF),
            pltpu.VMEM((count, ff), BF),
            pltpu.VMEM((count, ff), BF),
            wide,
            wide,
            wide,
            tall,
            tall,
            tall,
            pltpu.VMEM((count, width), F32),
            tall,
            pltpu.VMEM((count, 128), BF),
            pltpu.VMEM((2, 4, 2, 2, 2, 48, 384), BF),
            pltpu.VMEM((4, 2, 2, 2, 2, 2, 48, 384), BF),
            pltpu.VMEM((n, 2, 2, 2, 2, 48, 384), BF),
            pltpu.VMEM((n, 2, 2, 2, 2, 48, 384), BF),
            pltpu.VMEM((n, 2, 2, 2, 48, 384), BF),
            pltpu.VMEM((n, 2, 2, 48, 384), BF),
            pltpu.SemaphoreType.DMA((7,)),
            pltpu.SemaphoreType.DMA((3, count // 256)),
            pltpu.SemaphoreType.DMA((count // 256,)),
            pltpu.SemaphoreType.DMA((2, 4)),
            pltpu.SemaphoreType.DMA,
            pltpu.SemaphoreType.DMA((n,)),
            pltpu.SemaphoreType.DMA((EARLY_STOP, n)),
            pltpu.SemaphoreType.DMA((EARLY_STOP, n)),
            pltpu.SemaphoreType.DMA((n,)),
        ],
        compiler_params=pltpu.CompilerParams(vmem_limit_bytes=LIMIT, collective_id=2, has_side_effects=True),
        name="middle",
    )(tok, cot, att, ext, vec, wout, wup, wdown)


ORDER = [("g", 5), ("g", 0), ("g", 1), ("g", 2), ("q", 0), ("g", 3), ("g", 4)]
LAGS = {1: 1, 2: 5, 3: 4, 8: 4}
LATE_START = 1
HALF = [("h", 0), ("h", 1), ("h", 2), ("h", 3)]
HALF_START = 12


def backward_kernel(
    ndp,
    page,
    row,
    col,
    vec,
    small_in,
    qkv_h,
    ext_h,
    hot_h,
    page_k_h,
    bias,
    dext_h,
    datt_h,
    normt_h,
    wq_h,
    tok_h,
    dmid_h,
    parts_h,
    early_h,
    gtok_h,
    total_h,
    late_h,
    last_h,
    small_out,
    qkv,
    ext,
    hot,
    page_k,
    dext,
    datt,
    normt,
    wq,
    tok,
    dmid,
    gtok,
    dqkv,
    qa,
    ka,
    va,
    doa,
    kt,
    dqt,
    hot_t,
    square,
    dtab,
    own,
    own_half,
    acc,
    b0,
    b1,
    b2,
    b3,
    b4,
    late_acc,
    late_final,
    late_3,
    late_4,
    half_acc,
    half_final,
    half_0,
    half_1,
    half_2,
    half_3,
    more,
    late_more,
    half_more,
    small_acc,
    small_recv,
    in_sem,
    gt_sem,
    load_sem,
    send_sem,
    recv_sem,
    out_sem,
    late_load,
    late_send,
    late_recv,
    late_out,
    half_load,
    half_send,
    half_recv,
    half_out,
    small_send,
    small_got,
):
    count, width = tok.shape
    pairs = bias.shape[0]
    blocks = count // 256
    loads = []
    for i, (src, dst) in enumerate(
        [
            (qkv_h, qkv),
            (ext_h, ext),
            (hot_h, hot),
            (page_k_h, page_k),
            (dext_h, dext),
            (datt_h, datt),
            (normt_h, normt),
            (wq_h, wq),
            (tok_h, tok),
            (dmid_h, dmid),
        ]
    ):
        copy = pltpu.make_async_copy(src, dst, in_sem.at[i])
        copy.start()
        loads.append(copy)
    links = Links(ndp)
    links.greet(links.everyone())
    red = Reduction(
        links,
        3,
        ORDER,
        {"g": parts_h, "q": own},
        0,
        None,
        acc,
        [b0, b1, b2, b3, b4] + [more.at[k] for k in range(links.bits - 3)],
        b1,
        total_h,
        load_sem,
        send_sem,
        recv_sem,
        out_sem,
    )
    late = Reduction(
        links,
        3,
        EARLY,
        {"d": early_h},
        EARLY_STOP,
        None,
        late_acc,
        [None, None, None, late_3, late_4] + [late_more.at[k] for k in range(links.bits - 3)],
        late_final,
        late_h,
        late_load,
        late_send,
        late_recv,
        late_out,
    )
    half = Reduction(
        links,
        2,
        HALF,
        {"h": own_half},
        0,
        None,
        half_acc,
        [half_0, half_1, half_2, half_3] + [half_more.at[k] for k in range(links.bits - 2)],
        half_final,
        last_h,
        half_load,
        half_send,
        half_recv,
        half_out,
    )
    lags = lag_table(0, red.stages, 0, 3, LAGS)
    late_lags = lag_table(EARLY_STOP, late.stages, 0, 3, {EARLY_STOP: 1})
    half_lags = lag_table(0, half.stages, 0, 3, {1: 1, 2: 6})

    def tick(turn, r):
        red.tick(2 * turn + r // 2, r % 2, 0, 2, lags)
        late.tick(2 * turn + r // 2, r % 2, LATE_START, 2, late_lags)
        half.tick(turn, r, HALF_START, 4, half_lags)

    def tick_at(turn, place):
        for r in range(4):

            @pl.when(place == r)
            def _(r=r):
                tick(turn, r)

    for r in range(page.shape[0]):
        want = 31 - lax.broadcasted_iota(jnp.int32, (32, 128), 0)
        for axis in range(2):
            have = jnp.broadcast_to((col if axis else row)[r : r + 1, :], (32, 128))
            hot_t[32 * axis : 32 * axis + 32, r * 128 : r * 128 + 128] = jnp.where(have == want, 1.0, 0.0).astype(BF)
    small_acc[0] = small_in[...]
    low_half = lanes(count) < 64
    third = lanes(count) // 3
    for copy in loads[:6]:
        copy.wait()

    @pl.loop(0, pairs)
    def _(p):
        g, s = p // 2, p % 2
        queries, keys, values = qkv[p], qkv[pairs + p], qkv[2 * pairs + p]
        side = mm(hot[:, :64], bias[p]).astype(BF)
        zero = jnp.zeros_like(values)
        places = hot[...]
        qa[0, :, :128] = jnp.where(low_half, queries, places)
        qa[1, :, :128] = jnp.where(low_half, places, queries)
        ka[0, :, :128] = jnp.where(low_half, keys, side)
        ka[1, :, :128] = jnp.where(low_half, side, keys)
        va[0, :, :128] = jnp.where(low_half, values, zero)
        va[1, :, :128] = jnp.where(low_half, zero, values)
        for e in range(2):
            head = 2 * p + e
            qa[e, :, 128:] = ext[...]
            ka[e, :, 128:] = jnp.where(third == 2 + head, -1.0, page_k[...].astype(F32)).astype(BF)
            va[e, :, 128:] = jnp.where(third == head, 1.0, 0.0).astype(BF)
        doa[:, :128] = datt[:, pl.ds(pl.multiple_of(p * 128, 128), 128)]
        doa[:, 128:] = dext[...]
        kt[...] = keys.T
        dqt[...] = jnp.zeros_like(dqt)
        square[...] = jnp.zeros_like(square)

        @pl.loop(0, blocks)
        def _(b):
            tick_at(p, b)
            at = pl.ds(pl.multiple_of(b * 256, 256), 256)
            dks, dvs = [], []
            for e in range(2):
                prob = jnp.exp(mm(ka[e, at, :], qa[e], NT))
                d_prob = mm(va[e, at, :], doa[...], NT)
                d_scores = (prob * d_prob).astype(BF)
                dvs.append(mm(prob.astype(BF), doa[:, :128]))
                dks.append(mm(d_scores, qa[e, :, :128]))
                dqt[64 * e : 64 * e + 64, :] += mm(kt[64 * e : 64 * e + 64, at], d_scores)
            half = lanes(256) < 64
            dqkv[g, at, pl.ds(pl.multiple_of(s * 384 + 128, 128), 128)] = jnp.where(half, dks[0], dks[1]).astype(BF)
            dqkv[g, at, pl.ds(pl.multiple_of(s * 384 + 256, 128), 128)] = jnp.where(half, dvs[0], dvs[1]).astype(BF)
            part = jnp.where(half, dks[1], dks[0])
            hi = part.astype(BF)
            low = (part - hi.astype(F32)).astype(BF)
            both = mm(hot_t[:, at], jnp.concatenate([hi, low], axis=1))
            square[...] += both[:, :128] + both[:, 128:]

        dqkv[g, :, pl.ds(pl.multiple_of(s * 384, 128), 128)] = (dqt[...].T * 0.125).astype(BF)
        near = lanes(32) & 63
        for axis in range(2):
            part = square[32 * axis : 32 * axis + 32, :]
            part = jnp.where((near >= 32) if axis else (near < 32), part, 0.0)
            rolled = pltpu.roll(part, 96 * axis, axis=1, stride=1, stride_axis=0)
            dtab[p, axis : axis + 1, :] = jnp.sum(rolled, axis=0, keepdims=True)

        @pl.when(p == 0)
        def _():
            for copy in loads[6:]:
                copy.wait()

        value = mm(normt[...], dqkv[g, :, pl.ds(pl.multiple_of(s * 384, 128), 384)]).astype(BF)

        @pl.when(p < 2 * own.shape[0])
        def _():
            for f in range(4):
                for r in range(4):
                    own[g, f % 2, f // 2, s, r // 2, r % 2] = value[192 * f + 48 * r : 192 * f + 48 * r + 48, :]

        @pl.when(p >= 2 * own.shape[0])
        def _():
            for f in range(4):
                for r in range(4):
                    at = (p - 2 * own.shape[0], f % 2, f // 2, r // 2, r % 2)
                    own_half[at] = value[192 * f + 48 * r : 192 * f + 48 * r + 48, :]

    for p in range(pairs):
        for axis in range(2):
            i = 2 * p + axis
            small_acc[0, 12 + i // 6 : 13 + i // 6, 128 * (i % 6) : 128 * (i % 6) + 128] = dtab[p, axis : axis + 1, :]

    def gtok_out(b):
        at = pl.ds(pl.multiple_of(b * 256, 256), 256)
        return pltpu.make_async_copy(gtok.at[at, :], gtok_h.at[at, :], gt_sem.at[b])

    first_tick = pairs * blocks

    @pl.loop(0, blocks)
    def _(b):
        tick_at(pairs, b)
        at = pl.ds(pl.multiple_of(b * 256, 256), 256)
        d_norm = mm(dqkv[0, at, :], wq[0], NT)
        for g in range(1, pairs // 2):
            d_norm += mm(dqkv[g, at, :], wq[g], NT)
        rows = tok[at, :].astype(F32)
        center = rows - jnp.mean(rows, axis=-1, keepdims=True)
        scale = lax.rsqrt(jnp.mean(center * center, axis=-1, keepdims=True) + 1e-06)
        unit = center * scale
        small_acc[0, 0:1, :] += jnp.sum(d_norm * unit, axis=0, keepdims=True)
        small_acc[0, 1:2, :] += jnp.sum(d_norm, axis=0, keepdims=True)
        d_unit = d_norm * vec[0:1, :]
        back = scale * (
            d_unit - jnp.mean(d_unit, axis=-1, keepdims=True) - unit * jnp.mean(d_unit * unit, axis=-1, keepdims=True)
        )
        gtok[at, :] = (dmid[at, :] + back).astype(BF)
        gtok_out(b).start()

    others = links.everyone()

    def small_copy(i):
        return remote(small_acc.at[i], small_recv.at[i], small_send.at[i], small_got.at[i], others[i])

    small_copy(0).start()
    at_tick = first_tick + blocks
    for i in range(len(others)):
        tick((at_tick + i) // 4, (at_tick + i) % 4)
        small_copy(i).wait_recv()
        small_acc[i + 1] = small_acc[i] + small_recv[i]
        if i + 1 < len(others):
            small_copy(i + 1).start()
    small_out[...] = small_acc[len(others)]
    at_tick = at_tick + len(others)
    while at_tick % 4:
        tick(at_tick // 4, at_tick % 4)
        at_tick += 1
    last = max(
        last_tick(0, 2, len(ORDER), lags),
        last_tick(LATE_START, 2, len(EARLY), late_lags),
        last_tick(HALF_START, 4, len(HALF), half_lags),
    )

    @pl.loop(at_tick // 4, -(-last // 4))
    def _(turn):
        for r in range(4):
            tick(turn, r)

    red.finish()
    late.finish()
    half.finish()
    for i in range(len(others)):
        small_copy(i).wait_send()
    for b in range(blocks):
        gtok_out(b).wait()


def backward_call(ndp, places, vec, small, qkv, ext, hot, page_k, bias, dext, datt, normt, wq, tok, dmid, parts, half):
    count, width = datt.shape
    bits = ndp.bit_length() - 1
    n, m, q = len(ORDER), len(EARLY), len(HALF)
    last_extra = max(0, bits - 2)
    extra = max(0, bits - 3)
    stages = 2 + 2 * min(3, bits) + extra
    tall = pltpu.VMEM((count, width), BF)
    side = pltpu.VMEM((count, 128), BF)
    pair = pltpu.VMEM((2, count, 256), BF)
    return pl.pallas_call(
        functools.partial(backward_kernel, ndp),
        out_shape=[
            jax.ShapeDtypeStruct((count, width), BF),
            jax.ShapeDtypeStruct((n, 2, 2, 2, 48, 384), BF),
            jax.ShapeDtypeStruct((m, 2, 2, 2, 48, 384), BF),
            jax.ShapeDtypeStruct((q, 2, 2, 48, 384), BF),
            jax.ShapeDtypeStruct(small.shape, F32),
        ],
        in_specs=[VMEM] * 5 + [ANY] * 4 + [VMEM] + [ANY] * 8,
        out_specs=[ANY] * 4 + [VMEM],
        scratch_shapes=[
            pltpu.VMEM(qkv.shape, BF),
            side,
            side,
            side,
            side,
            tall,
            pltpu.VMEM((width, count), BF),
            pltpu.VMEM(wq.shape, BF),
            tall,
            pltpu.VMEM((count, width), F32),
            tall,
            pltpu.VMEM((3, count, width), BF),
            pair,
            pair,
            pair,
            pltpu.VMEM((count, 256), BF),
            pltpu.VMEM((128, count), BF),
            pltpu.VMEM((128, count), F32),
            pltpu.VMEM((64, count), BF),
            pltpu.VMEM((64, 128), F32),
            pltpu.VMEM((width // 128, 2, 128), F32),
            pltpu.VMEM((1, 2, 2, 2, 2, 2, 48, 384), BF),
            pltpu.VMEM((q, 2, 2, 2, 2, 48, 384), BF),
            pltpu.VMEM((n, 2, 2, 2, 2, 48, 384), BF),
            pltpu.VMEM((n, 2, 2, 2, 2, 48, 384), BF),
            pltpu.VMEM((n, 2, 2, 2, 48, 384), BF),
            pltpu.VMEM((n, 2, 2, 48, 384), BF),
            pltpu.VMEM((n, 2, 48, 384), BF),
            pltpu.VMEM((n, 48, 384), BF),
            pltpu.VMEM((m, 2, 2, 48, 384), BF),
            pltpu.VMEM((m, 2, 2, 2, 48, 384), BF),
            pltpu.VMEM((m, 2, 48, 384), BF),
            pltpu.VMEM((m, 48, 384), BF),
            pltpu.VMEM((q, 2, 2, 2, 48, 384), BF),
            pltpu.VMEM((q, 2, 2, 48, 384), BF),
            pltpu.VMEM((q, 2, 2, 2, 48, 384), BF),
            pltpu.VMEM((q, 2, 2, 48, 384), BF),
            pltpu.VMEM((q, 2, 48, 384), BF),
            pltpu.VMEM((q, 48, 384), BF),
            pltpu.VMEM((extra, n, 48, 384) if extra else (1, 1, 16, 128), BF),
            pltpu.VMEM((extra, m, 48, 384) if extra else (1, 1, 16, 128), BF),
            pltpu.VMEM((last_extra, q, 48, 384) if last_extra else (1, 1, 16, 128), BF),
            pltpu.VMEM((bits + 3,) + small.shape, F32),
            pltpu.VMEM((bits + 2,) + small.shape, F32),
            pltpu.SemaphoreType.DMA((10,)),
            pltpu.SemaphoreType.DMA((count // 256,)),
            pltpu.SemaphoreType.DMA((n,)),
            pltpu.SemaphoreType.DMA((stages, n)),
            pltpu.SemaphoreType.DMA((stages, n)),
            pltpu.SemaphoreType.DMA((n,)),
            pltpu.SemaphoreType.DMA((m,)),
            pltpu.SemaphoreType.DMA((stages, m)),
            pltpu.SemaphoreType.DMA((stages, m)),
            pltpu.SemaphoreType.DMA((m,)),
            pltpu.SemaphoreType.DMA((q,)),
            pltpu.SemaphoreType.DMA((stages, q)),
            pltpu.SemaphoreType.DMA((stages, q)),
            pltpu.SemaphoreType.DMA((q,)),
            pltpu.SemaphoreType.DMA((bits + 2,)),
            pltpu.SemaphoreType.DMA((bits + 2,)),
        ],
        compiler_params=pltpu.CompilerParams(vmem_limit_bytes=LIMIT, collective_id=1, has_side_effects=True),
        name="backward",
    )(*places, vec, small, qkv, ext, hot, page_k, bias, dext, datt, normt, wq, tok, dmid, parts, half)


def finish_kernel(
    total_h,
    late_h,
    last_h,
    layer_i,
    gtok_i,
    small,
    layer_h,
    gtok_h,
    wqkv_h,
    rel,
    wout_h,
    wup_h,
    bup,
    wdown_h,
    v0,
    v1,
    v2,
    v3,
    v4,
    v5,
    v6,
    total,
    late,
    last,
    wqkv,
    wout,
    wup,
    wdown,
    layer,
    gtok,
    in_sem,
    out_sem,
):
    f = lax.axis_index("fsdp")
    own = v0.shape[0]
    n, m = total.shape[0], late.shape[0]
    loads = [pltpu.make_async_copy(late_h.at[i], late.at[i], in_sem.at[i]) for i in range(m)]
    loads += [pltpu.make_async_copy(total_h.at[i], total.at[i], in_sem.at[m + i]) for i in range(n)]
    loads.append(pltpu.make_async_copy(last_h, last, in_sem.at[m + n]))
    through = [(layer_i, layer, layer_h), (gtok_i, gtok, gtok_h)]
    loads += [pltpu.make_async_copy(src, mid, in_sem.at[m + n + 1 + i]) for i, (src, mid, _) in enumerate(through)]
    for copy in loads:
        copy.start()
    pending = []

    def leave(src, dst):
        copy = pltpu.make_async_copy(src, dst, out_sem.at[len(pending)])
        copy.start()
        pending.append(copy)

    spare = [kind for kind, _ in ORDER].index("g")
    for h in range(2):
        loads[2 * h].wait()
        loads[2 * h + 1 if h == 0 else m + spare].wait()
        sides = []
        for c in range(2):
            both = [late.at[2 * h], late.at[2 * h + 1] if h == 0 else total.at[spare]]
            rows = [one[c, r // 2, r % 2].astype(F32) for one in both for r in range(4)]
            sides.append(jnp.concatenate(rows, axis=0).T)
        for c in range(2):
            wdown[384 * c : 384 * c + 384, 384 * h : 384 * h + 384] = sides[c]
        if h == 0:
            for i, (_, mid, dst) in enumerate(through):
                loads[m + n + 1 + i].wait()
                leave(mid, dst)
    leave(wdown, wdown_h)
    for i, (kind, j) in enumerate(ORDER):
        if i == spare:
            continue
        loads[m + i].wait()
        for c in range(2):
            for r in range(4):
                at = slice(48 * r, 48 * r + 48)
                value = total[i, c, r // 2, r % 2].astype(F32)
                if kind == "g" and j < 4:
                    wup[at, 768 * j + 384 * c : 768 * j + 384 * c + 384] = value
                elif kind == "g":
                    wout[at, 384 * c : 384 * c + 384] = value
                else:
                    for part in range(3):
                        start = 768 * part + 256 * j + 128 * c
                        wqkv[at, start : start + 128] = value[:, 128 * part : 128 * part + 128]
    leave(wup, wup_h)
    leave(wout, wout_h)
    loads[m + n].wait()
    for i in range(last.shape[0]):
        for r in range(4):
            value = last[i, r // 2, r % 2].astype(F32)
            for part in range(3):
                start = 768 * part + 128 * (2 + i)
                wqkv[48 * r : 48 * r + 48, start : start + 128] = value[:, 128 * part : 128 * part + 128]
    leave(wqkv, wqkv_h)

    def mine(rows, width, stride):
        out = jnp.zeros((rows.stop - rows.start, width), F32)
        for k in range(4):
            out = jnp.where(f == k, small[rows, stride * k : stride * k + width], out)
        return out

    vectors = mine(slice(0, 8), own, own)
    for i, ref in enumerate((v0, v1, v2, v3, v4, v5, v6)):
        ref[...] = vectors[i : i + 1, :].reshape(own)
    line = jnp.zeros((1, bup.shape[0]), F32)
    for k in range(4):
        line = jnp.where(f == k, small[8 + k : 9 + k, :], line)
    bup[...] = line.reshape(bup.shape[0])
    offsets = rel.shape[2]
    for i in range(rel.shape[0]):
        for axis in range(2):
            value = jnp.zeros((1, offsets), F32)
            for k in range(4):
                head = rel.shape[0] * k + i
                line = 2 * (head // 2) + axis
                start = 128 * (line % 6) + 64 * (1 - head % 2)
                at = 12 + line // 6
                value = jnp.where(f == k, small[at : at + 1, start : start + offsets], value)
            rel[i, axis : axis + 1, :] = value
    for copy in pending:
        copy.wait()


def finish_call(total, late, last, layer, gtok, small, own, rel):
    width = small.shape[1]
    vec = jax.ShapeDtypeStruct((own,), F32)
    shapes = [(own, 3 * width), (own, width), (own, 4 * width), (4 * own, width)]
    wqkv, wout, wup, wdown = [jax.ShapeDtypeStruct(s, F32) for s in shapes]
    return pl.pallas_call(
        finish_kernel,
        out_shape=[jax.ShapeDtypeStruct(layer.shape, BF), jax.ShapeDtypeStruct(gtok.shape, BF)]
        + [wqkv, jax.ShapeDtypeStruct(rel.shape, F32), wout, wup, jax.ShapeDtypeStruct((4 * own,), F32), wdown]
        + [vec] * 7,
        in_specs=[ANY] * 5 + [VMEM],
        out_specs=[ANY, ANY, ANY, VMEM, ANY, ANY, VMEM, ANY] + [VMEM] * 7,
        scratch_shapes=[pltpu.VMEM(x.shape, BF) for x in (total, late, last)]
        + [pltpu.VMEM(s, F32) for s in shapes]
        + [pltpu.VMEM(layer.shape, BF), pltpu.VMEM(gtok.shape, BF)]
        + [pltpu.SemaphoreType.DMA((total.shape[0] + late.shape[0] + 3,)), pltpu.SemaphoreType.DMA((6,))],
        compiler_params=pltpu.CompilerParams(vmem_limit_bytes=LIMIT),
        name="finish",
    )(total, late, last, layer, gtok, small)


def local(
    tokens,
    cotangent,
    page_id,
    pos_row,
    pos_col,
    ln1_gain,
    ln1_shift,
    w_qkv,
    rel_table,
    w_out,
    scale_attn,
    ln2_gain,
    ln2_shift,
    w_up,
    b_up,
    w_down,
    b_down,
    scale_mlp,
):
    ndp = lax.axis_size("dp")
    count, width = tokens.shape
    places = [x.reshape(count // 128, 128) for x in (page_id, pos_row, pos_col)]
    vectors = [ln1_gain, ln1_shift, scale_attn, ln2_gain, ln2_shift, b_down, scale_mlp]
    normt, qkv, att, ext, hot, page_k, bias, vec, wq, wout, wup, wdown = forward_call(
        ndp, places, vectors, b_up, rel_table, tokens, w_qkv, w_out, w_up, w_down
    )
    wq = wq.reshape(-1, width, width)
    wout = wout.reshape(width, width)
    wup = wup.reshape(-1, width, width)
    wdown = wdown.reshape(-1, width)
    layer_out, d_mid, d_att, d_ext, parts, early, small = middle_call(ndp, tokens, cotangent, att, ext, vec, wout, wup, wdown)
    grad_tokens, total, late, last, small = backward_call(
        ndp, places, vec, small, qkv, ext, hot, page_k, bias, d_ext, d_att, normt, wq, tokens, d_mid, parts, early
    )
    layer_out, grad_tokens, g_wqkv, g_rel, g_wout, g_wup, g_bup, g_wdown, *g = finish_call(
        total, late, last, layer_out, grad_tokens, small, ln1_gain.shape[0], rel_table
    )
    return (
        layer_out,
        grad_tokens,
        g[0],
        g[1],
        g_wqkv,
        g_rel,
        g_wout,
        g[2],
        g[3],
        g[4],
        g_wup,
        g_bup,
        g_wdown,
        g[5],
        g[6],
    )


def solution(mesh):
    rows = P(("dp", "fsdp"))
    slab = P(("dp", "fsdp"), None)
    vec = P("fsdp")
    mat = P("fsdp", None)
    cube = P("fsdp", None, None)
    in_specs = (slab, slab, rows, rows, rows, vec, vec, mat, cube, mat, vec, vec, vec, mat, vec, mat, vec, vec)
    out_specs = (slab, slab, vec, vec, mat, cube, mat, vec, vec, vec, mat, vec, mat, vec, vec)
    return jax.shard_map(local, mesh=mesh, in_specs=in_specs, out_specs=out_specs, check_vma=False)
```
